32 devices in a mesh: dp: 8 (over z, y), fsdp: 4 (over x, core).
Axes of the slice: x: 2, y: 2, z: 4, core: 2. Of those that a mesh axis runs over, the one named last changes fastest.
Arguments:
- tokens: bfloat16 [64, 512, 1024], P(('dp', 'fsdp')), may hold values from -6 to 6
- cotangent: bfloat16 [64, 512, 1024], P(('dp', 'fsdp')), may hold values from -6 to 6
- adapter_id: int32 [64], P(('dp', 'fsdp')), may hold values from 0 to 7
- global_pos: int32 [64, 64], P(('dp', 'fsdp')), may hold values from 0 to 511, as said below
- w_qkv: bfloat16 [1024, 3072], P(('dp', 'fsdp')), may hold values from -0.1875 to 0.1875
- w_out: bfloat16 [1024, 1024], P(('dp', 'fsdp')), may hold values from -0.75 to 0.75
- w_up: bfloat16 [1024, 4096], P(('dp', 'fsdp')), may hold values from -0.1875 to 0.1875
- w_down: bfloat16 [4096, 1024], P(('dp', 'fsdp')), may hold values from -0.09375 to 0.09375
- norm_gain: bfloat16 [1024, 2], P(('dp', 'fsdp')), may hold values from 0.5 to 1.5
- norm_bias: bfloat16 [1024, 2], P(('dp', 'fsdp')), may hold values from -3 to 3
- narrow_in: bfloat16 [1024, 640], P(('dp', 'fsdp')), may hold values from -0.1875 to 0.1875
- widen_out: bfloat16 [1024, 640], P(('dp', 'fsdp')), may hold values from -0.75 to 0.75
- ff_narrow: bfloat16 [4096, 128], P(('dp', 'fsdp')), may hold values from -0.09375 to 0.09375
- ff_widen: bfloat16 [4096, 128], P(('dp', 'fsdp')), may hold values from -0.75 to 0.75
Outputs:
- output: bfloat16 [64, 512, 1024], P(('dp', 'fsdp'))
- input_grad: bfloat16 [64, 512, 1024], P(('dp', 'fsdp'))
- narrow_in_grad: float32 [1024, 640], P(('dp', 'fsdp'))
- widen_out_grad: float32 [1024, 640], P(('dp', 'fsdp'))
- ff_narrow_grad: float32 [4096, 128], P(('dp', 'fsdp'))
- ff_widen_grad: float32 [4096, 128], P(('dp', 'fsdp'))
The draws below stay inside these ranges and needn't reach their ends.
Inputs may be any that keep to these rules, and one draw needn't show every extreme that they name: `global_pos`: the 64 positions in each sequence's row are distinct.
All inputs are finite; a program needn't handle non-finite values.
Results may differ from the reference program's by a relative error of at most 0.015.
The reference program's roundings to bfloat16 on the way count: a program that leaves them out, or rounds other values in their place, can miss the bound.
Values may be sent and summed in bfloat16 or wider, within the bound.
A program may use at most 192 MiB of HBM per device.

```python
import math
import jax
import jax.numpy as jnp
from jax import lax

D = 1024
FF = 4096
HEADS = 16
HEAD_DIM = 64
SETS = 8
R = 16
LEN = 512
WINDOW = 512
NGLOB = 64
SEQS = 64


def draw_global_pos(key, part):
    row_keys = jax.random.split(jax.random.fold_in(key, 17), SEQS)
    rows = jax.vmap(lambda row_key: jax.random.permutation(row_key, LEN)[:NGLOB])(row_keys)
    return rows.astype(jnp.int32)


def set_ends(result, key, low, largest):
    dims = result.shape
    index_at = [jax.random.randint(jax.random.fold_in(key, axis), (), 0, dims[axis]) for axis in range(len(dims))]
    result = result.at[tuple(index_at)].set(low)
    longest = dims.index(max(dims))
    index_at[longest] = (index_at[longest] + 1) % dims[longest]
    return result.at[tuple(index_at)].set(largest)


def raised(entries, own_key, source, target, shards_of, factor):
    owner, partner = [(jnp.arange(entries.shape[axis_at]) // (entries.shape[axis_at] // shards_of)).reshape([-1 if axis == axis_at else 1 for axis in range(entries.ndim)]) for axis_at in (source, target)]
    chosen = jax.random.permutation(own_key, shards_of)[partner]
    strong = (owner == chosen) | (owner == (partner + shards_of // 2) % shards_of)
    return jnp.where(strong, factor * entries, entries)


def block_levels(key, shape, pieces, least, largest):
    loudness = 1.0
    for position, blocks in pieces:
        heights = jax.random.uniform(jax.random.fold_in(jax.random.fold_in(key, 6), position), (blocks,), jnp.float32, least / len(pieces), largest / len(pieces))
        loudness = loudness * jnp.repeat(jnp.exp(heights), shape[position] // blocks).reshape((-1,) + (1,) * (len(shape) - 1 - position))
    return loudness


def centred(rng, dims, width, limit, cuts=(), kind=jnp.bfloat16):
    array = jax.random.normal(rng, dims, jnp.float32) * width
    if len(cuts) > 0:
        array = block_levels(rng, dims, cuts, -0.22, 0.18) * array
    return jnp.clip(array, min=-limit, max=limit).astype(kind)


def noise_with(stream_key, dims, width, bound, pieces, heavy, kind=jnp.bfloat16):
    array = width * jax.random.normal(stream_key, dims, jnp.float32)
    if pieces:
        array = array * block_levels(stream_key, dims, pieces, -0.22, 0.18)
    return jnp.clip(raised(array, jax.random.fold_in(stream_key, 3), *heavy), -bound, bound).astype(kind)


def setup_inputs(seed: int = 0) -> dict:
    splits = jax.random.split(jax.random.key(seed), 15)
    tokens = noise_with(splits[0], (SEQS, LEN, D), 1.0, 6.0, ((0, 32),), (0, 2, 32, 2.75))
    cotangent = noise_with(splits[1], (SEQS, LEN, D), 1.0, 6.0, ((0, 32),), (0, 2, 32, 2.75))
    adapter_id = set_ends(jax.random.randint(splits[2], (SEQS,), 0, SETS), jax.random.fold_in(splits[2], 1), 0, SETS - 1).astype(jnp.int32)
    global_pos = draw_global_pos(jax.random.fold_in(splits[14], 71), 0)
    w_qkv = centred(splits[4], (D, 3 * D), D ** -0.5, 0.1875, ((0, 32),))
    w_out = centred(splits[5], (D, D), (D // 16) ** -0.5, 0.75, ((0, 32),))
    w_up = centred(splits[6], (D, FF), D ** -0.5, 0.1875, ((0, 32),))
    w_down = centred(splits[7], (FF, D), FF ** -0.5, 0.09375, ((0, 32),))
    norm_gain = jnp.clip(1.0 + 0.1 * jax.random.normal(splits[8], (D, 2), jnp.float32), 0.5, 1.5).astype(jnp.bfloat16)
    norm_bias = centred(splits[9], (D, 2), 0.5, 3.0, ((0, 32),))
    narrow_in = centred(splits[10], (D, 5 * SETS * R), D ** -0.5, 0.1875, ((0, 32),))
    widen_out = centred(splits[11], (D, 5 * SETS * R), (4 * R) ** -0.5, 0.75, ((0, 32),))
    ff_narrow = centred(splits[12], (FF, SETS * R), FF ** -0.5, 0.09375, ((0, 32),))
    ff_widen = centred(splits[13], (FF, SETS * R), (4 * R) ** -0.5, 0.75, ((0, 32),))
    return {"tokens": tokens, "cotangent": cotangent, "adapter_id": adapter_id, "global_pos": global_pos, "w_qkv": w_qkv, "w_out": w_out, "w_up": w_up, "w_down": w_down, "norm_gain": norm_gain, "norm_bias": norm_bias, "narrow_in": narrow_in, "widen_out": widen_out, "ff_narrow": ff_narrow, "ff_widen": ff_widen}


@jax.custom_vjp
def low(v):
    return lax.optimization_barrier(v.astype(jnp.bfloat16)).astype(jnp.float32)

@jax.custom_vjp
def low_back(v):
    return v

def low_keep(v):
    return (low(v), None)

def low_pass(kept, grad):
    return (grad,)

def back_keep(v):
    return (v, None)

def back_low(kept, grad):
    return (low(grad),)
low.defvjp(low_keep, low_pass)
low_back.defvjp(back_keep, back_low)
HIGH = lax.Precision.HIGHEST

def rounded(values):
    return low_back(low(values))

def normalize(values, gain, shift):
    center = values - lax.optimization_barrier(jnp.mean(values, axis=-1, keepdims=True))
    spread = lax.optimization_barrier(jnp.mean(center * center, axis=-1, keepdims=True))
    return center * lax.rsqrt(spread + 1e-12) * gain + shift

def block_layer(x_blk, choose, allowed, frozen, adapters):
    w_qkv, w_out, w_up, w_down, gains, shifts = frozen
    narrow_in, widen_out, ff_narrow, ff_widen = adapters
    blocks, length, model_width = x_blk.shape
    set_cols = choose.shape[-1]
    picker = choose[:, None, :]

    def adapter(inputs, a_mat, bt_mat):
        narrowed = rounded(jnp.einsum('bli,is->bls', inputs, a_mat, precision=HIGH) * picker)
        return jnp.einsum('bls,os->blo', narrowed, bt_mat, precision=HIGH)

    def project(inputs, weight):
        return jnp.einsum('bli,io->blo', inputs, weight, precision=HIGH)
    heads_all = []
    for slot in range(3):
        cols = slice(slot * set_cols, (slot + 1) * set_cols)
        projected = project(x_blk, w_qkv[:, slot * model_width:(slot + 1) * model_width]) + adapter(x_blk, narrow_in[:, cols], widen_out[:, cols])
        heads_all.append(rounded(projected).reshape(blocks, length, HEADS, HEAD_DIM))
    query, key_mat, value_mat = heads_all
    scores = low_back(jnp.einsum('bqhd,bkhd->bhqk', query, key_mat, precision=HIGH) * HEAD_DIM ** (-0.5))
    scores = jnp.where(allowed[:, None], scores, -1e+30)
    weights_attn = low(jax.nn.softmax(scores, axis=-1))
    mixed_out = jnp.einsum('bhqk,bkhd->bqhd', weights_attn, value_mat, precision=HIGH).reshape(blocks, length, model_width)
    mixed_out = rounded(mixed_out)
    cols_o = slice(3 * set_cols, 4 * set_cols)
    cols_f = slice(4 * set_cols, 5 * set_cols)
    attn_out = low_back(project(mixed_out, w_out) + adapter(mixed_out, narrow_in[:, cols_o], widen_out[:, cols_o]))
    normed = normalize(x_blk + attn_out, gains[:, 0], shifts[:, 0])
    normed_low = low(normed)
    pre_act = low_back(project(normed_low, w_up) + adapter(normed_low, narrow_in[:, cols_f], ff_widen))
    activation = low(jax.nn.gelu(pre_act, approximate=False))
    down_out = low_back(project(activation, w_down) + adapter(activation, ff_narrow, widen_out[:, cols_f]))
    return normalize(normed + down_out, gains[:, 1], shifts[:, 1])

def reference(tokens, cotangent, adapter_id, global_pos, w_qkv, w_out, w_up, w_down, norm_gain, norm_bias, narrow_in, widen_out, ff_narrow, ff_widen):
    frozen = tuple((w.astype(jnp.float32) for w in (w_qkv, w_out, w_up, w_down, norm_gain, norm_bias)))
    adapters = tuple((w.astype(jnp.float32) for w in (narrow_in, widen_out, ff_narrow, ff_widen)))
    set_cols = SETS * R
    choose_all = (jnp.arange(set_cols, dtype=jnp.int32)[None, :] // R == adapter_id[:, None]).astype(jnp.float32)
    positions = jnp.arange(LEN, dtype=jnp.int32)
    is_global = jnp.any(global_pos[:, :, None] == positions[None, None, :], axis=1)
    nearby = jnp.abs(positions[:, None] - positions[None, :]) <= WINDOW // 2
    group_size = math.gcd(SEQS, 4)
    blocks_count = SEQS // group_size
    x_all = tokens.astype(jnp.float32).reshape(blocks_count, group_size, LEN, D)
    choose_blocks = choose_all.reshape(blocks_count, group_size, set_cols)
    global_blocks = is_global.reshape(blocks_count, group_size, LEN)

    def forward(x_in, adapter_set):

        def one_step(carry, items):
            x_blk, choose, globals_blk = items
            allowed = nearby[None] | globals_blk[:, None, :] | globals_blk[:, :, None]
            return (carry, block_layer(x_blk, choose, allowed, frozen, adapter_set))
        _, outputs = lax.scan(jax.checkpoint(one_step), jnp.zeros((), jnp.float32), (x_in, choose_blocks, global_blocks))
        return outputs
    outputs, pullback = jax.vjp(forward, x_all, adapters)
    grad_x, grad_adapters = pullback(cotangent.astype(jnp.float32).reshape(blocks_count, group_size, LEN, D))
    return (outputs.reshape(SEQS, LEN, D).astype(jnp.bfloat16), grad_x.reshape(SEQS, LEN, D).astype(jnp.bfloat16), grad_adapters[0], grad_adapters[1], grad_adapters[2], grad_adapters[3])
```

```python
import functools, math
import jax
import jax.numpy as jnp
from jax import lax
from jax.experimental import pallas as pl
from jax.experimental.pallas import tpu as pltpu
from jax.sharding import PartitionSpec as P

MESH = pl.DeviceIdType.MESH


class Grid:
    def __init__(self, sizes):
        self.dp, self.fsdp = sizes["dp"], sizes["fsdp"]
        if (self.dp, self.fsdp) == (8, 4):
            self.dims = {"z": ("dp", 2, 4), "y": ("dp", 1, 2), "x": ("fsdp", 2, 2), "c": ("fsdp", 1, 2)}
        elif (self.dp, self.fsdp) == (64, 4):
            self.dims = {"z": ("dp", 8, 8), "y": ("dp", 2, 4), "x": ("fsdp", 1, 4), "c": ("dp", 1, 2)}
        else:
            self.dims = {"z": ("dp", 1, self.dp), "y": ("dp", 1, 1), "x": ("fsdp", self.fsdp, 1), "c": ("fsdp", 1, self.fsdp)}
        self.n = {k: v[2] for k, v in self.dims.items()}
        self.devices = self.dp * self.fsdp
        self.planes = self.devices // self.n["z"]

    def stride(self, k):
        axis, step, _ = self.dims[k]
        return step * (self.fsdp if axis == "dp" else 1)

    def here(self):
        idx = {"dp": lax.axis_index("dp"), "fsdp": lax.axis_index("fsdp")}
        return {k: (idx[axis] // step) % size for k, (axis, step, size) in self.dims.items()}

    def device(self, pos):
        out = {"dp": 0, "fsdp": 0}
        for k, (axis, step, _) in self.dims.items():
            out[axis] = out[axis] + pos[k] * step
        return out["dp"], out["fsdp"]

    def slot(self, y, x, c):
        return y * self.stride("y") + x * self.stride("x") + c * self.stride("c")


def barrier_with(grid, here):
    barrier = pltpu.get_barrier_semaphore()
    count = 0
    for k in ("z", "y", "x", "c"):
        n = grid.n[k]
        for step in range(1, n):
            to = (here[k] + step) % n
            pl.semaphore_signal(barrier, inc=1, device_id=grid.device({**here, k: to}), device_id_type=MESH)
            count += 1
    pl.semaphore_wait(barrier, count)


class Gather:
    @staticmethod
    def parts(grid):
        return grid.n["z"] if grid.n["z"] <= 4 else 1

    @staticmethod
    def sem_total(grid):
        z, a, b, c = (grid.n[k] for k in ("z", "y", "x", "c"))
        k = Gather.parts(grid)
        return z + k * a + k * a * b + a * b

    def __init__(self, grid, here, src, out, send, recv, local):
        self.g, self.here, self.src, self.out = grid, here, src, out
        self.send, self.recv, self.local = send, recv, local
        self.k = Gather.parts(grid)
        self.nz, self.n2, self.n3 = grid.n["z"], grid.n["y"], grid.n["x"]
        self.base2 = self.nz
        self.base3 = self.base2 + self.k * self.n2
        self.base4 = self.base3 + self.k * self.n2 * self.n3
        self.sends = []
        self.first = here["c"] == 0
        self.p2 = jnp.where(self.first, here["y"], here["x"])
        self.p3 = jnp.where(self.first, here["x"], here["y"])

    def dev(self, z=None, p2=None, p3=None, c=None):
        h = self.here
        p2 = self.p2 if p2 is None else p2
        p3 = self.p3 if p3 is None else p3
        return self.g.device({
            "z": h["z"] if z is None else z,
            "y": jnp.where(self.first, p2, p3),
            "x": jnp.where(self.first, p3, p2),
            "c": h["c"] if c is None else c,
        })

    def m(self, p2, p3):
        return self.g.slot(jnp.where(self.first, p2, p3), jnp.where(self.first, p3, p2), self.here["c"])

    def part(self, i):
        return (self.here["z"] ^ i) if self.k == self.nz and self.nz & (self.nz - 1) == 0 else None

    def block(self, z, p2, p3):
        return self.out.at[:, self.m(p2, p3)] if z is None else self.out.at[z, self.m(p2, p3)]

    def push(self, src, dst, sem, dev):
        copy = pltpu.make_async_remote_copy(src_ref=src, dst_ref=dst, send_sem=self.send.at[sem], recv_sem=self.recv.at[sem], device_id=dev, device_id_type=MESH)
        copy.start()
        self.sends.append(copy)

    def pull(self, dst, sem):
        pltpu.make_async_remote_copy(src_ref=dst, dst_ref=dst, send_sem=self.send.at[sem], recv_sem=self.recv.at[sem], device_id=self.dev(), device_id_type=MESH).wait_recv()

    def sem2(self, z, p2):
        return self.base2 + (0 if z is None else z * self.n2) + p2

    def sem3(self, z, p2, p3):
        return self.base3 + ((0 if z is None else z * self.n2) + p2) * self.n3 + p3

    def send2(self, z, src=None):
        ref = self.block(z, self.p2, self.p3)
        for d in range(1, self.n2):
            self.push(ref if src is None else src, ref, self.sem2(z, self.p2), self.dev(p2=(self.p2 + d) % self.n2))

    def send3(self, z, p2, src=None):
        ref = self.block(z, p2, self.p3)
        for d in range(1, self.n3):
            self.push(ref if src is None else src, ref, self.sem3(z, p2, self.p3), self.dev(p3=(self.p3 + d) % self.n3))

    def core(self, p2, p3):
        if self.g.n["c"] > 1:
            ref = self.block(None, p2, p3)
            y, x = jnp.where(self.first, p2, p3), jnp.where(self.first, p3, p2)
            self.push(ref, ref, self.base4 + y * self.n3 + x, self.dev(c=1 - self.here["c"]))

    def begin(self):
        z = self.here["z"]
        m0 = self.m(self.p2, self.p3)
        self.own = pltpu.make_async_copy(self.src, self.out.at[z, m0], self.local)
        self.own.start()
        for i in range(1, self.nz):
            to = self.here["z"] ^ i if self.nz & (self.nz - 1) == 0 else (z + i) % self.nz
            self.push(self.src, self.out.at[z, m0], z, self.dev(z=to))
        if self.part(0) is not None:
            self.send3(z, self.p2, self.src)
            self.send2(z, self.src)

    def z_step(self, i):
        z = self.here["z"] ^ i if self.nz & (self.nz - 1) == 0 else (self.here["z"] + i) % self.nz
        self.pull(self.out.at[z, self.m(self.p2, self.p3)], z)
        if self.part(i) is not None:
            self.send2(z)
            self.send3(z, self.p2)

    def z_end(self):
        self.own.wait()
        if self.part(0) is None:
            self.send2(None)
            self.send3(None, self.p2)
        self.core(self.p2, self.p3)

    def step2(self, i):
        z = self.part(i)
        for d in range(1, self.n2):
            q = (self.p2 + d) % self.n2
            self.pull(self.block(z, q, self.p3), self.sem2(z, q))
            self.send3(z, q)

    def end2(self):
        for d in range(1, self.n2):
            self.core((self.p2 + d) % self.n2, self.p3)

    def step3(self, j):
        p2 = (self.p2 + j) % self.n2
        for d in range(1, self.n3):
            q = (self.p3 + d) % self.n3
            for i in range(self.k):
                z = self.part(i)
                self.pull(self.block(z, p2, q), self.sem3(z, p2, q))
            self.core(p2, q)

    def end(self):
        if self.g.n["c"] > 1:
            for y in range(self.n2):
                for x in range(self.n3):
                    self.pull(self.out.at[:, self.g.slot(y, x, 1 - self.here["c"])], self.base4 + y * self.n3 + x)

    def steps(self):
        out = [self.begin]
        out += [functools.partial(self.z_step, i) for i in range(1, self.nz)] + [self.z_end]
        out += [functools.partial(self.step2, i) for i in range(self.k)] + [self.end2]
        out += [functools.partial(self.step3, j) for j in range(self.n2)]
        return out

    def finish(self):
        self.end()
        for copy in self.sends:
            copy.wait_send()


def run_skewed(all_steps, lag):
    count = max(len(s) for s in all_steps)
    for slot in range(count + lag * (len(all_steps) - 1)):
        for i, steps in enumerate(all_steps):
            k = slot - lag * i
            if 0 <= k < len(steps):
                steps[k]()

SETS = 8
R = 16


def normalize(values, gain, shift):
    center = values - jnp.mean(values, axis=-1, keepdims=True)
    spread = jnp.mean(center * center, axis=-1, keepdims=True)
    return center * lax.rsqrt(spread + 1e-12) * gain + shift


def against(left, right):
    return lax.dot_general(
        left, right, (((1,), (1,)), ((), ())), preferred_element_type=jnp.float32
    )


def over_rows(left, right):
    return lax.dot_general(
        left, right, (((0,), (0,)), ((), ())), preferred_element_type=jnp.float32
    )


def product(left, right):
    return jnp.dot(left, right, preferred_element_type=jnp.float32)


def gelu_exact(values):
    return jax.nn.gelu(values, approximate=False)


def gather_kernel(grid, count, lag, first, *refs):
    srcs, outs = refs[:count], refs[count:2*count]
    send, recv, local = refs[2*count:]
    here = grid.here()
    barrier_with(grid, here)
    gs = [Gather(grid, here, srcs[i], outs[i], send.at[i], recv.at[i], local.at[i]) for i in range(count)]
    steps = [g.steps() for g in gs]
    if first:
        for s in steps:
            s.pop(0)()
    run_skewed(steps, lag)
    for g in gs:
        g.finish()

def all_gather(grid, arrays, cid=0, lag=1, first=True):
    count = len(arrays)
    total = Gather.sem_total(grid)
    out_shape = [jax.ShapeDtypeStruct((grid.n["z"], grid.planes) + a.shape, a.dtype) for a in arrays]
    return pl.pallas_call(
        functools.partial(gather_kernel, grid, count, lag, first),
        out_shape=out_shape,
        in_specs=[pl.BlockSpec(memory_space=pltpu.VMEM)] * count,
        out_specs=[pl.BlockSpec(memory_space=pl.ANY)] * count,
        scratch_shapes=[pltpu.SemaphoreType.DMA((count, total)), pltpu.SemaphoreType.DMA((count, total)), pltpu.SemaphoreType.DMA((count,))],
        compiler_params=pltpu.CompilerParams(collective_id=cid, has_side_effects=True, vmem_limit_bytes=8*2**20),
        name="gather",
    )(*arrays)


class Scatter:
    @staticmethod
    def sem_total(grid):
        return 1 + grid.n["x"] + grid.n["y"] + grid.n["z"]

    @staticmethod
    def scratch(grid, shape, dtype=jnp.bfloat16):
        rows, cols = shape
        z, y, x = grid.n["z"], grid.n["y"], grid.n["x"]
        out = []
        if grid.n["c"] > 1:
            out += [pltpu.VMEM((y * x, z, rows, cols), dtype)] * 2
        out += [pltpu.VMEM((x, y, z, rows, cols), dtype)] * 2
        out += [pltpu.VMEM((y, z, rows, cols), dtype)] * 2
        out += [pltpu.VMEM((z, rows, cols), dtype)] * 2
        out += [pltpu.VMEM((y * x, z, rows, cols), jnp.float32)]
        return out

    def __init__(self, grid, here, src, put, bufs, send, recv):
        self.g, self.here, self.src, self.put, self.send, self.recv = grid, here, src, put, send, recv
        bufs = list(bufs)
        self.two = grid.n["c"] > 1
        self.s1, self.r1 = (bufs.pop(0), bufs.pop(0)) if self.two else (None, None)
        self.s2, self.r2, self.s3, self.r3, self.s4, self.r4, self.acc = bufs
        self.nz, self.n2, self.n3 = grid.n["z"], grid.n["y"], grid.n["x"]
        self.first = here["c"] == 0
        self.p2 = jnp.where(self.first, here["y"], here["x"])
        self.p3 = jnp.where(self.first, here["x"], here["y"])
        self.sends, self.pulls = [], []

    def dev(self, z=None, p2=None, p3=None, c=None):
        h = self.here
        p2 = self.p2 if p2 is None else p2
        p3 = self.p3 if p3 is None else p3
        return self.g.device({
            "z": h["z"] if z is None else z,
            "y": jnp.where(self.first, p2, p3),
            "x": jnp.where(self.first, p3, p2),
            "c": h["c"] if c is None else c,
        })

    def flat(self, p2, p3):
        return jnp.where(self.first, p2 * self.n3 + p3, p3 * self.n3 + p2)

    def push(self, src, dst, sem_s, sem_r, dev):
        copy = pltpu.make_async_remote_copy(src_ref=src, dst_ref=dst, send_sem=self.send.at[sem_s], recv_sem=self.recv.at[sem_r], device_id=dev, device_id_type=MESH)
        copy.start()
        self.sends.append(copy)

    def pull(self, dst, sem):
        pltpu.make_async_remote_copy(src_ref=dst, dst_ref=dst, send_sem=self.send.at[sem], recv_sem=self.recv.at[sem], device_id=self.dev(), device_id_type=MESH).wait_recv()

    def begin(self):
        c = self.here["c"]
        for y in range(self.n2):
            for x in range(self.n3):
                i = y * self.n3 + x
                if self.two:
                    self.s1[i] = self.src[:, self.g.slot(y, x, 1 - c)].astype(self.s1.dtype)
        if self.two:
            self.push(self.s1, self.r1, 0, 0, self.dev(c=1 - c))

    def step1(self):
        c = self.here["c"]
        if self.two:
            self.pull(self.r1, 0)
        for y in range(self.n2):
            for x in range(self.n3):
                i = y * self.n3 + x
                part = self.src[:, self.g.slot(y, x, c)]
                self.acc[i] = part + self.r1[i].astype(jnp.float32) if self.two else part
        for d in range(1, self.n3):
            q = (self.p3 + d) % self.n3
            for j in range(self.n2):
                self.s2[d, j] = self.acc[self.flat(j, q)].astype(self.s2.dtype)
            self.push(self.s2.at[d], self.r2.at[d], 1 + d, 1 + d, self.dev(p3=q))

    def step2(self):
        for d in range(1, self.n3):
            self.pull(self.r2.at[d], 1 + d)
        for j in range(self.n2):
            i = self.flat(j, self.p3)
            total = self.acc[i]
            for d in range(1, self.n3):
                total = total + self.r2[d, j].astype(jnp.float32)
            self.acc[i] = total
        base = 1 + self.n3
        for d in range(1, self.n2):
            q = (self.p2 + d) % self.n2
            self.s3[d] = self.acc[self.flat(q, self.p3)].astype(self.s3.dtype)
            self.push(self.s3.at[d], self.r3.at[d], base + d, base + d, self.dev(p2=q))

    def step3(self):
        base = 1 + self.n3
        i = self.flat(self.p2, self.p3)
        total = self.acc[i]
        for d in range(1, self.n2):
            self.pull(self.r3.at[d], base + d)
            total = total + self.r3[d].astype(jnp.float32)
        self.acc[i] = total
        base = base + self.n2
        self.s4[...] = total.astype(self.s4.dtype)
        z = self.here["z"]
        for d in range(1, self.nz):
            q = (z + d) % self.nz
            self.push(self.s4.at[q], self.r4.at[d], base + d, base + d, self.dev(z=q))

    def step4(self):
        base = 1 + self.n3 + self.n2
        total = self.acc[self.flat(self.p2, self.p3), self.here["z"]]
        for d in range(1, self.nz):
            self.pull(self.r4.at[d], base + d)
            total = total + self.r4[d].astype(jnp.float32)
        self.put(total)

    def steps(self):
        return [self.begin, self.step1, self.step2, self.step3, self.step4]

    def finish(self):
        for copy in self.sends:
            copy.wait_send()


def scatter_kernel(grid, places, nout, *refs):
    count = len(places)
    srcs, outs = refs[:count], refs[count:count + nout]
    rest = refs[count + nout:]
    send, recv = rest[:2]
    rest = rest[2:]
    per = len(rest) // count
    here = grid.here()
    barrier_with(grid, here)
    units = []
    for i, (o, col) in enumerate(places):
        def put(total, o=o, col=col):
            outs[o][:, col:col + total.shape[1]] = total
        units.append(Scatter(grid, here, srcs[i], put, rest[i * per:(i + 1) * per], send.at[i], recv.at[i]))
    run_skewed([u.steps() for u in units], 1)
    for u in units:
        u.finish()


def reduce_scatter(grid, arrays, places, outs, cid):
    count = len(arrays)
    views = [a.reshape(grid.n["z"], grid.planes, a.shape[0] // grid.devices, a.shape[1]) for a in arrays]
    total = Scatter.sem_total(grid)
    scratch = [pltpu.SemaphoreType.DMA((count, total)), pltpu.SemaphoreType.DMA((count, total))]
    for v in views:
        scratch += Scatter.scratch(grid, v.shape[2:])
    return pl.pallas_call(
        functools.partial(scatter_kernel, grid, places, len(outs)),
        out_shape=[jax.ShapeDtypeStruct(o, jnp.float32) for o in outs],
        in_specs=[pl.BlockSpec(memory_space=pltpu.VMEM)] * count,
        out_specs=[pl.BlockSpec(memory_space=pltpu.VMEM)] * len(outs),
        scratch_shapes=scratch,
        compiler_params=pltpu.CompilerParams(collective_id=cid, has_side_effects=True, vmem_limit_bytes=60 * 2**20),
        name="scatter",
    )(*views)

HD=64
def dotf(a,b,ca,cb):
    return lax.dot_general(a,b,(((ca,),(cb,)),((),())),preferred_element_type=jnp.float32)

def set_bias(bias, row, col, half):
    n=bias.shape[0]
    i=lax.broadcasted_iota(jnp.int32,(n,n),0); j=lax.broadcasted_iota(jnp.int32,(n,n),1)
    near=jnp.abs(i-j)<=half
    ok=near|(jnp.broadcast_to(row,(n,n))>0)|(jnp.broadcast_to(col,(n,n))>0)
    bias[...]=jnp.where(ok,0.0,-1e30)

def fwd_kernel(half,row_ref,col_ref,q_ref,k_ref,v_ref,o_ref,p_ref,bias):
    @pl.when(pl.program_id(1)==0)
    def _(): set_bias(bias,row_ref[0],col_ref[0],half)
    width=q_ref.shape[1]
    q=q_ref[...]; k=k_ref[...]
    vt=v_ref[...].T
    outs=[]
    for h in range(width//HD):
        c=(h*HD)//128*128
        lane=lax.broadcasted_iota(jnp.int32,(1,128),1)//HD
        keep=(lane==(h*HD-c)//HD)
        kh=jnp.where(keep,k[:,c:c+128],jnp.zeros((),k.dtype))*jnp.asarray(HD**-0.5,k.dtype)
        s=dotf(kh,q[:,c:c+128],1,1)+bias[...]
        top=jnp.max(s,axis=0,keepdims=True)
        e=jnp.exp(s-top)
        tot=jnp.sum(e,axis=0,keepdims=True)
        p=(e*(1.0/tot)).astype(jnp.bfloat16)
        p_ref[h]=p
        outs.append(dotf(vt[h*HD:(h+1)*HD],p,1,0))
    o_ref[...]=jnp.concatenate(outs,axis=0).T.astype(o_ref.dtype)

def attn_fwd(q,k,v,row,col,seqs,length,per=2):
    rows,width=q.shape; heads=width//HD
    w=per*HD
    spec=pl.BlockSpec((length,w),lambda s,h:(s,h))
    return pl.pallas_call(functools.partial(fwd_kernel,256),grid=(seqs,heads//per),
      in_specs=[pl.BlockSpec((1,1,length),lambda s,h:(s,0,0)),pl.BlockSpec((1,length,1),lambda s,h:(s,0,0)),spec,spec,spec],
      out_specs=[spec,pl.BlockSpec((None,per,length,length),lambda s,h:(s,h,0,0))],
      out_shape=[jax.ShapeDtypeStruct(q.shape,q.dtype),jax.ShapeDtypeStruct((seqs,heads,length,length),q.dtype)],
      scratch_shapes=[pltpu.VMEM((length,length),jnp.float32)],
      compiler_params=pltpu.CompilerParams(vmem_limit_bytes=48*2**20),name="attend")(row,col,q,k,v)

def bwd_kernel(q_ref,k_ref,v_ref,p_ref,d_ref,dq_ref,dk_ref,dv_ref):
    width=q_ref.shape[1]
    q=q_ref[...]; k=k_ref[...]; v=v_ref[...]; d=d_ref[...]
    scale=jnp.asarray(HD**-0.5,q.dtype)
    kt=(k*scale).T
    qs=q*scale
    dqs=[]; dks=[]; dvs=[]
    lane=lax.broadcasted_iota(jnp.int32,(1,128),1)//HD
    for h in range(width//HD):
        c=(h*HD)//128*128
        keep=(lane==(h*HD-c)//HD)
        vh=jnp.where(keep,v[:,c:c+128],jnp.zeros((),v.dtype))
        pb=p_ref[h]
        p=pb.astype(jnp.float32)
        dp=dotf(vh,d[:,c:c+128],1,1)
        t=p*dp
        inner=jnp.sum(t,axis=0,keepdims=True)
        ds=(t-p*inner).astype(jnp.bfloat16)
        dqs.append(dotf(kt[h*HD:(h+1)*HD],ds,1,0))
        dks.append(dotf(ds,qs[:,c:c+128],1,0))
        dvs.append(dotf(pb,d[:,c:c+128],1,0))
    dq_ref[...]=jnp.concatenate(dqs,axis=0).T.astype(dq_ref.dtype)
    for g in range(width//128):
        keep=lane==0
        dk_ref[:,g*128:(g+1)*128]=jnp.where(keep,dks[2*g],dks[2*g+1]).astype(dk_ref.dtype)
        dv_ref[:,g*128:(g+1)*128]=jnp.where(keep,dvs[2*g],dvs[2*g+1]).astype(dv_ref.dtype)

def attn_bwd(q,k,v,p,d,seqs,length,per=2):
    rows,width=q.shape; heads=width//HD; w=per*HD
    spec=pl.BlockSpec((length,w),lambda s,h:(s,h))
    return pl.pallas_call(bwd_kernel,grid=(seqs,heads//per),
      in_specs=[spec,spec,spec,pl.BlockSpec((None,per,length,length),lambda s,h:(s,h,0,0)),spec],
      out_specs=[spec]*3,out_shape=[jax.ShapeDtypeStruct(q.shape,q.dtype)]*3,
      compiler_params=pltpu.CompilerParams(vmem_limit_bytes=48*2**20),name="attend_back")(q,k,v,p,d)


def local(sizes, tokens, cotangent, adapter_id, global_pos, w_qkv, w_out, w_up, w_down, norm_gain, norm_bias,
          narrow_in, widen_out, ff_narrow, ff_widen):
    grid = Grid(sizes)
    small = jnp.concatenate([norm_gain, norm_bias], axis=1).T
    share = small.shape[1]
    small = jnp.pad(small, ((0, 12), (0, 128 - share)))
    got = all_gather(grid, [w_qkv, narrow_in, widen_out, small, w_out, w_up, w_down, ff_narrow, ff_widen], 0, 2, True)

    def whole(a):
        return a.reshape(-1, a.shape[-1])

    wq_full, a_full, b_full, small_full, wo_full, wu_full, wd_full, ffa_full, ffb_full = [whole(a) for a in got]
    norms = small_full.reshape(grid.devices, 16, 128)[:, :4, :share].transpose(1, 0, 2).reshape(4, grid.devices * share)
    norms = norms.astype(jnp.float32)
    gain_one, gain_two, shift_one, shift_two = norms[0], norms[1], norms[2], norms[3]
    seq_local, length, model_width = tokens.shape
    rows_all = seq_local * length
    set_cols = SETS * R
    chosen = (
        lax.broadcasted_iota(jnp.int32, (seq_local, set_cols), 1) // R == adapter_id[:, None]
    ).astype(jnp.float32)
    chosen = jnp.broadcast_to(chosen[:, None, :], (seq_local, length, set_cols)).reshape(rows_all, set_cols)
    chosen_three = jnp.concatenate([chosen, chosen, chosen], axis=1)
    positions = lax.broadcasted_iota(jnp.int32, (length,), 0)
    is_global = jnp.any(global_pos[:, :, None] == positions[None, None, :], axis=1).astype(jnp.float32)

    def cols_of(slot):
        return slice(slot * set_cols, (slot + 1) * set_cols)

    flat_in = tokens.reshape(rows_all, model_width)
    t_qkv = (product(flat_in, a_full[:, : 3 * set_cols]) * chosen_three).astype(jnp.bfloat16)
    projected = []
    for slot in range(3):
        summed = product(flat_in, wq_full[:, slot * model_width : (slot + 1) * model_width]) + against(
            t_qkv[:, cols_of(slot)], b_full[:, cols_of(slot)]
        )
        projected.append(summed.astype(jnp.bfloat16))
    query_low, key_low, value_low = projected
    mixed_flat, weights_low = attn_fwd(query_low, key_low, value_low, is_global[:, None, :], is_global[:, :, None], seq_local, length, 4)
    t_out = (product(mixed_flat, a_full[:, cols_of(3)]) * chosen).astype(jnp.bfloat16)
    attn_out = product(mixed_flat, wo_full) + against(t_out, b_full[:, cols_of(3)])
    resid = flat_in.astype(jnp.float32) + attn_out
    normed, norm_one_back = jax.vjp(lambda values: normalize(values, gain_one, shift_one), resid)
    normed_low = normed.astype(jnp.bfloat16)
    t_up = (product(normed_low, a_full[:, cols_of(4)]) * chosen).astype(jnp.bfloat16)
    pre_act = product(normed_low, wu_full) + against(t_up, ffb_full)
    cdf = 0.5 * (1.0 + lax.erf(pre_act * (0.5 ** 0.5)))
    act_low = (pre_act * cdf).astype(jnp.bfloat16)
    slope = cdf + pre_act * jnp.exp(-0.5 * pre_act * pre_act) * ((0.5 / math.pi) ** 0.5)
    act_low, slope = lax.optimization_barrier((act_low, slope))
    t_down = (product(act_low, ffa_full) * chosen).astype(jnp.bfloat16)
    down_out = product(act_low, wd_full) + against(t_down, b_full[:, cols_of(4)])
    final = normed + down_out
    result, norm_two_back = jax.vjp(lambda values: normalize(values, gain_two, shift_two), final)
    d_final = norm_two_back(cotangent.reshape(rows_all, model_width).astype(jnp.float32))[0]
    d_down = d_final.astype(jnp.bfloat16)
    dt_down = (product(d_down, b_full[:, cols_of(4)]) * chosen).astype(jnp.bfloat16)
    grad_b_down = over_rows(d_down, t_down)
    grad_ff_narrow = over_rows(act_low, dt_down)
    d_act = against(d_down, wd_full) + against(dt_down, ffa_full)
    d_pre = (d_act * slope).astype(jnp.bfloat16)
    dt_up = (product(d_pre, ffb_full) * chosen).astype(jnp.bfloat16)
    grad_ff_widen = over_rows(d_pre, t_up)
    grad_a_up = over_rows(normed_low, dt_up)
    d_normed = d_final + against(d_pre, wu_full) + against(dt_up, a_full[:, cols_of(4)])
    d_resid = norm_one_back(d_normed)[0]
    d_attn = d_resid.astype(jnp.bfloat16)
    dt_out = (product(d_attn, b_full[:, cols_of(3)]) * chosen).astype(jnp.bfloat16)
    grad_b_out = over_rows(d_attn, t_out)
    grad_a_out = over_rows(mixed_flat, dt_out)
    d_mixed = (against(d_attn, wo_full) + against(dt_out, a_full[:, cols_of(3)])).astype(jnp.bfloat16)
    d_parts = attn_bwd(query_low, key_low, value_low, weights_low, d_mixed, seq_local, length, 4)
    dt_parts = [
        (product(d_parts[slot], b_full[:, cols_of(slot)]) * chosen).astype(jnp.bfloat16) for slot in range(3)
    ]
    dt_qkv = jnp.concatenate(dt_parts, axis=1)
    grad_b_qkv = [over_rows(d_parts[slot], t_qkv[:, cols_of(slot)]) for slot in range(3)]
    grad_a_qkv = over_rows(flat_in, dt_qkv)
    d_input = d_resid + against(dt_qkv, a_full[:, : 3 * set_cols])
    for slot in range(3):
        d_input = d_input + against(d_parts[slot], wq_full[:, slot * model_width : (slot + 1) * model_width])
    rows_own, ff_own = model_width // grid.devices, ff_narrow.shape[0]
    late = reduce_scatter(
        grid, [grad_ff_narrow, grad_ff_widen, grad_a_out, grad_a_up, grad_b_out, grad_b_down],
        [(0, 0), (1, 0), (2, 0), (2, set_cols), (3, 0), (3, set_cols)],
        [(ff_own, set_cols), (ff_own, set_cols), (rows_own, 2 * set_cols), (rows_own, 2 * set_cols)], 1)
    early = reduce_scatter(
        grid, [grad_a_qkv] + grad_b_qkv, [(0, 0), (1, 0), (1, set_cols), (1, 2 * set_cols)],
        [(rows_own, 3 * set_cols), (rows_own, 3 * set_cols)], 2)
    return (
        result.reshape(seq_local, length, model_width).astype(jnp.bfloat16),
        d_input.reshape(seq_local, length, model_width).astype(jnp.bfloat16),
        jnp.concatenate([early[0], late[2]], axis=1),
        jnp.concatenate([early[1], late[3]], axis=1),
        late[0],
        late[1],
    )


def solution(mesh):
    rows = P(("dp", "fsdp"), None)
    cube = P(("dp", "fsdp"), None, None)
    in_specs = (cube, cube, P(("dp", "fsdp"))) + (rows,) * 11
    out_specs = (cube, cube) + (rows,) * 4
    return jax.shard_map(functools.partial(local, dict(mesh.shape)), mesh=mesh, in_specs=in_specs, out_specs=out_specs, check_vma=False)
```

```python
import functools, math
import jax
import jax.numpy as jnp
from jax import lax
from jax.experimental import pallas as pl
from jax.experimental.pallas import tpu as pltpu
from jax.sharding import PartitionSpec as P

MESH = pl.DeviceIdType.MESH


class Grid:
    def __init__(self, sizes):
        self.dp, self.fsdp = sizes["dp"], sizes["fsdp"]
        if (self.dp, self.fsdp) == (8, 4):
            self.dims = {"z": ("dp", 2, 4), "y": ("dp", 1, 2), "x": ("fsdp", 2, 2), "c": ("fsdp", 1, 2)}
        elif (self.dp, self.fsdp) == (64, 4):
            self.dims = {"z": ("dp", 8, 8), "y": ("dp", 2, 4), "x": ("fsdp", 1, 4), "c": ("dp", 1, 2)}
        else:
            self.dims = {"z": ("dp", 1, self.dp), "y": ("dp", 1, 1), "x": ("fsdp", self.fsdp, 1), "c": ("fsdp", 1, self.fsdp)}
        self.n = {k: v[2] for k, v in self.dims.items()}
        self.devices = self.dp * self.fsdp
        self.planes = self.devices // self.n["z"]

    def stride(self, k):
        axis, step, _ = self.dims[k]
        return step * (self.fsdp if axis == "dp" else 1)

    def here(self):
        idx = {"dp": lax.axis_index("dp"), "fsdp": lax.axis_index("fsdp")}
        return {k: (idx[axis] // step) % size for k, (axis, step, size) in self.dims.items()}

    def device(self, pos):
        out = {"dp": 0, "fsdp": 0}
        for k, (axis, step, _) in self.dims.items():
            out[axis] = out[axis] + pos[k] * step
        return out["dp"], out["fsdp"]

    def slot(self, y, x, c):
        return y * self.stride("y") + x * self.stride("x") + c * self.stride("c")


def barrier_with(grid, here):
    barrier = pltpu.get_barrier_semaphore()
    count = 0
    for k in ("z", "y", "x", "c"):
        n = grid.n[k]
        for step in range(1, n):
            to = (here[k] + step) % n
            pl.semaphore_signal(barrier, inc=1, device_id=grid.device({**here, k: to}), device_id_type=MESH)
            count += 1
    pl.semaphore_wait(barrier, count)


class Gather:
    @staticmethod
    def parts(grid):
        return grid.n["z"] if grid.n["z"] <= 4 else 1

    @staticmethod
    def sem_total(grid):
        z, a, b, c = (grid.n[k] for k in ("z", "y", "x", "c"))
        k = Gather.parts(grid)
        return z + k * a + k * a * b + a * b

    def __init__(self, grid, here, src, out, send, recv, local):
        self.g, self.here, self.src, self.out = grid, here, src, out
        self.send, self.recv, self.local = send, recv, local
        self.k = Gather.parts(grid)
        self.nz, self.n2, self.n3 = grid.n["z"], grid.n["y"], grid.n["x"]
        self.base2 = self.nz
        self.base3 = self.base2 + self.k * self.n2
        self.base4 = self.base3 + self.k * self.n2 * self.n3
        self.sends = []
        self.first = here["c"] == 0
        self.p2 = jnp.where(self.first, here["y"], here["x"])
        self.p3 = jnp.where(self.first, here["x"], here["y"])

    def dev(self, z=None, p2=None, p3=None, c=None):
        h = self.here
        p2 = self.p2 if p2 is None else p2
        p3 = self.p3 if p3 is None else p3
        return self.g.device({
            "z": h["z"] if z is None else z,
            "y": jnp.where(self.first, p2, p3),
            "x": jnp.where(self.first, p3, p2),
            "c": h["c"] if c is None else c,
        })

    def m(self, p2, p3):
        return self.g.slot(jnp.where(self.first, p2, p3), jnp.where(self.first, p3, p2), self.here["c"])

    def part(self, i):
        return (self.here["z"] ^ i) if self.k == self.nz and self.nz & (self.nz - 1) == 0 else None

    def block(self, z, p2, p3):
        return self.out.at[:, self.m(p2, p3)] if z is None else self.out.at[z, self.m(p2, p3)]

    def copy(self, src, dst, sem, dev):
        return pltpu.make_async_remote_copy(src_ref=src, dst_ref=dst, send_sem=self.send.at[sem], recv_sem=self.recv.at[sem], device_id=dev, device_id_type=MESH)

    def pull(self, dst, sem):
        self.copy(dst, dst, sem, self.dev()).wait_recv()

    def sem2(self, z, p2):
        return self.base2 + (0 if z is None else z * self.n2) + p2

    def sem3(self, z, p2, p3):
        return self.base3 + ((0 if z is None else z * self.n2) + p2) * self.n3 + p3

    def to2(self, z, src=None):
        ref = self.block(z, self.p2, self.p3)
        return [self.copy(ref if src is None else src, ref, self.sem2(z, self.p2), self.dev(p2=(self.p2 + d) % self.n2)) for d in range(1, self.n2)]

    def to3(self, z, p2, src=None):
        ref = self.block(z, p2, self.p3)
        return [self.copy(ref if src is None else src, ref, self.sem3(z, p2, self.p3), self.dev(p3=(self.p3 + d) % self.n3)) for d in range(1, self.n3)]

    def to_core(self, p2, p3):
        if self.g.n["c"] == 1:
            return []
        ref = self.block(None, p2, p3)
        y, x = jnp.where(self.first, p2, p3), jnp.where(self.first, p3, p2)
        return [self.copy(ref, ref, self.base4 + y * self.n3 + x, self.dev(c=1 - self.here["c"]))]

    def line(self, i):
        z = self.here["z"]
        return z ^ i if self.nz & (self.nz - 1) == 0 else (z + i) % self.nz

    def own(self):
        return pltpu.make_async_copy(self.src, self.out.at[self.here["z"], self.m(self.p2, self.p3)], self.local)

    def begin(self):
        z = self.here["z"]
        m0 = self.m(self.p2, self.p3)
        out = [self.copy(self.src, self.out.at[z, m0], z, self.dev(z=self.line(i))) for i in range(1, self.nz)]
        if self.part(0) is not None:
            out += self.to3(z, self.p2, self.src) + self.to2(z, self.src)
        return out

    def wait_z(self, i):
        z = self.line(i)
        self.pull(self.out.at[z, self.m(self.p2, self.p3)], z)

    def after_z(self, i):
        return self.to2(self.part(i)) + self.to3(self.part(i), self.p2) if self.part(i) is not None else []

    def after_line(self):
        out = [] if self.part(0) is not None else self.to2(None) + self.to3(None, self.p2)
        return out + self.to_core(self.p2, self.p3)

    def wait2(self, i):
        z = self.part(i)
        for d in range(1, self.n2):
            q = (self.p2 + d) % self.n2
            self.pull(self.block(z, q, self.p3), self.sem2(z, q))

    def after2(self, i):
        return [c for d in range(1, self.n2) for c in self.to3(self.part(i), (self.p2 + d) % self.n2)]

    def after_all2(self):
        return [c for d in range(1, self.n2) for c in self.to_core((self.p2 + d) % self.n2, self.p3)]

    def wait3(self, j):
        p2 = (self.p2 + j) % self.n2
        for d in range(1, self.n3):
            q = (self.p3 + d) % self.n3
            for i in range(self.k):
                z = self.part(i)
                self.pull(self.block(z, p2, q), self.sem3(z, p2, q))

    def after3(self, j):
        p2 = (self.p2 + j) % self.n2
        return [c for d in range(1, self.n3) for c in self.to_core(p2, (self.p3 + d) % self.n3)]

    def pairs(self):
        part = functools.partial
        out = [(lambda: self.own().start(), self.begin)]
        out += [(part(self.wait_z, i), part(self.after_z, i)) for i in range(1, self.nz)]
        out += [(lambda: self.own().wait(), self.after_line)]
        out += [(part(self.wait2, i), part(self.after2, i)) for i in range(self.k)]
        out += [(lambda: None, self.after_all2)]
        out += [(part(self.wait3, j), part(self.after3, j)) for j in range(self.n2)]
        return out

    def steps(self):
        def act(wait, copies):
            wait()
            for c in copies():
                c.start()
        return [functools.partial(act, *p) for p in self.pairs()] + [self.arrived]

    def arrived(self):
        if self.g.n["c"] > 1:
            for y in range(self.n2):
                for x in range(self.n3):
                    self.pull(self.out.at[:, self.g.slot(y, x, 1 - self.here["c"])], self.base4 + y * self.n3 + x)

    def finish(self):
        for _, copies in self.pairs():
            for c in copies():
                c.wait_send()


def skewed(all_steps, lag):
    count = max(len(s) for s in all_steps)
    out = []
    for slot in range(count + lag * (len(all_steps) - 1)):
        for i, steps in enumerate(all_steps):
            k = slot - lag * i
            if 0 <= k < len(steps):
                out.append((i, steps[k]))
    return out


def run_skewed(all_steps, lag):
    for _, step in skewed(all_steps, lag):
        step()

SETS = 8
R = 16


def normalize(values, gain, shift):
    center = values - jnp.mean(values, axis=-1, keepdims=True)
    spread = jnp.mean(center * center, axis=-1, keepdims=True)
    return center * lax.rsqrt(spread + 1e-12) * gain + shift


def against(left, right):
    return lax.dot_general(
        left, right, (((1,), (1,)), ((), ())), preferred_element_type=jnp.float32
    )


def over_rows(left, right):
    return lax.dot_general(
        left, right, (((0,), (0,)), ((), ())), preferred_element_type=jnp.float32
    )


def product(left, right):
    return jnp.dot(left, right, preferred_element_type=jnp.float32)


def gelu_exact(values):
    return jax.nn.gelu(values, approximate=False)


def gather_kernel(grid, count, lag, first, *refs):
    srcs, outs = refs[:count], refs[count:2*count]
    send, recv, local = refs[2*count:]
    here = grid.here()
    barrier_with(grid, here)
    gs = [Gather(grid, here, srcs[i], outs[i], send.at[i], recv.at[i], local.at[i]) for i in range(count)]
    steps = [g.steps() for g in gs]
    if first:
        for s in steps:
            s.pop(0)()
    run_skewed(steps, lag)
    for g in gs:
        g.finish()

def all_gather(grid, arrays, cid=0, lag=1, first=True):
    count = len(arrays)
    total = Gather.sem_total(grid)
    out_shape = [jax.ShapeDtypeStruct((grid.n["z"], grid.planes) + a.shape, a.dtype) for a in arrays]
    return pl.pallas_call(
        functools.partial(gather_kernel, grid, count, lag, first),
        out_shape=out_shape,
        in_specs=[pl.BlockSpec(memory_space=pltpu.VMEM)] * count,
        out_specs=[pl.BlockSpec(memory_space=pl.ANY)] * count,
        scratch_shapes=[pltpu.SemaphoreType.DMA((count, total)), pltpu.SemaphoreType.DMA((count, total)), pltpu.SemaphoreType.DMA((count,))],
        compiler_params=pltpu.CompilerParams(collective_id=cid, has_side_effects=True, vmem_limit_bytes=8*2**20),
        name="gather",
    )(*arrays)


class Scatter:
    @staticmethod
    def sem_total(grid):
        return 1 + grid.n["x"] + grid.n["y"] + grid.n["z"]

    @staticmethod
    def scratch(grid, shape, dtype=jnp.bfloat16):
        rows, cols = shape
        z, y, x = grid.n["z"], grid.n["y"], grid.n["x"]
        out = []
        if grid.n["c"] > 1:
            out += [pltpu.VMEM((y * x, z, rows, cols), dtype)] * 2
        out += [pltpu.VMEM((x, y, z, rows, cols), dtype)] * 2
        out += [pltpu.VMEM((y, z, rows, cols), dtype)] * 2
        out += [pltpu.VMEM((z, rows, cols), dtype)] * 2
        out += [pltpu.VMEM((y * x, z, rows, cols), jnp.float32)]
        return out

    def __init__(self, grid, here, src, put, bufs, send, recv):
        self.g, self.here, self.src, self.put, self.send, self.recv = grid, here, src, put, send, recv
        bufs = list(bufs)
        self.two = grid.n["c"] > 1
        self.s1, self.r1 = (bufs.pop(0), bufs.pop(0)) if self.two else (None, None)
        self.s2, self.r2, self.s3, self.r3, self.s4, self.r4, self.acc = bufs
        self.nz, self.n2, self.n3 = grid.n["z"], grid.n["y"], grid.n["x"]
        self.first = here["c"] == 0
        self.p2 = jnp.where(self.first, here["y"], here["x"])
        self.p3 = jnp.where(self.first, here["x"], here["y"])
        self.sends, self.pulls = [], []

    def dev(self, z=None, p2=None, p3=None, c=None):
        h = self.here
        p2 = self.p2 if p2 is None else p2
        p3 = self.p3 if p3 is None else p3
        return self.g.device({
            "z": h["z"] if z is None else z,
            "y": jnp.where(self.first, p2, p3),
            "x": jnp.where(self.first, p3, p2),
            "c": h["c"] if c is None else c,
        })

    def flat(self, p2, p3):
        return jnp.where(self.first, p2 * self.n3 + p3, p3 * self.n3 + p2)

    def push(self, src, dst, sem_s, sem_r, dev):
        copy = pltpu.make_async_remote_copy(src_ref=src, dst_ref=dst, send_sem=self.send.at[sem_s], recv_sem=self.recv.at[sem_r], device_id=dev, device_id_type=MESH)
        copy.start()
        self.sends.append(copy)

    def pull(self, dst, sem):
        pltpu.make_async_remote_copy(src_ref=dst, dst_ref=dst, send_sem=self.send.at[sem], recv_sem=self.recv.at[sem], device_id=self.dev(), device_id_type=MESH).wait_recv()

    def begin(self):
        c = self.here["c"]
        for y in range(self.n2):
            for x in range(self.n3):
                i = y * self.n3 + x
                if self.two:
                    self.s1[i] = self.src[:, self.g.slot(y, x, 1 - c)].astype(self.s1.dtype)
        if self.two:
            self.push(self.s1, self.r1, 0, 0, self.dev(c=1 - c))

    def step1(self):
        c = self.here["c"]
        if self.two:
            self.pull(self.r1, 0)
        for y in range(self.n2):
            for x in range(self.n3):
                i = y * self.n3 + x
                part = self.src[:, self.g.slot(y, x, c)]
                self.acc[i] = part + self.r1[i].astype(jnp.float32) if self.two else part
        for d in range(1, self.n3):
            q = (self.p3 + d) % self.n3
            for j in range(self.n2):
                self.s2[d, j] = self.acc[self.flat(j, q)].astype(self.s2.dtype)
            self.push(self.s2.at[d], self.r2.at[d], 1 + d, 1 + d, self.dev(p3=q))

    def step2(self):
        for d in range(1, self.n3):
            self.pull(self.r2.at[d], 1 + d)
        for j in range(self.n2):
            i = self.flat(j, self.p3)
            total = self.acc[i]
            for d in range(1, self.n3):
                total = total + self.r2[d, j].astype(jnp.float32)
            self.acc[i] = total
        base = 1 + self.n3
        for d in range(1, self.n2):
            q = (self.p2 + d) % self.n2
            self.s3[d] = self.acc[self.flat(q, self.p3)].astype(self.s3.dtype)
            self.push(self.s3.at[d], self.r3.at[d], base + d, base + d, self.dev(p2=q))

    def step3(self):
        base = 1 + self.n3
        i = self.flat(self.p2, self.p3)
        total = self.acc[i]
        for d in range(1, self.n2):
            self.pull(self.r3.at[d], base + d)
            total = total + self.r3[d].astype(jnp.float32)
        self.acc[i] = total
        base = base + self.n2
        self.s4[...] = total.astype(self.s4.dtype)
        z = self.here["z"]
        for d in range(1, self.nz):
            q = (z + d) % self.nz
            self.push(self.s4.at[q], self.r4.at[d], base + d, base + d, self.dev(z=q))

    def step4(self):
        base = 1 + self.n3 + self.n2
        total = self.acc[self.flat(self.p2, self.p3), self.here["z"]]
        for d in range(1, self.nz):
            self.pull(self.r4.at[d], base + d)
            total = total + self.r4[d].astype(jnp.float32)
        self.put(total)

    def steps(self):
        return [self.begin, self.step1, self.step2, self.step3, self.step4]

    def finish(self):
        for copy in self.sends:
            copy.wait_send()


def scatter_kernel(grid, places, nout, *refs):
    count = len(places)
    srcs, outs = refs[:count], refs[count:count + nout]
    rest = refs[count + nout:]
    send, recv = rest[:2]
    rest = rest[2:]
    per = len(rest) // count
    here = grid.here()
    barrier_with(grid, here)
    units = []
    for i, (o, col) in enumerate(places):
        def put(total, o=o, col=col):
            outs[o][:, col:col + total.shape[1]] = total
        units.append(Scatter(grid, here, srcs[i], put, rest[i * per:(i + 1) * per], send.at[i], recv.at[i]))
    run_skewed([u.steps() for u in units], 1)
    for u in units:
        u.finish()


def reduce_scatter(grid, arrays, places, outs, cid):
    count = len(arrays)
    views = [a.reshape(grid.n["z"], grid.planes, a.shape[0] // grid.devices, a.shape[1]) for a in arrays]
    total = Scatter.sem_total(grid)
    scratch = [pltpu.SemaphoreType.DMA((count, total)), pltpu.SemaphoreType.DMA((count, total))]
    for v in views:
        scratch += Scatter.scratch(grid, v.shape[2:])
    return pl.pallas_call(
        functools.partial(scatter_kernel, grid, places, len(outs)),
        out_shape=[jax.ShapeDtypeStruct(o, jnp.float32) for o in outs],
        in_specs=[pl.BlockSpec(memory_space=pltpu.VMEM)] * count,
        out_specs=[pl.BlockSpec(memory_space=pltpu.VMEM)] * len(outs),
        scratch_shapes=scratch,
        compiler_params=pltpu.CompilerParams(collective_id=cid, has_side_effects=True, vmem_limit_bytes=60 * 2**20),
        name="scatter",
    )(*views)


HD=64
def dotf(a,b,ca,cb):
    return lax.dot_general(a,b,(((ca,),(cb,)),((),())),preferred_element_type=jnp.float32)

def set_bias(bias, row, col, half):
    n=bias.shape[0]
    i=lax.broadcasted_iota(jnp.int32,(n,n),0); j=lax.broadcasted_iota(jnp.int32,(n,n),1)
    near=jnp.abs(i-j)<=half
    ok=near|(jnp.broadcast_to(row,(n,n))>0)|(jnp.broadcast_to(col,(n,n))>0)
    bias[...]=jnp.where(ok,0.0,-1e30)

def fwd_kernel(half,row_ref,col_ref,q_ref,k_ref,v_ref,o_ref,p_ref,bias):
    @pl.when(pl.program_id(1)==0)
    def _(): set_bias(bias,row_ref[0],col_ref[0],half)
    width=q_ref.shape[1]
    q=q_ref[...]; k=k_ref[...]
    vt=v_ref[...].T
    outs=[]
    for h in range(width//HD):
        c=(h*HD)//128*128
        lane=lax.broadcasted_iota(jnp.int32,(1,128),1)//HD
        keep=(lane==(h*HD-c)//HD)
        kh=jnp.where(keep,k[:,c:c+128],jnp.zeros((),k.dtype))*jnp.asarray(HD**-0.5,k.dtype)
        s=dotf(kh,q[:,c:c+128],1,1)+bias[...]
        top=jnp.max(s,axis=0,keepdims=True)
        e=jnp.exp(s-top)
        tot=jnp.sum(e,axis=0,keepdims=True)
        p=(e*(1.0/tot)).astype(jnp.bfloat16)
        p_ref[h]=p
        outs.append(dotf(vt[h*HD:(h+1)*HD],p,1,0))
    o_ref[...]=jnp.concatenate(outs,axis=0).T.astype(o_ref.dtype)

def attn_fwd(q,k,v,row,col,seqs,length,per=2):
    rows,width=q.shape; heads=width//HD
    w=per*HD
    spec=pl.BlockSpec((length,w),lambda s,h:(s,h))
    return pl.pallas_call(functools.partial(fwd_kernel,256),grid=(seqs,heads//per),
      in_specs=[pl.BlockSpec((1,1,length),lambda s,h:(s,0,0)),pl.BlockSpec((1,length,1),lambda s,h:(s,0,0)),spec,spec,spec],
      out_specs=[spec,pl.BlockSpec((None,per,length,length),lambda s,h:(s,h,0,0))],
      out_shape=[jax.ShapeDtypeStruct(q.shape,q.dtype),jax.ShapeDtypeStruct((seqs,heads,length,length),q.dtype)],
      scratch_shapes=[pltpu.VMEM((length,length),jnp.float32)],
      compiler_params=pltpu.CompilerParams(vmem_limit_bytes=48*2**20),name="attend")(row,col,q,k,v)

def bwd_kernel(q_ref,k_ref,v_ref,p_ref,d_ref,dq_ref,dk_ref,dv_ref):
    width=q_ref.shape[1]
    q=q_ref[...]; k=k_ref[...]; v=v_ref[...]; d=d_ref[...]
    scale=jnp.asarray(HD**-0.5,q.dtype)
    kt=(k*scale).T
    qs=q*scale
    dqs=[]; dks=[]; dvs=[]
    lane=lax.broadcasted_iota(jnp.int32,(1,128),1)//HD
    for h in range(width//HD):
        c=(h*HD)//128*128
        keep=(lane==(h*HD-c)//HD)
        vh=jnp.where(keep,v[:,c:c+128],jnp.zeros((),v.dtype))
        pb=p_ref[h]
        p=pb.astype(jnp.float32)
        dp=dotf(vh,d[:,c:c+128],1,1)
        t=p*dp
        inner=jnp.sum(t,axis=0,keepdims=True)
        ds=(t-p*inner).astype(jnp.bfloat16)
        dqs.append(dotf(kt[h*HD:(h+1)*HD],ds,1,0))
        dks.append(dotf(ds,qs[:,c:c+128],1,0))
        dvs.append(dotf(pb,d[:,c:c+128],1,0))
    dq_ref[...]=jnp.concatenate(dqs,axis=0).T.astype(dq_ref.dtype)
    for g in range(width//128):
        keep=lane==0
        dk_ref[:,g*128:(g+1)*128]=jnp.where(keep,dks[2*g],dks[2*g+1]).astype(dk_ref.dtype)
        dv_ref[:,g*128:(g+1)*128]=jnp.where(keep,dvs[2*g],dvs[2*g+1]).astype(dv_ref.dtype)

def attn_bwd(q,k,v,p,d,seqs,length,per=2):
    rows,width=q.shape; heads=width//HD; w=per*HD
    spec=pl.BlockSpec((length,w),lambda s,h:(s,h))
    return pl.pallas_call(bwd_kernel,grid=(seqs,heads//per),
      in_specs=[spec,spec,spec,pl.BlockSpec((None,per,length,length),lambda s,h:(s,h,0,0)),spec],
      out_specs=[spec]*3,out_shape=[jax.ShapeDtypeStruct(q.shape,q.dtype)]*3,
      compiler_params=pltpu.CompilerParams(vmem_limit_bytes=48*2**20),name="attend_back")(q,k,v,p,d)


BF = jnp.bfloat16
F32 = jnp.float32

def flat2(v):
    return v.reshape(v.shape[0] * v.shape[1] * v.shape[2], v.shape[3])

def whole_rows(ref, c0, c1):
    return flat2(ref[:, :, :, c0:c1])

UNITS = ("small", "ab", "qkv", "out", "up0", "ff", "up1", "up2", "up3", "dn0", "dn1", "dn2", "dn3")
NCH = 4

def forward_kernel(grid, lag, *refs):
    n_in = 4 + 7
    (x, pick, row, col, s_small, s_ab, s_qkv, s_out, s_up, s_ff, s_dn) = refs[:n_in]
    outs = refs[n_in:n_in + 18]
    (g_small, g_ab, g_qkv, g_out, g_up, g_ff, g_dn, o_q, o_k, o_v, o_p, o_mix, o_h, o_f, o_yb, o_t, o_gb, o_sl) = outs
    (b_small, b_ab, b_qkv, b_out, b_ff, b_w, v_q, v_k, v_v, stage, bias, v_mix, v_h, v_f, v_yb, v_t, v_gb, tacc,
     send, recv, local, lsem, osem, ssem) = refs[n_in + 18:]
    rows, width = x.shape
    length = bias.shape[0]
    seqs = rows // length
    cols = pick.shape[2]
    here = grid.here()
    barrier_with(grid, here)
    spots = {"small": (s_small, g_small), "ab": (s_ab, g_ab), "qkv": (s_qkv, g_qkv), "out": (s_out, g_out), "ff": (s_ff, g_ff)}
    cw, dw = s_up.shape[1] // NCH, s_dn.shape[1] // NCH
    for j in range(NCH):
        spots["up%d" % j] = (s_up.at[:, j * cw:(j + 1) * cw], g_up.at[j])
        spots["dn%d" % j] = (s_dn.at[:, j * dw:(j + 1) * dw], g_dn.at[j])
    units = [Gather(grid, here, *spots[n], send.at[i], recv.at[i], local.at[i]) for i, n in enumerate(UNITS)]
    order = skewed([u.steps() for u in units], lag)
    state = {"at": 0}
    last = {i: max(k for k, (j, _) in enumerate(order) if j == i) for i in range(len(units))}

    def pump(count):
        end = min(state["at"] + count, len(order))
        for k in range(state["at"], end):
            order[k][1]()
        state["at"] = end

    def need(name):
        pump(max(0, last[UNITS.index(name)] + 1 - state["at"]))

    def load(src, dst, k):
        return pltpu.make_async_copy(src, dst, lsem.at[k])

    need("ab")
    c_small, c_ab = load(g_small, b_small, 0), load(g_ab, b_ab, 1)
    c_small.start()
    c_ab.start()
    need("qkv")
    c_qkv = load(g_qkv, b_qkv, 2)
    c_qkv.start()
    c_small.wait()
    c_ab.wait()
    c_qkv.wait()

    step = 256
    blocks = rows // step

    def rows_at(r):
        return pl.ds(pl.multiple_of(r * step, step), step)

    def picked(r):
        return pick[(r * step) // length]

    for slot, dst in enumerate((v_q, v_k, v_v)):
        @pl.loop(0, blocks)
        def _(r, slot=slot, dst=dst):
            at = rows_at(r)
            xa = x[at, :]
            t = (jnp.dot(xa, whole_rows(b_ab, slot * cols, (slot + 1) * cols), preferred_element_type=F32) * picked(r)).astype(BF)
            v_t[at, slot * cols:(slot + 1) * cols] = t
            acc = jnp.dot(xa, whole_rows(b_qkv, slot * width, (slot + 1) * width), preferred_element_type=F32)
            acc = acc + dotf(t, whole_rows(b_ab, (5 + slot) * cols, (6 + slot) * cols), 1, 1)
            dst[at, :] = acc.astype(BF)
        pump(3)
    saves = [pltpu.make_async_copy(v_q, o_q, osem.at[0]), pltpu.make_async_copy(v_k, o_k, osem.at[1]), pltpu.make_async_copy(v_v, o_v, osem.at[2])]
    for c in saves:
        c.start()

    per = 4
    groups = width // (per * HD)
    total = seqs * groups
    chunks = []
    left = last[UNITS.index("up2")] - state["at"]
    base = state["at"]
    share = max(1, left // total)

    def save_p(i, slot):
        return pltpu.make_async_copy(stage.at[slot], o_p.at[i], ssem.at[slot])

    def attend(i, carry):
        seq, hp = i // groups, i % groups
        @pl.when(hp == 0)
        def _():
            set_bias(bias, row[seq], col[seq], length // 2)
        slot = i % 2
        @pl.when(i >= 2)
        def _():
            save_p(i - 2, slot).wait()
        at = pl.ds(pl.multiple_of(seq * length, length), length)
        q = v_q[at, pl.ds(pl.multiple_of(hp * per * HD, per * HD), per * HD)]
        k = v_k[at, pl.ds(pl.multiple_of(hp * per * HD, per * HD), per * HD)]
        vt = v_v[at, pl.ds(pl.multiple_of(hp * per * HD, per * HD), per * HD)].T
        got = []
        lane = lax.broadcasted_iota(jnp.int32, (1, 128), 1) // HD
        for h in range(per):
            c = (h * HD) // 128 * 128
            kh = jnp.where(lane == (h * HD - c) // HD, k[:, c:c + 128], jnp.zeros((), BF)) * jnp.asarray(HD ** -0.5, BF)
            s = dotf(kh, q[:, c:c + 128], 1, 1) + bias[...]
            e = jnp.exp(s - jnp.max(s, axis=0, keepdims=True))
            p = (e * (1.0 / jnp.sum(e, axis=0, keepdims=True))).astype(BF)
            stage[slot, (h // 2) * length:(h // 2 + 1) * length, (h % 2) * length:(h % 2 + 1) * length] = p
            got.append(dotf(vt[h * HD:(h + 1) * HD], p, 1, 0))
        v_mix[at, pl.ds(pl.multiple_of(hp * per * HD, per * HD), per * HD)] = jnp.concatenate(got, axis=0).T.astype(BF)
        save_p(i, slot).start()
        for n in range(total):
            lo, hi = base + n * share, base + (n + 1) * share
            @pl.when(i == n)
            def _():
                for k2 in range(lo, hi):
                    order[k2][1]()
        return carry

    lax.fori_loop(0, total, attend, 0)
    state["at"] = base + share * total
    save_mix = pltpu.make_async_copy(v_mix, o_mix, osem.at[3])
    save_mix.start()

    need("out")
    c_out = load(g_out, b_out, 3)
    c_out.start()
    per_group = grid.devices // (width // 128)
    small = b_small[...].reshape(width // 128, per_group, 16, 128).astype(F32).sum(axis=1)
    norms = jnp.concatenate([small[g] for g in range(width // 128)], axis=1)
    gain, shift = norms[0:1], norms[2:3]
    c_out.wait()

    @pl.loop(0, blocks)
    def _(r):
        at = rows_at(r)
        oa = v_mix[at, :]
        t = (jnp.dot(oa, whole_rows(b_ab, 3 * cols, 4 * cols), preferred_element_type=F32) * picked(r)).astype(BF)
        v_t[at, 3 * cols:4 * cols] = t
        acc = jnp.dot(oa, whole_rows(b_out, 0, width), preferred_element_type=F32)
        acc = acc + dotf(t, whole_rows(b_ab, 8 * cols, 9 * cols), 1, 1)
        h = x[at, :].astype(F32) + acc
        v_h[at, :] = h
        center = h - jnp.mean(h, axis=1, keepdims=True)
        spread = jnp.mean(center * center, axis=1, keepdims=True)
        y = center * lax.rsqrt(spread + 1e-12) * gain + shift
        v_f[at, :] = y
        yb = y.astype(BF)
        v_yb[at, :] = yb
        v_t[at, 4 * cols:5 * cols] = (jnp.dot(yb, whole_rows(b_ab, 4 * cols, 5 * cols), preferred_element_type=F32) * picked(r)).astype(BF)

    saves2 = [pltpu.make_async_copy(v_h, o_h, osem.at[4]), pltpu.make_async_copy(v_yb, o_yb, osem.at[5])]
    for c in saves2:
        c.start()

    def save_s(j, slot):
        return pltpu.make_async_copy(stage.at[slot], o_sl.at[j], ssem.at[slot])

    save_p(total - 2, 0).wait()
    save_p(total - 1, 1).wait()

    def load_up(j, slot):
        return load(g_up.at[j], b_w.at[slot], 4 + slot)

    for j in range(NCH):
        need("up%d" % j)
        if j == 0:
            load_up(0, 0).start()
            need("ff")
            c_ff = load(g_ff, b_ff, 6)
            c_ff.start()
            c_ff.wait()
        else:
            load_up(j, j % 2).start()
        load_up(j, j % 2).wait()
        if j >= 2:
            save_s(j - 2, j % 2).wait()
        pump(4)

        @pl.loop(0, blocks)
        def _(r, j=j):
            at = rows_at(r)
            u = jnp.dot(v_yb[at, :], whole_rows(b_w.at[j % 2], 0, cw), preferred_element_type=F32)
            wide = flat2(b_ff[:, :, :, cols:2 * cols])[j * cw:(j + 1) * cw]
            u = u + dotf(v_t[at, 4 * cols:5 * cols], wide, 1, 1)
            cdf = 0.5 * (1.0 + lax.erf(u * (0.5 ** 0.5)))
            gb = (u * cdf).astype(BF)
            v_gb[at, j * cw:(j + 1) * cw] = gb
            stage[j % 2, at, :] = (cdf + u * jnp.exp(-0.5 * u * u) * ((0.5 / math.pi) ** 0.5)).astype(BF)

        save_s(j, j % 2).start()
    pump(4)

    @pl.loop(0, blocks)
    def _(r):
        at = rows_at(r)
        acc = jnp.dot(v_gb[at, :], flat2(b_ff[:, :, :, 0:cols]), preferred_element_type=F32)
        v_t[at, 5 * cols:6 * cols] = (acc * picked(r)).astype(BF)

    save_gb = pltpu.make_async_copy(v_gb, o_gb, osem.at[6])
    save_gb.start()
    save_t = pltpu.make_async_copy(v_t, o_t, osem.at[7])
    save_t.start()

    for j in range(NCH):
        need("dn%d" % j)
        slot = j % 2
        view = b_w.at[slot]
        c_dn = load(g_dn.at[j], tacc.at[slot], 7)
        c_dn.start()
        c_dn.wait()
        pump(4)

        @pl.loop(0, blocks)
        def _(r, j=j, slot=slot):
            at = rows_at(r)
            acc = jnp.dot(v_gb[at, :], flat2(tacc[slot]), preferred_element_type=F32)
            wide = whole_rows(b_ab, 9 * cols, 10 * cols)[j * dw:(j + 1) * dw]
            acc = acc + dotf(v_t[at, 5 * cols:6 * cols], wide, 1, 1)
            v_f[at, j * dw:(j + 1) * dw] = v_f[at, j * dw:(j + 1) * dw] + acc

    pump(len(order))
    save_f = pltpu.make_async_copy(v_f, o_f, osem.at[8])
    save_f.start()
    for u in units:
        u.finish()
    save_s(NCH - 2, 0).wait()
    save_s(NCH - 1, 1).wait()
    for c in saves + saves2 + [save_mix, save_gb, save_t, save_f]:
        c.wait()


def forward(grid, x, pick, row, col, shards, lag, cid):
    rows, width = x.shape
    length = col.shape[1]
    seqs = rows // length
    cols = pick.shape[2]
    z, m = grid.n["z"], grid.planes
    s_small, s_ab, s_qkv, s_out, s_up, s_ff, s_dn = shards
    cw, dw = s_up.shape[1] // NCH, s_dn.shape[1] // NCH
    total = Gather.sem_total(grid)
    nu = len(UNITS)
    def g(a, c=None, lead=()):
        return jax.ShapeDtypeStruct(lead + (z, m, a.shape[0], a.shape[1] if c is None else c), BF)
    S = jax.ShapeDtypeStruct
    out_shape = [g(s_small), g(s_ab), g(s_qkv), g(s_out), g(s_up, cw, (NCH,)), g(s_ff), g(s_dn, dw, (NCH,)),
        S(x.shape, BF), S(x.shape, BF), S(x.shape, BF), S((seqs * width // (4 * HD), 2 * length, 2 * length), BF),
        S(x.shape, BF), S(x.shape, F32), S(x.shape, F32), S(x.shape, BF), S((rows, 6 * cols), BF), S((rows, s_up.shape[1]), BF), S((NCH, rows, cw), BF)]
    V = pltpu.VMEM
    scratch = [V((z, m) + s_small.shape, BF), V((z, m) + s_ab.shape, BF), V((z, m) + s_qkv.shape, BF), V((z, m) + s_out.shape, BF), V((z, m) + s_ff.shape, BF),
        V((2, z, m, s_up.shape[0], cw), BF),
        V(x.shape, BF), V(x.shape, BF), V(x.shape, BF), V((2, 2 * length, 2 * length), BF), V((length, length), F32), V(x.shape, BF), V(x.shape, F32), V(x.shape, F32), V(x.shape, BF),
        V((rows, 6 * cols), BF), V((rows, s_up.shape[1]), BF), V((2, z, m, s_dn.shape[0], dw), BF),
        pltpu.SemaphoreType.DMA((nu, total)), pltpu.SemaphoreType.DMA((nu, total)), pltpu.SemaphoreType.DMA((nu,)), pltpu.SemaphoreType.DMA((8,)), pltpu.SemaphoreType.DMA((9,)), pltpu.SemaphoreType.DMA((2,))]
    return pl.pallas_call(
        functools.partial(forward_kernel, grid, lag),
        out_shape=out_shape,
        in_specs=[pl.BlockSpec(memory_space=pltpu.VMEM)] * 11,
        out_specs=[pl.BlockSpec(memory_space=pl.ANY)] * 18,
        scratch_shapes=scratch,
        compiler_params=pltpu.CompilerParams(collective_id=cid, has_side_effects=True, vmem_limit_bytes=67043328),
        name="forward",
    )(x, pick, row, col, *shards)


def tdot(a, b):
    return lax.dot_general(a, b, (((0,), (0,)), ((), ())), preferred_element_type=F32)

def norm_parts(z):
    center = z - jnp.mean(z, axis=1, keepdims=True)
    inv = lax.rsqrt(jnp.mean(center * center, axis=1, keepdims=True) + 1e-12)
    return center * inv, inv

def norm_back(hat, inv, g):
    return inv * (g - jnp.mean(g, axis=1, keepdims=True) - hat * jnp.mean(g * hat, axis=1, keepdims=True))

def middle_kernel(pick, norms, t, ab, f, cot, h, yb, mix, wo, gb, sl, wd, wu, ff,
                  o_res, o_dh, o_do, g_fa, g_fb, g_ao, g_au, g_bo, g_bd,
                  v_f, v_cot, v_res, v_de, v_dy, v_yb, v_mix, v_wo, v_du, tdn, tup, tout, acc, sem, osem):
    j = pl.program_id(0)
    last = pl.num_programs(0) - 1
    rows, width = v_f.shape
    cols = pick.shape[2]
    step = 256
    blocks = rows // step
    length = rows // pick.shape[0]

    def rows_at(r):
        return pl.ds(pl.multiple_of(r * step, step), step)

    def picked(r):
        return pick[(r * step) // length]

    def slot(i):
        return ab[:, i * cols:(i + 1) * cols]

    loads = [pltpu.make_async_copy(f, v_f, sem.at[0]), pltpu.make_async_copy(cot, v_cot, sem.at[1]),
             pltpu.make_async_copy(h, v_f, sem.at[2]), pltpu.make_async_copy(yb, v_yb, sem.at[3]),
             pltpu.make_async_copy(mix, v_mix, sem.at[4]), pltpu.make_async_copy(wo, v_wo, sem.at[5])]
    save_res = pltpu.make_async_copy(v_res, o_res, osem.at[0])
    gain_one, gain_two, shift_two = norms[0:1, :], norms[1:2, :], norms[3:4, :]

    @pl.when(j == 0)
    def _():
        loads[0].start()
        loads[1].start()
        loads[0].wait()
        loads[1].wait()

        @pl.loop(0, blocks)
        def _(r):
            at = rows_at(r)
            hat, inv = norm_parts(v_f[at, :])
            v_res[at, :] = (hat * gain_two + shift_two).astype(BF)
            df = norm_back(hat, inv, v_cot[at, :].astype(F32) * gain_two)
            v_dy[at, :] = df
            de = df.astype(BF)
            v_de[at, :] = de
            tdn[at, :] = (jnp.dot(de, slot(9), preferred_element_type=F32) * picked(r)).astype(BF)

        save_res.start()
        for c in loads[2:]:
            c.start()
        g_bd[...] = tdot(v_de[...], t[:, 5 * cols:6 * cols])
        acc[...] = jnp.zeros_like(acc)

    half = 512

    @pl.loop(0, rows // half)
    def _(r):
        at = pl.ds(pl.multiple_of(r * half, half), half)
        dg = dotf(tdn[at, :], ff[:, 0:cols], 1, 1)
        for c in range(NCH):
            w = wd.shape[2]
            dg = dg + dotf(v_de[at, c * w:(c + 1) * w], wd[c], 1, 1)
        du = (dg * sl[at, :].astype(F32)).astype(BF)
        v_du[at, :] = du
        v_dy[at, :] = v_dy[at, :] + dotf(du, wu[...], 1, 1)
        acc[at, :] = acc[at, :] + jnp.dot(du, ff[:, cols:2 * cols], preferred_element_type=F32)

    g_fa[...] = tdot(gb[...], tdn[...])
    g_fb[...] = tdot(v_du[...], t[:, 4 * cols:5 * cols])

    @pl.when(j == last)
    def _():
        for c in loads[2:]:
            c.wait()
        save_res.wait()

        @pl.loop(0, blocks)
        def _(r):
            at = rows_at(r)
            dtu = (acc[at, :] * picked(r)).astype(BF)
            tup[at, :] = dtu
            dy = v_dy[at, :] + dotf(dtu, slot(4), 1, 1)
            hat, inv = norm_parts(v_f[at, :])
            dh = norm_back(hat, inv, dy * gain_one)
            v_dy[at, :] = dh
            da = dh.astype(BF)
            v_de[at, :] = da
            dto = (jnp.dot(da, slot(8), preferred_element_type=F32) * picked(r)).astype(BF)
            tout[at, :] = dto
            v_res[at, :] = (dotf(da, v_wo[...], 1, 1) + dotf(dto, slot(3), 1, 1)).astype(BF)

        save_dh = pltpu.make_async_copy(v_dy, o_dh, osem.at[1])
        save_do = pltpu.make_async_copy(v_res, o_do, osem.at[2])
        save_dh.start()
        save_do.start()
        g_au[...] = tdot(v_yb[...], tup[...])
        g_bo[...] = tdot(v_de[...], t[:, 3 * cols:4 * cols])
        g_ao[...] = tdot(v_mix[...], tout[...])
        save_dh.wait()
        save_do.wait()


def middle(pick, norms, t, ab, f, cot, h, yb, mix, wo, gb, sl, dn, up, ff):
    rows, width = f.shape
    cols = pick.shape[2]
    total = gb.shape[1]
    blk = 512
    per = sl.shape[2] // blk
    S, V = jax.ShapeDtypeStruct, pltpu.VMEM
    whole = pl.BlockSpec(memory_space=pltpu.VMEM)
    far = pl.BlockSpec(memory_space=pl.ANY)
    wcol = dn.shape[2]
    return pl.pallas_call(
        middle_kernel,
        grid=(total // blk,),
        in_specs=[whole] * 4 + [far] * 6 + [
            pl.BlockSpec((rows, blk), lambda j: (0, j)),
            pl.BlockSpec((None, rows, blk), lambda j: (j // per, 0, j % per)),
            pl.BlockSpec((NCH, blk, wcol), lambda j: (0, j, 0)),
            pl.BlockSpec((None, width, blk), lambda j: (j // per, 0, j % per)),
            pl.BlockSpec((blk, 2 * cols), lambda j: (j, 0)),
        ],
        out_specs=[far] * 3 + [pl.BlockSpec((blk, cols), lambda j: (j, 0))] * 2 + [pl.BlockSpec((width, cols), lambda j: (0, 0))] * 4,
        out_shape=[S(f.shape, BF), S(f.shape, F32), S(f.shape, BF), S((total, cols), F32), S((total, cols), F32)] + [S((width, cols), F32)] * 4,
        scratch_shapes=[V(f.shape, F32), V(f.shape, BF), V(f.shape, BF), V(f.shape, BF), V(f.shape, F32), V(f.shape, BF), V(f.shape, BF), V((width, width), BF),
                        V((rows, blk), BF), V((rows, cols), BF), V((rows, cols), BF), V((rows, cols), BF), V((rows, cols), F32),
                        pltpu.SemaphoreType.DMA((6,)), pltpu.SemaphoreType.DMA((3,))],
        compiler_params=pltpu.CompilerParams(vmem_limit_bytes=60 * 2**20),
        name="middle",
    )(pick, norms, t, ab, f, cot, h, yb, mix, wo, gb, sl, dn, up, ff)


def attend_back_kernel(q_ref, k_ref, v_ref, p_ref, d_ref, dq_ref, dk_ref, dv_ref):
    length, wide = q_ref.shape
    q, k, v, d = q_ref[...], k_ref[...], v_ref[...], d_ref[...]
    scale = jnp.asarray(HD ** -0.5, BF)
    kt, qs = (k * scale).T, q * scale
    lane = lax.broadcasted_iota(jnp.int32, (1, 128), 1) // HD
    dqs, dks, dvs = [], [], []
    for h in range(wide // HD):
        c = (h * HD) // 128 * 128
        vh = jnp.where(lane == (h * HD - c) // HD, v[:, c:c + 128], jnp.zeros((), BF))
        pb = p_ref[(h // 2) * length:(h // 2 + 1) * length, (h % 2) * length:(h % 2 + 1) * length]
        p = pb.astype(F32)
        dp = dotf(vh, d[:, c:c + 128], 1, 1)
        t = p * dp
        ds = (t - p * jnp.sum(t, axis=0, keepdims=True)).astype(BF)
        dqs.append(dotf(kt[h * HD:(h + 1) * HD], ds, 1, 0))
        dks.append(dotf(ds, qs[:, c:c + 128], 1, 0))
        dvs.append(dotf(pb, d[:, c:c + 128], 1, 0))
    dq_ref[...] = jnp.concatenate(dqs, axis=0).T.astype(BF)
    for g in range(wide // 128):
        dk_ref[:, g * 128:(g + 1) * 128] = jnp.where(lane == 0, dks[2 * g], dks[2 * g + 1]).astype(BF)
        dv_ref[:, g * 128:(g + 1) * 128] = jnp.where(lane == 0, dvs[2 * g], dvs[2 * g + 1]).astype(BF)

def attend_back(q, k, v, p, d, seqs):
    rows, width = q.shape
    length = rows // seqs
    wide = 4 * HD
    groups = width // wide
    spec = pl.BlockSpec((length, wide), lambda s, h: (s, h))
    return pl.pallas_call(
        attend_back_kernel, grid=(seqs, groups),
        in_specs=[spec, spec, spec, pl.BlockSpec((None, 2 * length, 2 * length), lambda s, h: (s * groups + h, 0, 0)), spec],
        out_specs=[spec] * 3, out_shape=[jax.ShapeDtypeStruct(q.shape, BF)] * 3,
        compiler_params=pltpu.CompilerParams(vmem_limit_bytes=48 * 2**20), name="attend_back")(q, k, v, p, d)


def local_plain(sizes, tokens, cotangent, adapter_id, global_pos, w_qkv, w_out, w_up, w_down, norm_gain, norm_bias,
          narrow_in, widen_out, ff_narrow, ff_widen):
    grid = Grid(sizes)
    small = jnp.concatenate([norm_gain, norm_bias], axis=1).T
    share = small.shape[1]
    small = jnp.pad(small, ((0, 12), (0, 128 - share)))
    got = all_gather(grid, [w_qkv, narrow_in, widen_out, small, w_out, w_up, w_down, ff_narrow, ff_widen], 0, 2, True)

    def whole(a):
        return a.reshape(-1, a.shape[-1])

    wq_full, a_full, b_full, small_full, wo_full, wu_full, wd_full, ffa_full, ffb_full = [whole(a) for a in got]
    norms = small_full.reshape(grid.devices, 16, 128)[:, :4, :share].transpose(1, 0, 2).reshape(4, grid.devices * share)
    norms = norms.astype(jnp.float32)
    gain_one, gain_two, shift_one, shift_two = norms[0], norms[1], norms[2], norms[3]
    seq_local, length, model_width = tokens.shape
    rows_all = seq_local * length
    set_cols = SETS * R
    chosen = (
        lax.broadcasted_iota(jnp.int32, (seq_local, set_cols), 1) // R == adapter_id[:, None]
    ).astype(jnp.float32)
    chosen = jnp.broadcast_to(chosen[:, None, :], (seq_local, length, set_cols)).reshape(rows_all, set_cols)
    chosen_three = jnp.concatenate([chosen, chosen, chosen], axis=1)
    positions = lax.broadcasted_iota(jnp.int32, (length,), 0)
    is_global = jnp.any(global_pos[:, :, None] == positions[None, None, :], axis=1).astype(jnp.float32)

    def cols_of(slot):
        return slice(slot * set_cols, (slot + 1) * set_cols)

    flat_in = tokens.reshape(rows_all, model_width)
    t_qkv = (product(flat_in, a_full[:, : 3 * set_cols]) * chosen_three).astype(jnp.bfloat16)
    projected = []
    for slot in range(3):
        summed = product(flat_in, wq_full[:, slot * model_width : (slot + 1) * model_width]) + against(
            t_qkv[:, cols_of(slot)], b_full[:, cols_of(slot)]
        )
        projected.append(summed.astype(jnp.bfloat16))
    query_low, key_low, value_low = projected
    mixed_flat, weights_low = attn_fwd(query_low, key_low, value_low, is_global[:, None, :], is_global[:, :, None], seq_local, length, 4)
    t_out = (product(mixed_flat, a_full[:, cols_of(3)]) * chosen).astype(jnp.bfloat16)
    attn_out = product(mixed_flat, wo_full) + against(t_out, b_full[:, cols_of(3)])
    resid = flat_in.astype(jnp.float32) + attn_out
    normed, norm_one_back = jax.vjp(lambda values: normalize(values, gain_one, shift_one), resid)
    normed_low = normed.astype(jnp.bfloat16)
    t_up = (product(normed_low, a_full[:, cols_of(4)]) * chosen).astype(jnp.bfloat16)
    pre_act = product(normed_low, wu_full) + against(t_up, ffb_full)
    cdf = 0.5 * (1.0 + lax.erf(pre_act * (0.5 ** 0.5)))
    act_low = (pre_act * cdf).astype(jnp.bfloat16)
    slope = cdf + pre_act * jnp.exp(-0.5 * pre_act * pre_act) * ((0.5 / math.pi) ** 0.5)
    act_low, slope = lax.optimization_barrier((act_low, slope))
    t_down = (product(act_low, ffa_full) * chosen).astype(jnp.bfloat16)
    down_out = product(act_low, wd_full) + against(t_down, b_full[:, cols_of(4)])
    final = normed + down_out
    result, norm_two_back = jax.vjp(lambda values: normalize(values, gain_two, shift_two), final)
    d_final = norm_two_back(cotangent.reshape(rows_all, model_width).astype(jnp.float32))[0]
    d_down = d_final.astype(jnp.bfloat16)
    dt_down = (product(d_down, b_full[:, cols_of(4)]) * chosen).astype(jnp.bfloat16)
    grad_b_down = over_rows(d_down, t_down)
    grad_ff_narrow = over_rows(act_low, dt_down)
    d_act = against(d_down, wd_full) + against(dt_down, ffa_full)
    d_pre = (d_act * slope).astype(jnp.bfloat16)
    dt_up = (product(d_pre, ffb_full) * chosen).astype(jnp.bfloat16)
    grad_ff_widen = over_rows(d_pre, t_up)
    grad_a_up = over_rows(normed_low, dt_up)
    d_normed = d_final + against(d_pre, wu_full) + against(dt_up, a_full[:, cols_of(4)])
    d_resid = norm_one_back(d_normed)[0]
    d_attn = d_resid.astype(jnp.bfloat16)
    dt_out = (product(d_attn, b_full[:, cols_of(3)]) * chosen).astype(jnp.bfloat16)
    grad_b_out = over_rows(d_attn, t_out)
    grad_a_out = over_rows(mixed_flat, dt_out)
    d_mixed = (against(d_attn, wo_full) + against(dt_out, a_full[:, cols_of(3)])).astype(jnp.bfloat16)
    d_parts = attn_bwd(query_low, key_low, value_low, weights_low, d_mixed, seq_local, length, 4)
    dt_parts = [
        (product(d_parts[slot], b_full[:, cols_of(slot)]) * chosen).astype(jnp.bfloat16) for slot in range(3)
    ]
    dt_qkv = jnp.concatenate(dt_parts, axis=1)
    grad_b_qkv = [over_rows(d_parts[slot], t_qkv[:, cols_of(slot)]) for slot in range(3)]
    grad_a_qkv = over_rows(flat_in, dt_qkv)
    d_input = d_resid + against(dt_qkv, a_full[:, : 3 * set_cols])
    for slot in range(3):
        d_input = d_input + against(d_parts[slot], wq_full[:, slot * model_width : (slot + 1) * model_width])
    rows_own, ff_own = model_width // grid.devices, ff_narrow.shape[0]
    late = reduce_scatter(
        grid, [grad_ff_narrow, grad_ff_widen, grad_a_out, grad_a_up, grad_b_out, grad_b_down],
        [(0, 0), (1, 0), (2, 0), (2, set_cols), (3, 0), (3, set_cols)],
        [(ff_own, set_cols), (ff_own, set_cols), (rows_own, 2 * set_cols), (rows_own, 2 * set_cols)], 1)
    early = reduce_scatter(
        grid, [grad_a_qkv] + grad_b_qkv, [(0, 0), (1, 0), (1, set_cols), (1, 2 * set_cols)],
        [(rows_own, 3 * set_cols), (rows_own, 3 * set_cols)], 2)
    return (
        result.reshape(seq_local, length, model_width).astype(jnp.bfloat16),
        d_input.reshape(seq_local, length, model_width).astype(jnp.bfloat16),
        jnp.concatenate([early[0], late[2]], axis=1),
        jnp.concatenate([early[1], late[3]], axis=1),
        late[0],
        late[1],
    )


LAG = 2


def local(sizes, tokens, cotangent, adapter_id, global_pos, w_qkv, w_out, w_up, w_down, norm_gain, norm_bias,
          narrow_in, widen_out, ff_narrow, ff_widen):
    grid = Grid(sizes)
    seq_local, length, width = tokens.shape
    rows = seq_local * length
    own = w_qkv.shape[0]
    fits = own % 16 == 0 and 128 % own == 0 and rows == 2 * length and w_up.shape[1] == 4 * rows and width == rows
    if not fits:
        return local_plain(sizes, tokens, cotangent, adapter_id, global_pos, w_qkv, w_out, w_up, w_down, norm_gain,
                           norm_bias, narrow_in, widen_out, ff_narrow, ff_widen)
    cols = SETS * R
    flat_in = tokens.reshape(rows, width)
    pick = (lax.broadcasted_iota(jnp.int32, (seq_local, 1, cols), 2) // R == adapter_id[:, None, None]).astype(F32)
    positions = lax.broadcasted_iota(jnp.int32, (length,), 0)
    is_global = jnp.any(global_pos[:, :, None] == positions[None, None, :], axis=1).astype(F32)
    place = (lax.axis_index("dp") * grid.fsdp + lax.axis_index("fsdp")) % (128 // own)
    small = jnp.tile(jnp.concatenate([norm_gain, norm_bias], axis=1).T, (1, 128 // own))
    mine = lax.broadcasted_iota(jnp.int32, (1, 128), 1) // own == place
    small = jnp.pad(jnp.where(mine, small, jnp.zeros((), BF)), ((0, 12), (0, 0)))
    shards = (small, jnp.concatenate([narrow_in, widen_out], axis=1), w_qkv, w_out, w_up,
              jnp.concatenate([ff_narrow, ff_widen], axis=1), w_down)
    (g_small, g_ab, g_qkv, g_out, g_up, g_ff, g_dn, q, k, v, p, mix, h, f, yb, t, gb, sl) = forward(
        grid, flat_in, pick, is_global[:, None, :], is_global[:, :, None], shards, LAG, 0)
    ab, wq, wo, ff = (flat2(a) for a in (g_ab, g_qkv, g_out, g_ff))
    up = g_up.reshape(NCH, width, -1)
    dn = g_dn.reshape(NCH, w_up.shape[1], -1)
    per = 128 // own
    norms = g_small.reshape(width // 128, per, 16, 128).astype(F32).sum(axis=1)[:, :4].transpose(1, 0, 2).reshape(4, width)
    norms = jnp.pad(norms, ((0, 4), (0, 0)))
    res, dh, do, g_fa, g_fb, g_ao, g_au, g_bo, g_bd = middle(
        pick, norms, t, ab, f, cotangent.reshape(rows, width), h, yb, mix, wo, gb, sl, dn, up, ff)
    d_parts = attend_back(q, k, v, p, do, seq_local)
    chosen = jnp.broadcast_to(pick, (seq_local, length, cols)).reshape(rows, cols)

    def cols_of(slot):
        return slice(slot * cols, (slot + 1) * cols)

    dt_parts = [(product(d_parts[s], ab[:, cols_of(5 + s)]) * chosen).astype(BF) for s in range(3)]
    dt_qkv = jnp.concatenate(dt_parts, axis=1)
    grad_b_qkv = [over_rows(d_parts[s], t[:, cols_of(s)]) for s in range(3)]
    grad_a_qkv = over_rows(flat_in, dt_qkv)
    d_input = dh + against(dt_qkv, ab[:, : 3 * cols])
    for s in range(3):
        d_input = d_input + against(d_parts[s], wq[:, s * width:(s + 1) * width])
    ff_own = ff_narrow.shape[0]
    late = reduce_scatter(grid, [g_fa, g_fb, g_ao, g_au, g_bo, g_bd],
                          [(0, 0), (1, 0), (2, 0), (2, cols), (3, 0), (3, cols)],
                          [(ff_own, cols), (ff_own, cols), (own, 2 * cols), (own, 2 * cols)], 1)
    early = reduce_scatter(grid, [grad_a_qkv] + grad_b_qkv, [(0, 0), (1, 0), (1, cols), (1, 2 * cols)],
                           [(own, 3 * cols), (own, 3 * cols)], 2)
    return (
        res.reshape(tokens.shape),
        d_input.reshape(tokens.shape).astype(BF),
        jnp.concatenate([early[0], late[2]], axis=1),
        jnp.concatenate([early[1], late[3]], axis=1),
        late[0],
        late[1],
    )


def solution(mesh):
    rows = P(("dp", "fsdp"), None)
    cube = P(("dp", "fsdp"), None, None)
    in_specs = (cube, cube, P(("dp", "fsdp"))) + (rows,) * 11
    out_specs = (cube, cube) + (rows,) * 4
    return jax.shard_map(functools.partial(local, dict(mesh.shape)), mesh=mesh, in_specs=in_specs, out_specs=out_specs, check_vma=False)
```

```python
import functools, math
import jax
import jax.numpy as jnp
from jax import lax
from jax.experimental import pallas as pl
from jax.experimental.pallas import tpu as pltpu
from jax.sharding import PartitionSpec as P

MESH = pl.DeviceIdType.MESH


class Grid:
    def __init__(self, sizes):
        self.dp, self.fsdp = sizes["dp"], sizes["fsdp"]
        if (self.dp, self.fsdp) == (8, 4):
            self.dims = {"z": ("dp", 2, 4), "y": ("dp", 1, 2), "x": ("fsdp", 2, 2), "c": ("fsdp", 1, 2)}
        elif (self.dp, self.fsdp) == (64, 4):
            self.dims = {"z": ("dp", 8, 8), "y": ("dp", 2, 4), "x": ("fsdp", 1, 4), "c": ("dp", 1, 2)}
        else:
            self.dims = {"z": ("dp", 1, self.dp), "y": ("dp", 1, 1), "x": ("fsdp", self.fsdp, 1), "c": ("fsdp", 1, self.fsdp)}
        self.n = {k: v[2] for k, v in self.dims.items()}
        self.devices = self.dp * self.fsdp
        self.planes = self.devices // self.n["z"]

    def stride(self, k):
        axis, step, _ = self.dims[k]
        return step * (self.fsdp if axis == "dp" else 1)

    def here(self):
        idx = {"dp": lax.axis_index("dp"), "fsdp": lax.axis_index("fsdp")}
        return {k: (idx[axis] // step) % size for k, (axis, step, size) in self.dims.items()}

    def device(self, pos):
        out = {"dp": 0, "fsdp": 0}
        for k, (axis, step, _) in self.dims.items():
            out[axis] = out[axis] + pos[k] * step
        return out["dp"], out["fsdp"]

    def slot(self, y, x, c):
        return y * self.stride("y") + x * self.stride("x") + c * self.stride("c")


def barrier_with(grid, here):
    barrier = pltpu.get_barrier_semaphore()
    count = 0
    for k in ("z", "y", "x", "c"):
        n = grid.n[k]
        for step in range(1, n):
            to = (here[k] + step) % n
            pl.semaphore_signal(barrier, inc=1, device_id=grid.device({**here, k: to}), device_id_type=MESH)
            count += 1
    pl.semaphore_wait(barrier, count)


class Gather:
    @staticmethod
    def parts(grid):
        return grid.n["z"] if grid.n["z"] <= 4 else 1

    @staticmethod
    def sem_total(grid):
        z, a, b, c = (grid.n[k] for k in ("z", "y", "x", "c"))
        k = Gather.parts(grid)
        return z + k * a + k * a * b + a * b

    def __init__(self, grid, here, src, out, send, recv, local):
        self.g, self.here, self.src, self.out = grid, here, src, out
        self.send, self.recv, self.local = send, recv, local
        self.k = Gather.parts(grid)
        self.nz, self.n2, self.n3 = grid.n["z"], grid.n["y"], grid.n["x"]
        self.base2 = self.nz
        self.base3 = self.base2 + self.k * self.n2
        self.base4 = self.base3 + self.k * self.n2 * self.n3
        self.sends = []
        self.first = here["c"] == 0
        self.p2 = jnp.where(self.first, here["y"], here["x"])
        self.p3 = jnp.where(self.first, here["x"], here["y"])

    def dev(self, z=None, p2=None, p3=None, c=None):
        h = self.here
        p2 = self.p2 if p2 is None else p2
        p3 = self.p3 if p3 is None else p3
        return self.g.device({
            "z": h["z"] if z is None else z,
            "y": jnp.where(self.first, p2, p3),
            "x": jnp.where(self.first, p3, p2),
            "c": h["c"] if c is None else c,
        })

    def m(self, p2, p3):
        return self.g.slot(jnp.where(self.first, p2, p3), jnp.where(self.first, p3, p2), self.here["c"])

    def part(self, i):
        return (self.here["z"] ^ i) if self.k == self.nz and self.nz & (self.nz - 1) == 0 else None

    def block(self, z, p2, p3):
        return self.out.at[:, self.m(p2, p3)] if z is None else self.out.at[z, self.m(p2, p3)]

    def copy(self, src, dst, sem, dev):
        return pltpu.make_async_remote_copy(src_ref=src, dst_ref=dst, send_sem=self.send.at[sem], recv_sem=self.recv.at[sem], device_id=dev, device_id_type=MESH)

    def pull(self, dst, sem):
        self.copy(dst, dst, sem, self.dev()).wait_recv()

    def sem2(self, z, p2):
        return self.base2 + (0 if z is None else z * self.n2) + p2

    def sem3(self, z, p2, p3):
        return self.base3 + ((0 if z is None else z * self.n2) + p2) * self.n3 + p3

    def to2(self, z, src=None):
        ref = self.block(z, self.p2, self.p3)
        return [self.copy(ref if src is None else src, ref, self.sem2(z, self.p2), self.dev(p2=(self.p2 + d) % self.n2)) for d in range(1, self.n2)]

    def to3(self, z, p2, src=None):
        ref = self.block(z, p2, self.p3)
        return [self.copy(ref if src is None else src, ref, self.sem3(z, p2, self.p3), self.dev(p3=(self.p3 + d) % self.n3)) for d in range(1, self.n3)]

    def to_core(self, p2, p3):
        if self.g.n["c"] == 1:
            return []
        ref = self.block(None, p2, p3)
        y, x = jnp.where(self.first, p2, p3), jnp.where(self.first, p3, p2)
        return [self.copy(ref, ref, self.base4 + y * self.n3 + x, self.dev(c=1 - self.here["c"]))]

    def line(self, i):
        z = self.here["z"]
        return z ^ i if self.nz & (self.nz - 1) == 0 else (z + i) % self.nz

    def own(self):
        return pltpu.make_async_copy(self.src, self.out.at[self.here["z"], self.m(self.p2, self.p3)], self.local)

    def begin(self):
        z = self.here["z"]
        m0 = self.m(self.p2, self.p3)
        out = [self.copy(self.src, self.out.at[z, m0], z, self.dev(z=self.line(i))) for i in range(1, self.nz)]
        if self.part(0) is not None:
            out += self.to3(z, self.p2, self.src) + self.to2(z, self.src)
        return out

    def wait_z(self, i):
        z = self.line(i)
        self.pull(self.out.at[z, self.m(self.p2, self.p3)], z)

    def after_z(self, i):
        return self.to2(self.part(i)) + self.to3(self.part(i), self.p2) if self.part(i) is not None else []

    def after_line(self):
        out = [] if self.part(0) is not None else self.to2(None) + self.to3(None, self.p2)
        return out + self.to_core(self.p2, self.p3)

    def wait2(self, i):
        z = self.part(i)
        for d in range(1, self.n2):
            q = (self.p2 + d) % self.n2
            self.pull(self.block(z, q, self.p3), self.sem2(z, q))

    def after2(self, i):
        return [c for d in range(1, self.n2) for c in self.to3(self.part(i), (self.p2 + d) % self.n2)]

    def after_all2(self):
        return [c for d in range(1, self.n2) for c in self.to_core((self.p2 + d) % self.n2, self.p3)]

    def wait3(self, j):
        p2 = (self.p2 + j) % self.n2
        for d in range(1, self.n3):
            q = (self.p3 + d) % self.n3
            for i in range(self.k):
                z = self.part(i)
                self.pull(self.block(z, p2, q), self.sem3(z, p2, q))

    def after3(self, j):
        p2 = (self.p2 + j) % self.n2
        return [c for d in range(1, self.n3) for c in self.to_core(p2, (self.p3 + d) % self.n3)]

    def pairs(self):
        part = functools.partial
        out = [(lambda: self.own().start(), self.begin)]
        out += [(part(self.wait_z, i), part(self.after_z, i)) for i in range(1, self.nz)]
        out += [(lambda: self.own().wait(), self.after_line)]
        out += [(part(self.wait2, i), part(self.after2, i)) for i in range(self.k)]
        out += [(lambda: None, self.after_all2)]
        out += [(part(self.wait3, j), part(self.after3, j)) for j in range(self.n2)]
        return out

    def steps(self):
        def act(wait, copies):
            wait()
            for c in copies():
                c.start()
        return [functools.partial(act, *p) for p in self.pairs()] + [self.arrived]

    def arrived(self):
        if self.g.n["c"] > 1:
            for y in range(self.n2):
                for x in range(self.n3):
                    self.pull(self.out.at[:, self.g.slot(y, x, 1 - self.here["c"])], self.base4 + y * self.n3 + x)

    def finish(self):
        for _, copies in self.pairs():
            for c in copies():
                c.wait_send()


def skewed(all_steps, lag):
    count = max(len(s) for s in all_steps)
    out = []
    for slot in range(count + lag * (len(all_steps) - 1)):
        for i, steps in enumerate(all_steps):
            k = slot - lag * i
            if 0 <= k < len(steps):
                out.append((i, steps[k]))
    return out


def run_skewed(all_steps, lag):
    for _, step in skewed(all_steps, lag):
        step()

SETS = 8
R = 16


def normalize(values, gain, shift):
    center = values - jnp.mean(values, axis=-1, keepdims=True)
    spread = jnp.mean(center * center, axis=-1, keepdims=True)
    return center * lax.rsqrt(spread + 1e-12) * gain + shift


def against(left, right):
    return lax.dot_general(
        left, right, (((1,), (1,)), ((), ())), preferred_element_type=jnp.float32
    )


def over_rows(left, right):
    return lax.dot_general(
        left, right, (((0,), (0,)), ((), ())), preferred_element_type=jnp.float32
    )


def product(left, right):
    return jnp.dot(left, right, preferred_element_type=jnp.float32)


def gelu_exact(values):
    return jax.nn.gelu(values, approximate=False)


def gather_kernel(grid, count, lag, first, *refs):
    srcs, outs = refs[:count], refs[count:2*count]
    send, recv, local = refs[2*count:]
    here = grid.here()
    barrier_with(grid, here)
    gs = [Gather(grid, here, srcs[i], outs[i], send.at[i], recv.at[i], local.at[i]) for i in range(count)]
    steps = [g.steps() for g in gs]
    if first:
        for s in steps:
            s.pop(0)()
    run_skewed(steps, lag)
    for g in gs:
        g.finish()

def all_gather(grid, arrays, cid=0, lag=1, first=True):
    count = len(arrays)
    total = Gather.sem_total(grid)
    out_shape = [jax.ShapeDtypeStruct((grid.n["z"], grid.planes) + a.shape, a.dtype) for a in arrays]
    return pl.pallas_call(
        functools.partial(gather_kernel, grid, count, lag, first),
        out_shape=out_shape,
        in_specs=[pl.BlockSpec(memory_space=pltpu.VMEM)] * count,
        out_specs=[pl.BlockSpec(memory_space=pl.ANY)] * count,
        scratch_shapes=[pltpu.SemaphoreType.DMA((count, total)), pltpu.SemaphoreType.DMA((count, total)), pltpu.SemaphoreType.DMA((count,))],
        compiler_params=pltpu.CompilerParams(collective_id=cid, has_side_effects=True, vmem_limit_bytes=8*2**20),
        name="gather",
    )(*arrays)


class Scatter:
    @staticmethod
    def sem_total(grid):
        return 1 + grid.n["x"] + grid.n["y"] + grid.n["z"]

    @staticmethod
    def scratch(grid, shape, dtype=jnp.bfloat16):
        rows, cols = shape
        z, y, x = grid.n["z"], grid.n["y"], grid.n["x"]
        out = []
        if grid.n["c"] > 1:
            out += [pltpu.VMEM((y * x, z, rows, cols), dtype)] * 2
        out += [pltpu.VMEM((max(x - 1, 1), y, z, rows, cols), dtype)] * 2
        out += [pltpu.VMEM((max(y - 1, 1), z, rows, cols), dtype)] * 2
        out += [pltpu.VMEM((z, rows, cols), dtype), pltpu.VMEM((max(z - 1, 1), rows, cols), dtype)]
        out += [pltpu.VMEM((y * x, z, rows, cols), jnp.float32)]
        return out

    def __init__(self, grid, here, src, put, bufs, send, recv):
        self.g, self.here, self.src, self.put, self.send, self.recv = grid, here, src, put, send, recv
        bufs = list(bufs)
        self.two = grid.n["c"] > 1
        self.s1, self.r1 = (bufs.pop(0), bufs.pop(0)) if self.two else (None, None)
        self.s2, self.r2, self.s3, self.r3, self.s4, self.r4, self.acc = bufs
        self.nz, self.n2, self.n3 = grid.n["z"], grid.n["y"], grid.n["x"]
        self.first = here["c"] == 0
        self.p2 = jnp.where(self.first, here["y"], here["x"])
        self.p3 = jnp.where(self.first, here["x"], here["y"])
        self.sends, self.pulls = [], []

    def dev(self, z=None, p2=None, p3=None, c=None):
        h = self.here
        p2 = self.p2 if p2 is None else p2
        p3 = self.p3 if p3 is None else p3
        return self.g.device({
            "z": h["z"] if z is None else z,
            "y": jnp.where(self.first, p2, p3),
            "x": jnp.where(self.first, p3, p2),
            "c": h["c"] if c is None else c,
        })

    def flat(self, p2, p3):
        return jnp.where(self.first, p2 * self.n3 + p3, p3 * self.n3 + p2)

    def push(self, make):
        make().start()
        self.sends.append(make)

    def copy(self, src, dst, sem, dev):
        return pltpu.make_async_remote_copy(src_ref=src, dst_ref=dst, send_sem=self.send.at[sem], recv_sem=self.recv.at[sem], device_id=dev, device_id_type=MESH)

    def far(self, p, d, n):
        return (p + d) % n

    def pull(self, dst, sem):
        pltpu.make_async_remote_copy(src_ref=dst, dst_ref=dst, send_sem=self.send.at[sem], recv_sem=self.recv.at[sem], device_id=self.dev(), device_id_type=MESH).wait_recv()

    def begin(self):
        c = self.here["c"]
        for y in range(self.n2):
            for x in range(self.n3):
                i = y * self.n3 + x
                if self.two:
                    self.s1[i] = self.src[:, self.g.slot(y, x, 1 - c)].astype(self.s1.dtype)
        if self.two:
            self.push(lambda: self.copy(self.s1, self.r1, 0, self.dev(c=1 - self.here["c"])))

    def step1(self):
        c = self.here["c"]
        if self.two:
            self.pull(self.r1, 0)
        for y in range(self.n2):
            for x in range(self.n3):
                i = y * self.n3 + x
                part = self.src[:, self.g.slot(y, x, c)]
                self.acc[i] = part + self.r1[i].astype(jnp.float32) if self.two else part
        for d in range(1, self.n3):
            q = (self.p3 + d) % self.n3
            for j in range(self.n2):
                self.s2[d - 1, j] = self.acc[self.flat(j, q)].astype(self.s2.dtype)
            self.push(lambda d=d: self.copy(self.s2.at[d - 1], self.r2.at[d - 1], 1 + d, self.dev(p3=self.far(self.p3, d, self.n3))))

    def step2(self):
        for d in range(1, self.n3):
            self.pull(self.r2.at[d - 1], 1 + d)
        for j in range(self.n2):
            i = self.flat(j, self.p3)
            total = self.acc[i]
            for d in range(1, self.n3):
                total = total + self.r2[d - 1, j].astype(jnp.float32)
            self.acc[i] = total
        base = 1 + self.n3
        for d in range(1, self.n2):
            q = (self.p2 + d) % self.n2
            self.s3[d - 1] = self.acc[self.flat(q, self.p3)].astype(self.s3.dtype)
            self.push(lambda d=d: self.copy(self.s3.at[d - 1], self.r3.at[d - 1], base + d, self.dev(p2=self.far(self.p2, d, self.n2))))

    def step3(self):
        base = 1 + self.n3
        i = self.flat(self.p2, self.p3)
        total = self.acc[i]
        for d in range(1, self.n2):
            self.pull(self.r3.at[d - 1], base + d)
            total = total + self.r3[d - 1].astype(jnp.float32)
        self.acc[i] = total
        base = base + self.n2
        self.s4[...] = total.astype(self.s4.dtype)
        for d in range(1, self.nz):
            self.push(lambda d=d: self.copy(self.s4.at[self.far(self.here["z"], d, self.nz)], self.r4.at[d - 1], base + d, self.dev(z=self.far(self.here["z"], d, self.nz))))

    def step4(self):
        base = 1 + self.n3 + self.n2
        total = self.acc[self.flat(self.p2, self.p3), self.here["z"]]
        for d in range(1, self.nz):
            self.pull(self.r4.at[d - 1], base + d)
            total = total + self.r4[d - 1].astype(jnp.float32)
        self.put(total)

    def steps(self):
        return [self.begin, self.step1, self.step2, self.step3, self.step4]

    def finish(self):
        for make in self.sends:
            make().wait_send()


def scatter_kernel(grid, places, nout, *refs):
    count = len(places)
    srcs, outs = refs[:count], refs[count:count + nout]
    rest = refs[count + nout:]
    send, recv = rest[:2]
    rest = rest[2:]
    per = len(rest) // count
    here = grid.here()
    barrier_with(grid, here)
    units = []
    for i, (o, col) in enumerate(places):
        def put(total, o=o, col=col):
            outs[o][:, col:col + total.shape[1]] = total
        units.append(Scatter(grid, here, srcs[i], put, rest[i * per:(i + 1) * per], send.at[i], recv.at[i]))
    run_skewed([u.steps() for u in units], 1)
    for u in units:
        u.finish()


def reduce_scatter(grid, arrays, places, outs, cid):
    count = len(arrays)
    views = [a.reshape(grid.n["z"], grid.planes, a.shape[0] // grid.devices, a.shape[1]) for a in arrays]
    total = Scatter.sem_total(grid)
    scratch = [pltpu.SemaphoreType.DMA((count, total)), pltpu.SemaphoreType.DMA((count, total))]
    for v in views:
        scratch += Scatter.scratch(grid, v.shape[2:])
    return pl.pallas_call(
        functools.partial(scatter_kernel, grid, places, len(outs)),
        out_shape=[jax.ShapeDtypeStruct(o, jnp.float32) for o in outs],
        in_specs=[pl.BlockSpec(memory_space=pltpu.VMEM)] * count,
        out_specs=[pl.BlockSpec(memory_space=pltpu.VMEM)] * len(outs),
        scratch_shapes=scratch,
        compiler_params=pltpu.CompilerParams(collective_id=cid, has_side_effects=True, vmem_limit_bytes=60 * 2**20),
        name="scatter",
    )(*views)


HD=64
def dotf(a,b,ca,cb):
    return lax.dot_general(a,b,(((ca,),(cb,)),((),())),preferred_element_type=jnp.float32)

def set_bias(bias, row, col, half):
    n=bias.shape[0]
    i=lax.broadcasted_iota(jnp.int32,(n,n),0); j=lax.broadcasted_iota(jnp.int32,(n,n),1)
    near=jnp.abs(i-j)<=half
    ok=near|(jnp.broadcast_to(row,(n,n))>0)|(jnp.broadcast_to(col,(n,n))>0)
    bias[...]=jnp.where(ok,0.0,-1e30)

def fwd_kernel(half,row_ref,col_ref,q_ref,k_ref,v_ref,o_ref,p_ref,bias):
    @pl.when(pl.program_id(1)==0)
    def _(): set_bias(bias,row_ref[0],col_ref[0],half)
    width=q_ref.shape[1]
    q=q_ref[...]; k=k_ref[...]
    vt=v_ref[...].T
    outs=[]
    for h in range(width//HD):
        c=(h*HD)//128*128
        lane=lax.broadcasted_iota(jnp.int32,(1,128),1)//HD
        keep=(lane==(h*HD-c)//HD)
        kh=jnp.where(keep,k[:,c:c+128],jnp.zeros((),k.dtype))*jnp.asarray(HD**-0.5,k.dtype)
        s=dotf(kh,q[:,c:c+128],1,1)+bias[...]
        top=jnp.max(s,axis=0,keepdims=True)
        e=jnp.exp(s-top)
        tot=jnp.sum(e,axis=0,keepdims=True)
        p=(e*(1.0/tot)).astype(jnp.bfloat16)
        p_ref[h]=p
        outs.append(dotf(vt[h*HD:(h+1)*HD],p,1,0))
    o_ref[...]=jnp.concatenate(outs,axis=0).T.astype(o_ref.dtype)

def attn_fwd(q,k,v,row,col,seqs,length,per=2):
    rows,width=q.shape; heads=width//HD
    w=per*HD
    spec=pl.BlockSpec((length,w),lambda s,h:(s,h))
    return pl.pallas_call(functools.partial(fwd_kernel,256),grid=(seqs,heads//per),
      in_specs=[pl.BlockSpec((1,1,length),lambda s,h:(s,0,0)),pl.BlockSpec((1,length,1),lambda s,h:(s,0,0)),spec,spec,spec],
      out_specs=[spec,pl.BlockSpec((None,per,length,length),lambda s,h:(s,h,0,0))],
      out_shape=[jax.ShapeDtypeStruct(q.shape,q.dtype),jax.ShapeDtypeStruct((seqs,heads,length,length),q.dtype)],
      scratch_shapes=[pltpu.VMEM((length,length),jnp.float32)],
      compiler_params=pltpu.CompilerParams(vmem_limit_bytes=48*2**20),name="attend")(row,col,q,k,v)

def bwd_kernel(q_ref,k_ref,v_ref,p_ref,d_ref,dq_ref,dk_ref,dv_ref):
    width=q_ref.shape[1]
    q=q_ref[...]; k=k_ref[...]; v=v_ref[...]; d=d_ref[...]
    scale=jnp.asarray(HD**-0.5,q.dtype)
    kt=(k*scale).T
    qs=q*scale
    dqs=[]; dks=[]; dvs=[]
    lane=lax.broadcasted_iota(jnp.int32,(1,128),1)//HD
    for h in range(width//HD):
        c=(h*HD)//128*128
        keep=(lane==(h*HD-c)//HD)
        vh=jnp.where(keep,v[:,c:c+128],jnp.zeros((),v.dtype))
        pb=p_ref[h]
        p=pb.astype(jnp.float32)
        dp=dotf(vh,d[:,c:c+128],1,1)
        t=p*dp
        inner=jnp.sum(t,axis=0,keepdims=True)
        ds=(t-p*inner).astype(jnp.bfloat16)
        dqs.append(dotf(kt[h*HD:(h+1)*HD],ds,1,0))
        dks.append(dotf(ds,qs[:,c:c+128],1,0))
        dvs.append(dotf(pb,d[:,c:c+128],1,0))
    dq_ref[...]=jnp.concatenate(dqs,axis=0).T.astype(dq_ref.dtype)
    for g in range(width//128):
        keep=lane==0
        dk_ref[:,g*128:(g+1)*128]=jnp.where(keep,dks[2*g],dks[2*g+1]).astype(dk_ref.dtype)
        dv_ref[:,g*128:(g+1)*128]=jnp.where(keep,dvs[2*g],dvs[2*g+1]).astype(dv_ref.dtype)

def attn_bwd(q,k,v,p,d,seqs,length,per=2):
    rows,width=q.shape; heads=width//HD; w=per*HD
    spec=pl.BlockSpec((length,w),lambda s,h:(s,h))
    return pl.pallas_call(bwd_kernel,grid=(seqs,heads//per),
      in_specs=[spec,spec,spec,pl.BlockSpec((None,per,length,length),lambda s,h:(s,h,0,0)),spec],
      out_specs=[spec]*3,out_shape=[jax.ShapeDtypeStruct(q.shape,q.dtype)]*3,
      compiler_params=pltpu.CompilerParams(vmem_limit_bytes=48*2**20),name="attend_back")(q,k,v,p,d)


BF = jnp.bfloat16
F32 = jnp.float32

def flat2(v):
    return v.reshape(v.shape[0] * v.shape[1] * v.shape[2], v.shape[3])

def whole_rows(ref, c0, c1):
    return flat2(ref[:, :, :, c0:c1])

UNITS = ("small", "ab", "qkv", "out", "up0", "ff", "up1", "up2", "up3", "dn0", "dn1", "dn2", "dn3")
NCH = 4

def forward_kernel(grid, lag, *refs):
    n_in = 4 + 7
    (x, pick, row, col, s_small, s_ab, s_qkv, s_out, s_up, s_ff, s_dn) = refs[:n_in]
    outs = refs[n_in:n_in + 18]
    (g_small, g_ab, g_qkv, g_out, g_up, g_ff, g_dn, o_q, o_k, o_v, o_p, o_mix, o_h, o_f, o_yb, o_t, o_gb, o_sl) = outs
    (b_small, b_ab, b_qkv, b_out, b_ff, b_w, v_q, v_k, v_v, stage, bias, v_mix, v_h, v_f, v_yb, v_t, v_gb, tacc,
     send, recv, local, lsem, osem, ssem) = refs[n_in + 18:]
    rows, width = x.shape
    length = bias.shape[0]
    seqs = rows // length
    cols = pick.shape[2]
    here = grid.here()
    barrier_with(grid, here)
    spots = {"small": (s_small, g_small), "ab": (s_ab, g_ab), "qkv": (s_qkv, g_qkv), "out": (s_out, g_out), "ff": (s_ff, g_ff)}
    cw, dw = s_up.shape[1] // NCH, s_dn.shape[1] // NCH
    for j in range(NCH):
        spots["up%d" % j] = (s_up.at[:, j * cw:(j + 1) * cw], g_up.at[j])
        spots["dn%d" % j] = (s_dn.at[:, j * dw:(j + 1) * dw], g_dn.at[j])
    units = [Gather(grid, here, *spots[n], send.at[i], recv.at[i], local.at[i]) for i, n in enumerate(UNITS)]
    order = skewed([u.steps() for u in units], lag)
    state = {"at": 0}
    last = {i: max(k for k, (j, _) in enumerate(order) if j == i) for i in range(len(units))}

    def pump(count):
        end = min(state["at"] + count, len(order))
        for k in range(state["at"], end):
            order[k][1]()
        state["at"] = end

    def need(name):
        pump(max(0, last[UNITS.index(name)] + 1 - state["at"]))

    def load(src, dst, k):
        return pltpu.make_async_copy(src, dst, lsem.at[k])

    need("ab")
    c_small, c_ab = load(g_small, b_small, 0), load(g_ab, b_ab, 1)
    c_small.start()
    c_ab.start()
    need("qkv")
    c_qkv = load(g_qkv, b_qkv, 2)
    c_qkv.start()
    c_small.wait()
    c_ab.wait()
    c_qkv.wait()

    step = 256
    blocks = rows // step

    def rows_at(r):
        return pl.ds(pl.multiple_of(r * step, step), step)

    def picked(r):
        return pick[(r * step) // length]

    for slot, dst in enumerate((v_q, v_k, v_v)):
        @pl.loop(0, blocks)
        def _(r, slot=slot, dst=dst):
            at = rows_at(r)
            xa = x[at, :]
            t = (jnp.dot(xa, whole_rows(b_ab, slot * cols, (slot + 1) * cols), preferred_element_type=F32) * picked(r)).astype(BF)
            v_t[at, slot * cols:(slot + 1) * cols] = t
            acc = jnp.dot(xa, whole_rows(b_qkv, slot * width, (slot + 1) * width), preferred_element_type=F32)
            acc = acc + dotf(t, whole_rows(b_ab, (5 + slot) * cols, (6 + slot) * cols), 1, 1)
            dst[at, :] = acc.astype(BF)
        pump(3)
    saves = [pltpu.make_async_copy(v_q, o_q, osem.at[0]), pltpu.make_async_copy(v_k, o_k, osem.at[1]), pltpu.make_async_copy(v_v, o_v, osem.at[2])]
    for c in saves:
        c.start()

    per = 4
    groups = width // (per * HD)
    total = seqs * groups
    chunks = []
    left = last[UNITS.index("up2")] - state["at"]
    base = state["at"]
    share = max(1, left // total)

    def save_p(i, slot):
        return pltpu.make_async_copy(stage.at[slot], o_p.at[i], ssem.at[slot])

    def attend(i, carry):
        seq, hp = i // groups, i % groups
        @pl.when(hp == 0)
        def _():
            set_bias(bias, row[seq], col[seq], length // 2)
        slot = i % 2
        @pl.when(i >= 2)
        def _():
            save_p(i - 2, slot).wait()
        at = pl.ds(pl.multiple_of(seq * length, length), length)
        q = v_q[at, pl.ds(pl.multiple_of(hp * per * HD, per * HD), per * HD)]
        k = v_k[at, pl.ds(pl.multiple_of(hp * per * HD, per * HD), per * HD)]
        vt = v_v[at, pl.ds(pl.multiple_of(hp * per * HD, per * HD), per * HD)].T
        got = []
        lane = lax.broadcasted_iota(jnp.int32, (1, 128), 1) // HD
        for h in range(per):
            c = (h * HD) // 128 * 128
            kh = jnp.where(lane == (h * HD - c) // HD, k[:, c:c + 128], jnp.zeros((), BF)) * jnp.asarray(HD ** -0.5, BF)
            s = dotf(kh, q[:, c:c + 128], 1, 1) + bias[...]
            e = jnp.exp(s - jnp.max(s, axis=0, keepdims=True))
            p = (e * (1.0 / jnp.sum(e, axis=0, keepdims=True))).astype(BF)
            stage[slot, (h // 2) * length:(h // 2 + 1) * length, (h % 2) * length:(h % 2 + 1) * length] = p
            got.append(dotf(vt[h * HD:(h + 1) * HD], p, 1, 0))
        v_mix[at, pl.ds(pl.multiple_of(hp * per * HD, per * HD), per * HD)] = jnp.concatenate(got, axis=0).T.astype(BF)
        save_p(i, slot).start()
        for n in range(total):
            lo, hi = base + n * share, base + (n + 1) * share
            @pl.when(i == n)
            def _():
                for k2 in range(lo, hi):
                    order[k2][1]()
        return carry

    lax.fori_loop(0, total, attend, 0)
    state["at"] = base + share * total
    save_mix = pltpu.make_async_copy(v_mix, o_mix, osem.at[3])
    save_mix.start()

    need("out")
    c_out = load(g_out, b_out, 3)
    c_out.start()
    per_group = grid.devices // (width // 128)
    small = b_small[...].reshape(width // 128, per_group, 16, 128).astype(F32).sum(axis=1)
    norms = jnp.concatenate([small[g] for g in range(width // 128)], axis=1)
    gain, shift = norms[0:1], norms[2:3]
    c_out.wait()

    @pl.loop(0, blocks)
    def _(r):
        at = rows_at(r)
        oa = v_mix[at, :]
        t = (jnp.dot(oa, whole_rows(b_ab, 3 * cols, 4 * cols), preferred_element_type=F32) * picked(r)).astype(BF)
        v_t[at, 3 * cols:4 * cols] = t
        acc = jnp.dot(oa, whole_rows(b_out, 0, width), preferred_element_type=F32)
        acc = acc + dotf(t, whole_rows(b_ab, 8 * cols, 9 * cols), 1, 1)
        h = x[at, :].astype(F32) + acc
        v_h[at, :] = h
        center = h - jnp.mean(h, axis=1, keepdims=True)
        spread = jnp.mean(center * center, axis=1, keepdims=True)
        y = center * lax.rsqrt(spread + 1e-12) * gain + shift
        v_f[at, :] = y
        yb = y.astype(BF)
        v_yb[at, :] = yb
        v_t[at, 4 * cols:5 * cols] = (jnp.dot(yb, whole_rows(b_ab, 4 * cols, 5 * cols), preferred_element_type=F32) * picked(r)).astype(BF)

    saves2 = [pltpu.make_async_copy(v_h, o_h, osem.at[4]), pltpu.make_async_copy(v_yb, o_yb, osem.at[5])]
    for c in saves2:
        c.start()

    def save_s(j, slot):
        return pltpu.make_async_copy(stage.at[slot], o_sl.at[j], ssem.at[slot])

    save_p(total - 2, 0).wait()
    save_p(total - 1, 1).wait()

    def load_up(j, slot):
        return load(g_up.at[j], b_w.at[slot], 4 + slot)

    for j in range(NCH):
        need("up%d" % j)
        if j == 0:
            load_up(0, 0).start()
            need("ff")
            c_ff = load(g_ff, b_ff, 6)
            c_ff.start()
            c_ff.wait()
        else:
            load_up(j, j % 2).start()
        load_up(j, j % 2).wait()
        if j >= 2:
            save_s(j - 2, j % 2).wait()
        pump(4)

        @pl.loop(0, blocks)
        def _(r, j=j):
            at = rows_at(r)
            u = jnp.dot(v_yb[at, :], whole_rows(b_w.at[j % 2], 0, cw), preferred_element_type=F32)
            wide = flat2(b_ff[:, :, :, cols:2 * cols])[j * cw:(j + 1) * cw]
            u = u + dotf(v_t[at, 4 * cols:5 * cols], wide, 1, 1)
            cdf = 0.5 * (1.0 + lax.erf(u * (0.5 ** 0.5)))
            gb = (u * cdf).astype(BF)
            v_gb[at, j * cw:(j + 1) * cw] = gb
            stage[j % 2, at, :] = (cdf + u * jnp.exp(-0.5 * u * u) * ((0.5 / math.pi) ** 0.5)).astype(BF)

        save_s(j, j % 2).start()
    pump(4)

    @pl.loop(0, blocks)
    def _(r):
        at = rows_at(r)
        acc = jnp.dot(v_gb[at, :], flat2(b_ff[:, :, :, 0:cols]), preferred_element_type=F32)
        v_t[at, 5 * cols:6 * cols] = (acc * picked(r)).astype(BF)

    save_gb = pltpu.make_async_copy(v_gb, o_gb, osem.at[6])
    save_gb.start()
    save_t = pltpu.make_async_copy(v_t, o_t, osem.at[7])
    save_t.start()

    for j in range(NCH):
        need("dn%d" % j)
        slot = j % 2
        view = b_w.at[slot]
        c_dn = load(g_dn.at[j], tacc.at[slot], 7)
        c_dn.start()
        c_dn.wait()
        pump(4)

        @pl.loop(0, blocks)
        def _(r, j=j, slot=slot):
            at = rows_at(r)
            acc = jnp.dot(v_gb[at, :], flat2(tacc[slot]), preferred_element_type=F32)
            wide = whole_rows(b_ab, 9 * cols, 10 * cols)[j * dw:(j + 1) * dw]
            acc = acc + dotf(v_t[at, 5 * cols:6 * cols], wide, 1, 1)
            v_f[at, j * dw:(j + 1) * dw] = v_f[at, j * dw:(j + 1) * dw] + acc

    pump(len(order))
    save_f = pltpu.make_async_copy(v_f, o_f, osem.at[8])
    save_f.start()
    for u in units:
        u.finish()
    save_s(NCH - 2, 0).wait()
    save_s(NCH - 1, 1).wait()
    for c in saves + saves2 + [save_mix, save_gb, save_t, save_f]:
        c.wait()


def forward(grid, x, pick, row, col, shards, lag, cid):
    rows, width = x.shape
    length = col.shape[1]
    seqs = rows // length
    cols = pick.shape[2]
    z, m = grid.n["z"], grid.planes
    s_small, s_ab, s_qkv, s_out, s_up, s_ff, s_dn = shards
    cw, dw = s_up.shape[1] // NCH, s_dn.shape[1] // NCH
    total = Gather.sem_total(grid)
    nu = len(UNITS)
    def g(a, c=None, lead=()):
        return jax.ShapeDtypeStruct(lead + (z, m, a.shape[0], a.shape[1] if c is None else c), BF)
    S = jax.ShapeDtypeStruct
    out_shape = [g(s_small), g(s_ab), g(s_qkv), g(s_out), g(s_up, cw, (NCH,)), g(s_ff), g(s_dn, dw, (NCH,)),
        S(x.shape, BF), S(x.shape, BF), S(x.shape, BF), S((seqs * width // (4 * HD), 2 * length, 2 * length), BF),
        S(x.shape, BF), S(x.shape, F32), S(x.shape, F32), S(x.shape, BF), S((rows, 6 * cols), BF), S((rows, s_up.shape[1]), BF), S((NCH, rows, cw), BF)]
    V = pltpu.VMEM
    scratch = [V((z, m) + s_small.shape, BF), V((z, m) + s_ab.shape, BF), V((z, m) + s_qkv.shape, BF), V((z, m) + s_out.shape, BF), V((z, m) + s_ff.shape, BF),
        V((2, z, m, s_up.shape[0], cw), BF),
        V(x.shape, BF), V(x.shape, BF), V(x.shape, BF), V((2, 2 * length, 2 * length), BF), V((length, length), F32), V(x.shape, BF), V(x.shape, F32), V(x.shape, F32), V(x.shape, BF),
        V((rows, 6 * cols), BF), V((rows, s_up.shape[1]), BF), V((2, z, m, s_dn.shape[0], dw), BF),
        pltpu.SemaphoreType.DMA((nu, total)), pltpu.SemaphoreType.DMA((nu, total)), pltpu.SemaphoreType.DMA((nu,)), pltpu.SemaphoreType.DMA((8,)), pltpu.SemaphoreType.DMA((9,)), pltpu.SemaphoreType.DMA((2,))]
    return pl.pallas_call(
        functools.partial(forward_kernel, grid, lag),
        out_shape=out_shape,
        in_specs=[pl.BlockSpec(memory_space=pltpu.VMEM)] * 11,
        out_specs=[pl.BlockSpec(memory_space=pl.ANY)] * 18,
        scratch_shapes=scratch,
        compiler_params=pltpu.CompilerParams(collective_id=cid, has_side_effects=True, vmem_limit_bytes=67043328),
        name="forward",
    )(x, pick, row, col, *shards)


def tdot(a, b):
    return lax.dot_general(a, b, (((0,), (0,)), ((), ())), preferred_element_type=F32)

def norm_parts(z):
    center = z - jnp.mean(z, axis=1, keepdims=True)
    inv = lax.rsqrt(jnp.mean(center * center, axis=1, keepdims=True) + 1e-12)
    return center * inv, inv

def norm_back(hat, inv, g):
    return inv * (g - jnp.mean(g, axis=1, keepdims=True) - hat * jnp.mean(g * hat, axis=1, keepdims=True))

def middle_kernel(pick, norms, t, ab, f, cot, h, yb, mix, wo, gb, sl, wd, wu, ff,
                  o_res, o_dh, o_do, g_fa, g_fb, g_ao, g_au, g_bo, g_bd,
                  v_f, v_cot, v_res, v_de, v_dy, v_yb, v_mix, v_wo, v_du, tdn, tup, tout, acc, sem, osem):
    j = pl.program_id(0)
    last = pl.num_programs(0) - 1
    rows, width = v_f.shape
    cols = pick.shape[2]
    step = 256
    blocks = rows // step
    length = rows // pick.shape[0]

    def rows_at(r):
        return pl.ds(pl.multiple_of(r * step, step), step)

    def picked(r):
        return pick[(r * step) // length]

    def slot(i):
        return ab[:, i * cols:(i + 1) * cols]

    loads = [pltpu.make_async_copy(f, v_f, sem.at[0]), pltpu.make_async_copy(cot, v_cot, sem.at[1]),
             pltpu.make_async_copy(h, v_f, sem.at[2]), pltpu.make_async_copy(yb, v_yb, sem.at[3]),
             pltpu.make_async_copy(mix, v_mix, sem.at[4]), pltpu.make_async_copy(wo, v_wo, sem.at[5])]
    save_res = pltpu.make_async_copy(v_res, o_res, osem.at[0])
    gain_one, gain_two, shift_two = norms[0:1, :], norms[1:2, :], norms[3:4, :]

    @pl.when(j == 0)
    def _():
        loads[0].start()
        loads[1].start()
        loads[0].wait()
        loads[1].wait()

        @pl.loop(0, blocks)
        def _(r):
            at = rows_at(r)
            hat, inv = norm_parts(v_f[at, :])
            v_res[at, :] = (hat * gain_two + shift_two).astype(BF)
            df = norm_back(hat, inv, v_cot[at, :].astype(F32) * gain_two)
            v_dy[at, :] = df
            de = df.astype(BF)
            v_de[at, :] = de
            tdn[at, :] = (jnp.dot(de, slot(9), preferred_element_type=F32) * picked(r)).astype(BF)

        save_res.start()
        for c in loads[2:]:
            c.start()
        g_bd[...] = tdot(v_de[...], t[:, 5 * cols:6 * cols])
        acc[...] = jnp.zeros_like(acc)

    half = 512

    @pl.loop(0, rows // half)
    def _(r):
        at = pl.ds(pl.multiple_of(r * half, half), half)
        dg = dotf(tdn[at, :], ff[:, 0:cols], 1, 1)
        for c in range(NCH):
            w = wd.shape[2]
            dg = dg + dotf(v_de[at, c * w:(c + 1) * w], wd[c], 1, 1)
        du = (dg * sl[at, :].astype(F32)).astype(BF)
        v_du[at, :] = du
        v_dy[at, :] = v_dy[at, :] + dotf(du, wu[...], 1, 1)
        acc[at, :] = acc[at, :] + jnp.dot(du, ff[:, cols:2 * cols], preferred_element_type=F32)

    g_fa[...] = tdot(gb[...], tdn[...])
    g_fb[...] = tdot(v_du[...], t[:, 4 * cols:5 * cols])

    @pl.when(j == last)
    def _():
        for c in loads[2:]:
            c.wait()
        save_res.wait()

        @pl.loop(0, blocks)
        def _(r):
            at = rows_at(r)
            dtu = (acc[at, :] * picked(r)).astype(BF)
            tup[at, :] = dtu
            dy = v_dy[at, :] + dotf(dtu, slot(4), 1, 1)
            hat, inv = norm_parts(v_f[at, :])
            dh = norm_back(hat, inv, dy * gain_one)
            v_dy[at, :] = dh
            da = dh.astype(BF)
            v_de[at, :] = da
            dto = (jnp.dot(da, slot(8), preferred_element_type=F32) * picked(r)).astype(BF)
            tout[at, :] = dto
            v_res[at, :] = (dotf(da, v_wo[...], 1, 1) + dotf(dto, slot(3), 1, 1)).astype(BF)

        save_dh = pltpu.make_async_copy(v_dy, o_dh, osem.at[1])
        save_do = pltpu.make_async_copy(v_res, o_do, osem.at[2])
        save_dh.start()
        save_do.start()
        g_au[...] = tdot(v_yb[...], tup[...])
        g_bo[...] = tdot(v_de[...], t[:, 3 * cols:4 * cols])
        g_ao[...] = tdot(v_mix[...], tout[...])
        save_dh.wait()
        save_do.wait()


def middle(pick, norms, t, ab, f, cot, h, yb, mix, wo, gb, sl, dn, up, ff):
    rows, width = f.shape
    cols = pick.shape[2]
    total = gb.shape[1]
    blk = 512
    per = sl.shape[2] // blk
    S, V = jax.ShapeDtypeStruct, pltpu.VMEM
    whole = pl.BlockSpec(memory_space=pltpu.VMEM)
    far = pl.BlockSpec(memory_space=pl.ANY)
    wcol = dn.shape[2]
    return pl.pallas_call(
        middle_kernel,
        grid=(total // blk,),
        in_specs=[whole] * 4 + [far] * 6 + [
            pl.BlockSpec((rows, blk), lambda j: (0, j)),
            pl.BlockSpec((None, rows, blk), lambda j: (j // per, 0, j % per)),
            pl.BlockSpec((NCH, blk, wcol), lambda j: (0, j, 0)),
            pl.BlockSpec((None, width, blk), lambda j: (j // per, 0, j % per)),
            pl.BlockSpec((blk, 2 * cols), lambda j: (j, 0)),
        ],
        out_specs=[far] * 3 + [pl.BlockSpec((blk, cols), lambda j: (j, 0))] * 2 + [pl.BlockSpec((width, cols), lambda j: (0, 0))] * 4,
        out_shape=[S(f.shape, BF), S(f.shape, F32), S(f.shape, BF), S((total, cols), F32), S((total, cols), F32)] + [S((width, cols), F32)] * 4,
        scratch_shapes=[V(f.shape, F32), V(f.shape, BF), V(f.shape, BF), V(f.shape, BF), V(f.shape, F32), V(f.shape, BF), V(f.shape, BF), V((width, width), BF),
                        V((rows, blk), BF), V((rows, cols), BF), V((rows, cols), BF), V((rows, cols), BF), V((rows, cols), F32),
                        pltpu.SemaphoreType.DMA((6,)), pltpu.SemaphoreType.DMA((3,))],
        compiler_params=pltpu.CompilerParams(vmem_limit_bytes=60 * 2**20),
        name="middle",
    )(pick, norms, t, ab, f, cot, h, yb, mix, wo, gb, sl, dn, up, ff)


def back_kernel(grid, *refs):
    q, k, v, p, d, x, dh, ab, t, pick, wq = refs[:11]
    late = refs[11:17]
    o_x, o_a, o_b, o_fa, o_fb = refs[17:22]
    (b_q, b_k, b_v, b_d, b_p, v_dq, v_dk, v_dv, v_wq, v_dt, b_dh, b_x, e_a, e_b,
     lsem, wsem, hsem, xsem, send, recv) = refs[22:42]
    rest = list(refs[42:])
    here = grid.here()
    barrier_with(grid, here)
    rows, width = x.shape
    length, wide = b_q.shape[1], b_q.shape[2]
    groups = width // wide
    total = rows // length * groups
    cols = pick.shape[2]
    step = b_x.shape[1]
    blocks = rows // step
    nz = grid.n["z"]

    def put_in(out, col):
        def put(value):
            out[:, col:col + value.shape[1]] = value
        return put

    per = len(rest) // 8
    puts = [put_in(o_fa, 0), put_in(o_fb, 0), put_in(o_a, 3 * cols), put_in(o_a, 4 * cols), put_in(o_b, 3 * cols),
            put_in(o_b, 4 * cols), put_in(o_b, 0), put_in(o_a, 0)]
    units = [Scatter(grid, here, src, puts[i], rest[i * per:(i + 1) * per], send.at[i], recv.at[i])
             for i, src in enumerate(tuple(late) + (e_b, e_a))]
    steps = [u.steps() for u in units]

    def loads(i, slot):
        at = pl.ds(pl.multiple_of(i // groups * length, length), length)
        cs = pl.ds(pl.multiple_of(i % groups * wide, wide), wide)
        out = [pltpu.make_async_copy(a.at[at, cs], b.at[slot], lsem.at[slot, n]) for n, (a, b) in enumerate(((q, b_q), (k, b_k), (v, b_v), (d, b_d)))]
        return out + [pltpu.make_async_copy(p.at[i], b_p.at[slot], lsem.at[slot, 4])]

    def rows_at(r):
        return pl.ds(pl.multiple_of(r * step, step), step)

    def load_h(r, slot):
        return pltpu.make_async_copy(dh.at[rows_at(r), :], b_dh.at[slot], hsem.at[slot])

    def save_x(r, slot):
        return pltpu.make_async_copy(b_x.at[slot], o_x.at[rows_at(r), :], xsem.at[slot])

    for c in loads(0, 0):
        c.start()
    load_w = pltpu.make_async_copy(wq, v_wq, wsem)
    load_w.start()
    for s in steps[:6]:
        s[0]()
    order = [s[n] for n in range(1, 5) for s in steps[:6]]
    share = -(-len(order) // total)
    scale = jnp.asarray(HD ** -0.5, BF)
    lane = lax.broadcasted_iota(jnp.int32, (1, 128), 1) // HD

    def attend(i, carry):
        slot = i % 2

        @pl.when(i + 1 < total)
        def _():
            for c in loads(i + 1, 1 - slot):
                c.start()

        for c in loads(i, slot):
            c.wait()
        qb, kb, vb, db = b_q[slot], b_k[slot], b_v[slot], b_d[slot]
        kt, qs = (kb * scale).T, qb * scale
        dqs, dks, dvs = [], [], []
        for h in range(wide // HD):
            c = (h * HD) // 128 * 128
            vh = jnp.where(lane == (h * HD - c) // HD, vb[:, c:c + 128], jnp.zeros((), BF))
            pb = b_p[slot, (h // 2) * length:(h // 2 + 1) * length, (h % 2) * length:(h % 2 + 1) * length]
            pf = pb.astype(F32)
            dp = dotf(vh, db[:, c:c + 128], 1, 1)
            w = pf * dp
            ds = (w - pf * jnp.sum(w, axis=0, keepdims=True)).astype(BF)
            dqs.append(dotf(kt[h * HD:(h + 1) * HD], ds, 1, 0))
            dks.append(dotf(ds, qs[:, c:c + 128], 1, 0))
            dvs.append(dotf(pb, db[:, c:c + 128], 1, 0))
        at = pl.ds(pl.multiple_of(i // groups * length, length), length)
        v_dq[at, pl.ds(pl.multiple_of(i % groups * wide, wide), wide)] = jnp.concatenate(dqs, axis=0).T.astype(BF)
        for g in range(wide // 128):
            cs = pl.ds(pl.multiple_of(i % groups * wide + g * 128, 128), 128)
            v_dk[at, cs] = jnp.where(lane == 0, dks[2 * g], dks[2 * g + 1]).astype(BF)
            v_dv[at, cs] = jnp.where(lane == 0, dvs[2 * g], dvs[2 * g + 1]).astype(BF)
        for n in range(total):
            @pl.when(i == n)
            def _(n=n):
                for act in order[n * share:(n + 1) * share]:
                    act()
        return carry

    lax.fori_loop(0, total, attend, 0)
    load_h(0, 0).start()
    grads = (v_dq, v_dk, v_dv)
    part = width // nz

    @pl.loop(0, nz)
    def _(n):
        cs = pl.ds(pl.multiple_of(n * part, part), part)
        for s, g in enumerate(grads):
            e_b[n, :, :, s * cols:(s + 1) * cols] = tdot(g[:, cs], t[:, s * cols:(s + 1) * cols]).reshape(e_b.shape[1:3] + (cols,))

    steps[6][0]()

    @pl.loop(0, blocks)
    def _(r):
        at = rows_at(r)
        for s, g in enumerate(grads):
            v_dt[at, s * cols:(s + 1) * cols] = (jnp.dot(g[at, :], ab[:, (5 + s) * cols:(6 + s) * cols], preferred_element_type=F32) * pick[(r * step) // length]).astype(BF)

    @pl.loop(0, nz)
    def _(n):
        e_a[n] = tdot(x[:, pl.ds(pl.multiple_of(n * part, part), part)], v_dt[...]).reshape(e_a.shape[1:])

    steps[7][0]()
    steps[6][1]()
    load_w.wait()
    plan = [[] for _ in range(blocks)]
    tail = []
    for n in range(1, 5):
        (plan[n - 1] if n - 1 < blocks else tail).append(steps[7][n])
        if n < 4:
            (plan[n - 1] if n - 1 < blocks else tail).append(steps[6][n + 1])

    def finish(r, carry):
        slot = r % 2

        @pl.when(r + 1 < blocks)
        def _():
            load_h(r + 1, 1 - slot).start()

        load_h(r, slot).wait()

        @pl.when(r >= 2)
        def _():
            save_x(r - 2, slot).wait()

        at = rows_at(r)
        acc = b_dh[slot] + dotf(v_dt[at, :], ab[:, 0:3 * cols], 1, 1)
        for s, g in enumerate(grads):
            acc = acc + dotf(g[at, :], v_wq[:, s * width:(s + 1) * width], 1, 1)
        b_x[slot] = acc.astype(BF)
        save_x(r, slot).start()
        for n in range(blocks):
            @pl.when(r == n)
            def _(n=n):
                for act in plan[n]:
                    act()
        return carry

    lax.fori_loop(0, blocks, finish, 0)
    for act in tail:
        act()
    for u in units:
        u.finish()
    for r in range(max(0, blocks - 2), blocks):
        save_x(r, r % 2).wait()


def back(grid, q, k, v, p, d, x, dh, ab, t, pick, wq, late, cid):
    rows, width = x.shape
    seqs, cols = pick.shape[0], pick.shape[2]
    length, wide, step = rows // seqs, 4 * HD, 256
    z, m = grid.n["z"], grid.planes
    views = [a.reshape(z, m, a.shape[0] // grid.devices, a.shape[1]) for a in late]
    own = width // grid.devices
    S, V = jax.ShapeDtypeStruct, pltpu.VMEM
    sems = Scatter.sem_total(grid)
    scratch = [V((2, length, wide), BF)] * 4 + [V((2,) + p.shape[1:], BF)] + [V(x.shape, BF)] * 3 + [
        V(wq.shape, BF), V((rows, 3 * cols), BF), V((2, step, width), F32), V((2, step, width), BF),
        V((z, m, own, 3 * cols), F32), V((z, m, own, 3 * cols), F32),
        pltpu.SemaphoreType.DMA((2, 5)), pltpu.SemaphoreType.DMA, pltpu.SemaphoreType.DMA((2,)), pltpu.SemaphoreType.DMA((2,)),
        pltpu.SemaphoreType.DMA((8, sems)), pltpu.SemaphoreType.DMA((8, sems))]
    for shape in [w.shape[2:] for w in views] + [(own, 3 * cols)] * 2:
        scratch += Scatter.scratch(grid, shape)
    far, near = pl.BlockSpec(memory_space=pl.ANY), pl.BlockSpec(memory_space=pltpu.VMEM)
    return pl.pallas_call(
        functools.partial(back_kernel, grid),
        out_shape=[S(x.shape, BF), S((own, 5 * cols), F32), S((own, 5 * cols), F32)] + [S(w.shape[2:], F32) for w in views[:2]],
        in_specs=[far] * 5 + [near, far, near, near, near, far] + [near] * 6,
        out_specs=[far] + [near] * 4,
        scratch_shapes=scratch,
        compiler_params=pltpu.CompilerParams(collective_id=cid, has_side_effects=True, vmem_limit_bytes=67043328),
        name="back",
    )(q, k, v, p, d, x, dh, ab, t, pick, wq, *views)


def local_plain(sizes, tokens, cotangent, adapter_id, global_pos, w_qkv, w_out, w_up, w_down, norm_gain, norm_bias,
          narrow_in, widen_out, ff_narrow, ff_widen):
    grid = Grid(sizes)
    small = jnp.concatenate([norm_gain, norm_bias], axis=1).T
    share = small.shape[1]
    small = jnp.pad(small, ((0, 12), (0, 128 - share)))
    got = all_gather(grid, [w_qkv, narrow_in, widen_out, small, w_out, w_up, w_down, ff_narrow, ff_widen], 0, 2, True)

    def whole(a):
        return a.reshape(-1, a.shape[-1])

    wq_full, a_full, b_full, small_full, wo_full, wu_full, wd_full, ffa_full, ffb_full = [whole(a) for a in got]
    norms = small_full.reshape(grid.devices, 16, 128)[:, :4, :share].transpose(1, 0, 2).reshape(4, grid.devices * share)
    norms = norms.astype(jnp.float32)
    gain_one, gain_two, shift_one, shift_two = norms[0], norms[1], norms[2], norms[3]
    seq_local, length, model_width = tokens.shape
    rows_all = seq_local * length
    set_cols = SETS * R
    chosen = (
        lax.broadcasted_iota(jnp.int32, (seq_local, set_cols), 1) // R == adapter_id[:, None]
    ).astype(jnp.float32)
    chosen = jnp.broadcast_to(chosen[:, None, :], (seq_local, length, set_cols)).reshape(rows_all, set_cols)
    chosen_three = jnp.concatenate([chosen, chosen, chosen], axis=1)
    positions = lax.broadcasted_iota(jnp.int32, (length,), 0)
    is_global = jnp.any(global_pos[:, :, None] == positions[None, None, :], axis=1).astype(jnp.float32)

    def cols_of(slot):
        return slice(slot * set_cols, (slot + 1) * set_cols)

    flat_in = tokens.reshape(rows_all, model_width)
    t_qkv = (product(flat_in, a_full[:, : 3 * set_cols]) * chosen_three).astype(jnp.bfloat16)
    projected = []
    for slot in range(3):
        summed = product(flat_in, wq_full[:, slot * model_width : (slot + 1) * model_width]) + against(
            t_qkv[:, cols_of(slot)], b_full[:, cols_of(slot)]
        )
        projected.append(summed.astype(jnp.bfloat16))
    query_low, key_low, value_low = projected
    mixed_flat, weights_low = attn_fwd(query_low, key_low, value_low, is_global[:, None, :], is_global[:, :, None], seq_local, length, 4)
    t_out = (product(mixed_flat, a_full[:, cols_of(3)]) * chosen).astype(jnp.bfloat16)
    attn_out = product(mixed_flat, wo_full) + against(t_out, b_full[:, cols_of(3)])
    resid = flat_in.astype(jnp.float32) + attn_out
    normed, norm_one_back = jax.vjp(lambda values: normalize(values, gain_one, shift_one), resid)
    normed_low = normed.astype(jnp.bfloat16)
    t_up = (product(normed_low, a_full[:, cols_of(4)]) * chosen).astype(jnp.bfloat16)
    pre_act = product(normed_low, wu_full) + against(t_up, ffb_full)
    cdf = 0.5 * (1.0 + lax.erf(pre_act * (0.5 ** 0.5)))
    act_low = (pre_act * cdf).astype(jnp.bfloat16)
    slope = cdf + pre_act * jnp.exp(-0.5 * pre_act * pre_act) * ((0.5 / math.pi) ** 0.5)
    act_low, slope = lax.optimization_barrier((act_low, slope))
    t_down = (product(act_low, ffa_full) * chosen).astype(jnp.bfloat16)
    down_out = product(act_low, wd_full) + against(t_down, b_full[:, cols_of(4)])
    final = normed + down_out
    result, norm_two_back = jax.vjp(lambda values: normalize(values, gain_two, shift_two), final)
    d_final = norm_two_back(cotangent.reshape(rows_all, model_width).astype(jnp.float32))[0]
    d_down = d_final.astype(jnp.bfloat16)
    dt_down = (product(d_down, b_full[:, cols_of(4)]) * chosen).astype(jnp.bfloat16)
    grad_b_down = over_rows(d_down, t_down)
    grad_ff_narrow = over_rows(act_low, dt_down)
    d_act = against(d_down, wd_full) + against(dt_down, ffa_full)
    d_pre = (d_act * slope).astype(jnp.bfloat16)
    dt_up = (product(d_pre, ffb_full) * chosen).astype(jnp.bfloat16)
    grad_ff_widen = over_rows(d_pre, t_up)
    grad_a_up = over_rows(normed_low, dt_up)
    d_normed = d_final + against(d_pre, wu_full) + against(dt_up, a_full[:, cols_of(4)])
    d_resid = norm_one_back(d_normed)[0]
    d_attn = d_resid.astype(jnp.bfloat16)
    dt_out = (product(d_attn, b_full[:, cols_of(3)]) * chosen).astype(jnp.bfloat16)
    grad_b_out = over_rows(d_attn, t_out)
    grad_a_out = over_rows(mixed_flat, dt_out)
    d_mixed = (against(d_attn, wo_full) + against(dt_out, a_full[:, cols_of(3)])).astype(jnp.bfloat16)
    d_parts = attn_bwd(query_low, key_low, value_low, weights_low, d_mixed, seq_local, length, 4)
    dt_parts = [
        (product(d_parts[slot], b_full[:, cols_of(slot)]) * chosen).astype(jnp.bfloat16) for slot in range(3)
    ]
    dt_qkv = jnp.concatenate(dt_parts, axis=1)
    grad_b_qkv = [over_rows(d_parts[slot], t_qkv[:, cols_of(slot)]) for slot in range(3)]
    grad_a_qkv = over_rows(flat_in, dt_qkv)
    d_input = d_resid + against(dt_qkv, a_full[:, : 3 * set_cols])
    for slot in range(3):
        d_input = d_input + against(d_parts[slot], wq_full[:, slot * model_width : (slot + 1) * model_width])
    rows_own, ff_own = model_width // grid.devices, ff_narrow.shape[0]
    late = reduce_scatter(
        grid, [grad_ff_narrow, grad_ff_widen, grad_a_out, grad_a_up, grad_b_out, grad_b_down],
        [(0, 0), (1, 0), (2, 0), (2, set_cols), (3, 0), (3, set_cols)],
        [(ff_own, set_cols), (ff_own, set_cols), (rows_own, 2 * set_cols), (rows_own, 2 * set_cols)], 1)
    early = reduce_scatter(
        grid, [grad_a_qkv] + grad_b_qkv, [(0, 0), (1, 0), (1, set_cols), (1, 2 * set_cols)],
        [(rows_own, 3 * set_cols), (rows_own, 3 * set_cols)], 2)
    return (
        result.reshape(seq_local, length, model_width).astype(jnp.bfloat16),
        d_input.reshape(seq_local, length, model_width).astype(jnp.bfloat16),
        jnp.concatenate([early[0], late[2]], axis=1),
        jnp.concatenate([early[1], late[3]], axis=1),
        late[0],
        late[1],
    )


LAG = 2


def local(sizes, tokens, cotangent, adapter_id, global_pos, w_qkv, w_out, w_up, w_down, norm_gain, norm_bias,
          narrow_in, widen_out, ff_narrow, ff_widen):
    grid = Grid(sizes)
    seq_local, length, width = tokens.shape
    rows = seq_local * length
    own = w_qkv.shape[0]
    fits = own % 16 == 0 and 128 % own == 0 and rows == 2 * length and w_up.shape[1] == 4 * rows and width == rows
    if not fits:
        return local_plain(sizes, tokens, cotangent, adapter_id, global_pos, w_qkv, w_out, w_up, w_down, norm_gain,
                           norm_bias, narrow_in, widen_out, ff_narrow, ff_widen)
    cols = SETS * R
    flat_in = tokens.reshape(rows, width)
    pick = (lax.broadcasted_iota(jnp.int32, (seq_local, 1, cols), 2) // R == adapter_id[:, None, None]).astype(F32)
    positions = lax.broadcasted_iota(jnp.int32, (length,), 0)
    is_global = jnp.any(global_pos[:, :, None] == positions[None, None, :], axis=1).astype(F32)
    place = (lax.axis_index("dp") * grid.fsdp + lax.axis_index("fsdp")) % (128 // own)
    small = jnp.tile(jnp.concatenate([norm_gain, norm_bias], axis=1).T, (1, 128 // own))
    mine = lax.broadcasted_iota(jnp.int32, (1, 128), 1) // own == place
    small = jnp.pad(jnp.where(mine, small, jnp.zeros((), BF)), ((0, 12), (0, 0)))
    shards = (small, jnp.concatenate([narrow_in, widen_out], axis=1), w_qkv, w_out, w_up,
              jnp.concatenate([ff_narrow, ff_widen], axis=1), w_down)
    (g_small, g_ab, g_qkv, g_out, g_up, g_ff, g_dn, q, k, v, p, mix, h, f, yb, t, gb, sl) = forward(
        grid, flat_in, pick, is_global[:, None, :], is_global[:, :, None], shards, LAG, 0)
    ab, wq, wo, ff = (flat2(a) for a in (g_ab, g_qkv, g_out, g_ff))
    up = g_up.reshape(NCH, width, -1)
    dn = g_dn.reshape(NCH, w_up.shape[1], -1)
    per = 128 // own
    norms = g_small.reshape(width // 128, per, 16, 128).astype(F32).sum(axis=1)[:, :4].transpose(1, 0, 2).reshape(4, width)
    norms = jnp.pad(norms, ((0, 4), (0, 0)))
    res, dh, do, g_fa, g_fb, g_ao, g_au, g_bo, g_bd = middle(
        pick, norms, t, ab, f, cotangent.reshape(rows, width), h, yb, mix, wo, gb, sl, dn, up, ff)
    d_input, grad_a, grad_b, grad_fa, grad_fb = back(
        grid, q, k, v, p, do, flat_in, dh, ab, t, pick, wq, [g_fa, g_fb, g_ao, g_au, g_bo, g_bd], 1)
    return res.reshape(tokens.shape), d_input.reshape(tokens.shape), grad_a, grad_b, grad_fa, grad_fb


def solution(mesh):
    rows = P(("dp", "fsdp"), None)
    cube = P(("dp", "fsdp"), None, None)
    in_specs = (cube, cube, P(("dp", "fsdp"))) + (rows,) * 11
    out_specs = (cube, cube) + (rows,) * 4
    return jax.shard_map(functools.partial(local, dict(mesh.shape)), mesh=mesh, in_specs=in_specs, out_specs=out_specs, check_vma=False)
```

```python
import functools, math
import jax
import jax.numpy as jnp
from jax import lax
from jax.experimental import pallas as pl
from jax.experimental.pallas import tpu as pltpu
from jax.sharding import PartitionSpec as P

MESH = pl.DeviceIdType.MESH


class Grid:
    def __init__(self, sizes):
        self.dp, self.fsdp = sizes["dp"], sizes["fsdp"]
        if (self.dp, self.fsdp) == (8, 4):
            self.dims = {"z": ("dp", 2, 4), "y": ("dp", 1, 2), "x": ("fsdp", 2, 2), "c": ("fsdp", 1, 2)}
        elif (self.dp, self.fsdp) == (64, 4):
            self.dims = {"z": ("dp", 8, 8), "y": ("dp", 2, 4), "x": ("fsdp", 1, 4), "c": ("dp", 1, 2)}
        else:
            self.dims = {"z": ("dp", 1, self.dp), "y": ("dp", 1, 1), "x": ("fsdp", self.fsdp, 1), "c": ("fsdp", 1, self.fsdp)}
        self.n = {k: v[2] for k, v in self.dims.items()}
        self.devices = self.dp * self.fsdp
        self.planes = self.devices // self.n["z"]

    def stride(self, k):
        axis, step, _ = self.dims[k]
        return step * (self.fsdp if axis == "dp" else 1)

    def here(self):
        idx = {"dp": lax.axis_index("dp"), "fsdp": lax.axis_index("fsdp")}
        return {k: (idx[axis] // step) % size for k, (axis, step, size) in self.dims.items()}

    def device(self, pos):
        out = {"dp": 0, "fsdp": 0}
        for k, (axis, step, _) in self.dims.items():
            out[axis] = out[axis] + pos[k] * step
        return out["dp"], out["fsdp"]

    def slot(self, y, x, c):
        return y * self.stride("y") + x * self.stride("x") + c * self.stride("c")


def barrier_with(grid, here):
    barrier = pltpu.get_barrier_semaphore()
    count = 0
    for k in ("z", "y", "x", "c"):
        n = grid.n[k]
        for step in range(1, n):
            to = (here[k] + step) % n
            pl.semaphore_signal(barrier, inc=1, device_id=grid.device({**here, k: to}), device_id_type=MESH)
            count += 1
    pl.semaphore_wait(barrier, count)


class Gather:
    @staticmethod
    def parts(grid):
        return grid.n["z"] if grid.n["z"] <= 4 else 1

    @staticmethod
    def sem_total(grid):
        z, a, b, c = (grid.n[k] for k in ("z", "y", "x", "c"))
        k = Gather.parts(grid)
        return z + k * a + k * a * b + a * b

    def __init__(self, grid, here, src, out, send, recv, local):
        self.g, self.here, self.src, self.out = grid, here, src, out
        self.send, self.recv, self.local = send, recv, local
        self.k = Gather.parts(grid)
        self.nz, self.n2, self.n3 = grid.n["z"], grid.n["y"], grid.n["x"]
        self.base2 = self.nz
        self.base3 = self.base2 + self.k * self.n2
        self.base4 = self.base3 + self.k * self.n2 * self.n3
        self.sends = []
        self.first = here["c"] == 0
        self.p2 = jnp.where(self.first, here["y"], here["x"])
        self.p3 = jnp.where(self.first, here["x"], here["y"])

    def dev(self, z=None, p2=None, p3=None, c=None):
        h = self.here
        p2 = self.p2 if p2 is None else p2
        p3 = self.p3 if p3 is None else p3
        return self.g.device({
            "z": h["z"] if z is None else z,
            "y": jnp.where(self.first, p2, p3),
            "x": jnp.where(self.first, p3, p2),
            "c": h["c"] if c is None else c,
        })

    def m(self, p2, p3):
        return self.g.slot(jnp.where(self.first, p2, p3), jnp.where(self.first, p3, p2), self.here["c"])

    def part(self, i):
        return (self.here["z"] ^ i) if self.k == self.nz and self.nz & (self.nz - 1) == 0 else None

    def block(self, z, p2, p3):
        return self.out.at[:, self.m(p2, p3)] if z is None else self.out.at[z, self.m(p2, p3)]

    def copy(self, src, dst, sem, dev):
        return pltpu.make_async_remote_copy(src_ref=src, dst_ref=dst, send_sem=self.send.at[sem], recv_sem=self.recv.at[sem], device_id=dev, device_id_type=MESH)

    def pull(self, dst, sem):
        self.copy(dst, dst, sem, self.dev()).wait_recv()

    def sem2(self, z, p2):
        return self.base2 + (0 if z is None else z * self.n2) + p2

    def sem3(self, z, p2, p3):
        return self.base3 + ((0 if z is None else z * self.n2) + p2) * self.n3 + p3

    def to2(self, z, src=None):
        ref = self.block(z, self.p2, self.p3)
        return [self.copy(ref if src is None else src, ref, self.sem2(z, self.p2), self.dev(p2=(self.p2 + d) % self.n2)) for d in range(1, self.n2)]

    def to3(self, z, p2, src=None):
        ref = self.block(z, p2, self.p3)
        return [self.copy(ref if src is None else src, ref, self.sem3(z, p2, self.p3), self.dev(p3=(self.p3 + d) % self.n3)) for d in range(1, self.n3)]

    def to_core(self, p2, p3):
        if self.g.n["c"] == 1:
            return []
        ref = self.block(None, p2, p3)
        y, x = jnp.where(self.first, p2, p3), jnp.where(self.first, p3, p2)
        return [self.copy(ref, ref, self.base4 + y * self.n3 + x, self.dev(c=1 - self.here["c"]))]

    def line(self, i):
        z = self.here["z"]
        return z ^ i if self.nz & (self.nz - 1) == 0 else (z + i) % self.nz

    def own(self):
        return pltpu.make_async_copy(self.src, self.out.at[self.here["z"], self.m(self.p2, self.p3)], self.local)

    def along(self):
        z = self.here["z"]
        m0 = self.m(self.p2, self.p3)
        return [self.copy(self.src, self.out.at[z, m0], z, self.dev(z=self.line(i))) for i in range(1, self.nz)]

    def launch(self):
        for c in self.along():
            c.start()

    def begin(self):
        z = self.here["z"]
        return self.to3(z, self.p2, self.src) + self.to2(z, self.src) if self.part(0) is not None else []

    def wait_z(self, i):
        z = self.line(i)
        self.pull(self.out.at[z, self.m(self.p2, self.p3)], z)

    def after_z(self, i):
        return self.to2(self.part(i)) + self.to3(self.part(i), self.p2) if self.part(i) is not None else []

    def after_line(self):
        out = [] if self.part(0) is not None else self.to2(None) + self.to3(None, self.p2)
        return out + self.to_core(self.p2, self.p3)

    def wait2(self, i):
        z = self.part(i)
        for d in range(1, self.n2):
            q = (self.p2 + d) % self.n2
            self.pull(self.block(z, q, self.p3), self.sem2(z, q))

    def after2(self, i):
        return [c for d in range(1, self.n2) for c in self.to3(self.part(i), (self.p2 + d) % self.n2)]

    def after_all2(self):
        return [c for d in range(1, self.n2) for c in self.to_core((self.p2 + d) % self.n2, self.p3)]

    def wait3(self, j):
        p2 = (self.p2 + j) % self.n2
        for d in range(1, self.n3):
            q = (self.p3 + d) % self.n3
            for i in range(self.k):
                z = self.part(i)
                self.pull(self.block(z, p2, q), self.sem3(z, p2, q))

    def after3(self, j):
        p2 = (self.p2 + j) % self.n2
        return [c for d in range(1, self.n3) for c in self.to_core(p2, (self.p3 + d) % self.n3)]

    def pairs(self):
        part = functools.partial
        out = [(lambda: self.own().start(), self.begin)]
        out += [(part(self.wait_z, i), part(self.after_z, i)) for i in range(1, self.nz)]
        out += [(lambda: self.own().wait(), self.after_line)]
        out += [(part(self.wait2, i), part(self.after2, i)) for i in range(self.k)]
        out += [(lambda: None, self.after_all2)]
        out += [(part(self.wait3, j), part(self.after3, j)) for j in range(self.n2)]
        return out

    def steps(self):
        def act(wait, copies):
            wait()
            for c in copies():
                c.start()
        return [functools.partial(act, *p) for p in self.pairs()] + [self.arrived]

    def arrived(self):
        if self.g.n["c"] > 1:
            for y in range(self.n2):
                for x in range(self.n3):
                    self.pull(self.out.at[:, self.g.slot(y, x, 1 - self.here["c"])], self.base4 + y * self.n3 + x)

    def finish(self):
        for c in self.along():
            c.wait_send()
        for _, copies in self.pairs():
            for c in copies():
                c.wait_send()


def skewed(all_steps, lag):
    count = max(len(s) for s in all_steps)
    out = []
    for slot in range(count + lag * (len(all_steps) - 1)):
        for i, steps in enumerate(all_steps):
            k = slot - lag * i
            if 0 <= k < len(steps):
                out.append((i, steps[k]))
    return out


def run_skewed(all_steps, lag):
    for _, step in skewed(all_steps, lag):
        step()

SETS = 8
R = 16


def normalize(values, gain, shift):
    center = values - jnp.mean(values, axis=-1, keepdims=True)
    spread = jnp.mean(center * center, axis=-1, keepdims=True)
    return center * lax.rsqrt(spread + 1e-12) * gain + shift


def against(left, right):
    return lax.dot_general(
        left, right, (((1,), (1,)), ((), ())), preferred_element_type=jnp.float32
    )


def over_rows(left, right):
    return lax.dot_general(
        left, right, (((0,), (0,)), ((), ())), preferred_element_type=jnp.float32
    )


def product(left, right):
    return jnp.dot(left, right, preferred_element_type=jnp.float32)


def gelu_exact(values):
    return jax.nn.gelu(values, approximate=False)


def gather_kernel(grid, count, lag, first, *refs):
    srcs, outs = refs[:count], refs[count:2*count]
    send, recv, local = refs[2*count:]
    here = grid.here()
    barrier_with(grid, here)
    gs = [Gather(grid, here, srcs[i], outs[i], send.at[i], recv.at[i], local.at[i]) for i in range(count)]
    for g in gs:
        g.launch()
    steps = [g.steps() for g in gs]
    if first:
        for s in steps:
            s.pop(0)()
    run_skewed(steps, lag)
    for g in gs:
        g.finish()

def all_gather(grid, arrays, cid=0, lag=1, first=True):
    count = len(arrays)
    total = Gather.sem_total(grid)
    out_shape = [jax.ShapeDtypeStruct((grid.n["z"], grid.planes) + a.shape, a.dtype) for a in arrays]
    return pl.pallas_call(
        functools.partial(gather_kernel, grid, count, lag, first),
        out_shape=out_shape,
        in_specs=[pl.BlockSpec(memory_space=pltpu.VMEM)] * count,
        out_specs=[pl.BlockSpec(memory_space=pl.ANY)] * count,
        scratch_shapes=[pltpu.SemaphoreType.DMA((count, total)), pltpu.SemaphoreType.DMA((count, total)), pltpu.SemaphoreType.DMA((count,))],
        compiler_params=pltpu.CompilerParams(collective_id=cid, has_side_effects=True, vmem_limit_bytes=8*2**20),
        name="gather",
    )(*arrays)


class Scatter:
    @staticmethod
    def sem_total(grid):
        return 1 + grid.n["x"] + grid.n["y"] + grid.n["z"]

    @staticmethod
    def scratch(grid, shape, dtype=jnp.bfloat16):
        rows, cols = shape
        z, y, x = grid.n["z"], grid.n["y"], grid.n["x"]
        out = []
        if grid.n["c"] > 1:
            out += [pltpu.VMEM((y * x, z, rows, cols), dtype)] * 2
        out += [pltpu.VMEM((max(x - 1, 1), y, z, rows, cols), dtype)] * 2
        out += [pltpu.VMEM((max(y - 1, 1), z, rows, cols), dtype)] * 2
        out += [pltpu.VMEM((z, rows, cols), dtype), pltpu.VMEM((max(z - 1, 1), rows, cols), dtype)]
        out += [pltpu.VMEM((y * x, z, rows, cols), jnp.float32)]
        return out

    def __init__(self, grid, here, src, put, bufs, send, recv):
        self.g, self.here, self.src, self.put, self.send, self.recv = grid, here, src, put, send, recv
        bufs = list(bufs)
        self.two = grid.n["c"] > 1
        self.s1, self.r1 = (bufs.pop(0), bufs.pop(0)) if self.two else (None, None)
        self.s2, self.r2, self.s3, self.r3, self.s4, self.r4, self.acc = bufs
        self.nz, self.n2, self.n3 = grid.n["z"], grid.n["y"], grid.n["x"]
        self.first = here["c"] == 0
        self.p2 = jnp.where(self.first, here["y"], here["x"])
        self.p3 = jnp.where(self.first, here["x"], here["y"])
        self.sends, self.pulls = [], []

    def dev(self, z=None, p2=None, p3=None, c=None):
        h = self.here
        p2 = self.p2 if p2 is None else p2
        p3 = self.p3 if p3 is None else p3
        return self.g.device({
            "z": h["z"] if z is None else z,
            "y": jnp.where(self.first, p2, p3),
            "x": jnp.where(self.first, p3, p2),
            "c": h["c"] if c is None else c,
        })

    def flat(self, p2, p3):
        return jnp.where(self.first, p2 * self.n3 + p3, p3 * self.n3 + p2)

    def push(self, make):
        make().start()
        self.sends.append(make)

    def copy(self, src, dst, sem, dev):
        return pltpu.make_async_remote_copy(src_ref=src, dst_ref=dst, send_sem=self.send.at[sem], recv_sem=self.recv.at[sem], device_id=dev, device_id_type=MESH)

    def far(self, p, d, n):
        return (p + d) % n

    def pull(self, dst, sem):
        pltpu.make_async_remote_copy(src_ref=dst, dst_ref=dst, send_sem=self.send.at[sem], recv_sem=self.recv.at[sem], device_id=self.dev(), device_id_type=MESH).wait_recv()

    def begin(self):
        c = self.here["c"]
        for y in range(self.n2):
            for x in range(self.n3):
                i = y * self.n3 + x
                if self.two:
                    self.s1[i] = self.src[:, self.g.slot(y, x, 1 - c)].astype(self.s1.dtype)
        if self.two:
            self.push(lambda: self.copy(self.s1, self.r1, 0, self.dev(c=1 - self.here["c"])))

    def step1(self):
        c = self.here["c"]
        if self.two:
            self.pull(self.r1, 0)
        for y in range(self.n2):
            for x in range(self.n3):
                i = y * self.n3 + x
                part = self.src[:, self.g.slot(y, x, c)]
                self.acc[i] = part + self.r1[i].astype(jnp.float32) if self.two else part
        for d in range(1, self.n3):
            q = (self.p3 + d) % self.n3
            for j in range(self.n2):
                self.s2[d - 1, j] = self.acc[self.flat(j, q)].astype(self.s2.dtype)
            self.push(lambda d=d: self.copy(self.s2.at[d - 1], self.r2.at[d - 1], 1 + d, self.dev(p3=self.far(self.p3, d, self.n3))))

    def step2(self):
        for d in range(1, self.n3):
            self.pull(self.r2.at[d - 1], 1 + d)
        for j in range(self.n2):
            i = self.flat(j, self.p3)
            total = self.acc[i]
            for d in range(1, self.n3):
                total = total + self.r2[d - 1, j].astype(jnp.float32)
            self.acc[i] = total
        base = 1 + self.n3
        for d in range(1, self.n2):
            q = (self.p2 + d) % self.n2
            self.s3[d - 1] = self.acc[self.flat(q, self.p3)].astype(self.s3.dtype)
            self.push(lambda d=d: self.copy(self.s3.at[d - 1], self.r3.at[d - 1], base + d, self.dev(p2=self.far(self.p2, d, self.n2))))

    def step3(self):
        base = 1 + self.n3
        i = self.flat(self.p2, self.p3)
        total = self.acc[i]
        for d in range(1, self.n2):
            self.pull(self.r3.at[d - 1], base + d)
            total = total + self.r3[d - 1].astype(jnp.float32)
        self.acc[i] = total
        base = base + self.n2
        self.s4[...] = total.astype(self.s4.dtype)
        for d in range(1, self.nz):
            self.push(lambda d=d: self.copy(self.s4.at[self.far(self.here["z"], d, self.nz)], self.r4.at[d - 1], base + d, self.dev(z=self.far(self.here["z"], d, self.nz))))

    def step4(self):
        base = 1 + self.n3 + self.n2
        total = self.acc[self.flat(self.p2, self.p3), self.here["z"]]
        for d in range(1, self.nz):
            self.pull(self.r4.at[d - 1], base + d)
            total = total + self.r4[d - 1].astype(jnp.float32)
        self.put(total)

    def steps(self):
        return [self.begin, self.step1, self.step2, self.step3, self.step4]

    def finish(self):
        for make in self.sends:
            make().wait_send()


def scatter_kernel(grid, places, nout, *refs):
    count = len(places)
    srcs, outs = refs[:count], refs[count:count + nout]
    rest = refs[count + nout:]
    send, recv = rest[:2]
    rest = rest[2:]
    per = len(rest) // count
    here = grid.here()
    barrier_with(grid, here)
    units = []
    for i, (o, col) in enumerate(places):
        def put(total, o=o, col=col):
            outs[o][:, col:col + total.shape[1]] = total
        units.append(Scatter(grid, here, srcs[i], put, rest[i * per:(i + 1) * per], send.at[i], recv.at[i]))
    run_skewed([u.steps() for u in units], 1)
    for u in units:
        u.finish()


def reduce_scatter(grid, arrays, places, outs, cid):
    count = len(arrays)
    views = [a.reshape(grid.n["z"], grid.planes, a.shape[0] // grid.devices, a.shape[1]) for a in arrays]
    total = Scatter.sem_total(grid)
    scratch = [pltpu.SemaphoreType.DMA((count, total)), pltpu.SemaphoreType.DMA((count, total))]
    for v in views:
        scratch += Scatter.scratch(grid, v.shape[2:])
    return pl.pallas_call(
        functools.partial(scatter_kernel, grid, places, len(outs)),
        out_shape=[jax.ShapeDtypeStruct(o, jnp.float32) for o in outs],
        in_specs=[pl.BlockSpec(memory_space=pltpu.VMEM)] * count,
        out_specs=[pl.BlockSpec(memory_space=pltpu.VMEM)] * len(outs),
        scratch_shapes=scratch,
        compiler_params=pltpu.CompilerParams(collective_id=cid, has_side_effects=True, vmem_limit_bytes=60 * 2**20),
        name="scatter",
    )(*views)


HD=64
def dotf(a,b,ca,cb):
    return lax.dot_general(a,b,(((ca,),(cb,)),((),())),preferred_element_type=jnp.float32)

def set_bias(bias, row, col, half):
    n=bias.shape[0]
    i=lax.broadcasted_iota(jnp.int32,(n,n),0); j=lax.broadcasted_iota(jnp.int32,(n,n),1)
    near=jnp.abs(i-j)<=half
    ok=near|(jnp.broadcast_to(row,(n,n))>0)|(jnp.broadcast_to(col,(n,n))>0)
    bias[...]=jnp.where(ok,0.0,-1e30)

def fwd_kernel(half,row_ref,col_ref,q_ref,k_ref,v_ref,o_ref,p_ref,bias):
    @pl.when(pl.program_id(1)==0)
    def _(): set_bias(bias,row_ref[0],col_ref[0],half)
    width=q_ref.shape[1]
    q=q_ref[...]; k=k_ref[...]
    vt=v_ref[...].T
    outs=[]
    for h in range(width//HD):
        c=(h*HD)//128*128
        lane=lax.broadcasted_iota(jnp.int32,(1,128),1)//HD
        keep=(lane==(h*HD-c)//HD)
        kh=jnp.where(keep,k[:,c:c+128],jnp.zeros((),k.dtype))*jnp.asarray(HD**-0.5,k.dtype)
        s=dotf(kh,q[:,c:c+128],1,1)+bias[...]
        top=jnp.max(s,axis=0,keepdims=True)
        e=jnp.exp(s-top)
        tot=jnp.sum(e,axis=0,keepdims=True)
        p=(e*(1.0/tot)).astype(jnp.bfloat16)
        p_ref[h]=p
        outs.append(dotf(vt[h*HD:(h+1)*HD],p,1,0))
    o_ref[...]=jnp.concatenate(outs,axis=0).T.astype(o_ref.dtype)

def attn_fwd(q,k,v,row,col,seqs,length,per=2):
    rows,width=q.shape; heads=width//HD
    w=per*HD
    spec=pl.BlockSpec((length,w),lambda s,h:(s,h))
    return pl.pallas_call(functools.partial(fwd_kernel,256),grid=(seqs,heads//per),
      in_specs=[pl.BlockSpec((1,1,length),lambda s,h:(s,0,0)),pl.BlockSpec((1,length,1),lambda s,h:(s,0,0)),spec,spec,spec],
      out_specs=[spec,pl.BlockSpec((None,per,length,length),lambda s,h:(s,h,0,0))],
      out_shape=[jax.ShapeDtypeStruct(q.shape,q.dtype),jax.ShapeDtypeStruct((seqs,heads,length,length),q.dtype)],
      scratch_shapes=[pltpu.VMEM((length,length),jnp.float32)],
      compiler_params=pltpu.CompilerParams(vmem_limit_bytes=48*2**20),name="attend")(row,col,q,k,v)

def bwd_kernel(q_ref,k_ref,v_ref,p_ref,d_ref,dq_ref,dk_ref,dv_ref):
    width=q_ref.shape[1]
    q=q_ref[...]; k=k_ref[...]; v=v_ref[...]; d=d_ref[...]
    scale=jnp.asarray(HD**-0.5,q.dtype)
    kt=(k*scale).T
    qs=q*scale
    dqs=[]; dks=[]; dvs=[]
    lane=lax.broadcasted_iota(jnp.int32,(1,128),1)//HD
    for h in range(width//HD):
        c=(h*HD)//128*128
        keep=(lane==(h*HD-c)//HD)
        vh=jnp.where(keep,v[:,c:c+128],jnp.zeros((),v.dtype))
        pb=p_ref[h]
        p=pb.astype(jnp.float32)
        dp=dotf(vh,d[:,c:c+128],1,1)
        t=p*dp
        inner=jnp.sum(t,axis=0,keepdims=True)
        ds=(t-p*inner).astype(jnp.bfloat16)
        dqs.append(dotf(kt[h*HD:(h+1)*HD],ds,1,0))
        dks.append(dotf(ds,qs[:,c:c+128],1,0))
        dvs.append(dotf(pb,d[:,c:c+128],1,0))
    dq_ref[...]=jnp.concatenate(dqs,axis=0).T.astype(dq_ref.dtype)
    for g in range(width//128):
        keep=lane==0
        dk_ref[:,g*128:(g+1)*128]=jnp.where(keep,dks[2*g],dks[2*g+1]).astype(dk_ref.dtype)
        dv_ref[:,g*128:(g+1)*128]=jnp.where(keep,dvs[2*g],dvs[2*g+1]).astype(dv_ref.dtype)

def attn_bwd(q,k,v,p,d,seqs,length,per=2):
    rows,width=q.shape; heads=width//HD; w=per*HD
    spec=pl.BlockSpec((length,w),lambda s,h:(s,h))
    return pl.pallas_call(bwd_kernel,grid=(seqs,heads//per),
      in_specs=[spec,spec,spec,pl.BlockSpec((None,per,length,length),lambda s,h:(s,h,0,0)),spec],
      out_specs=[spec]*3,out_shape=[jax.ShapeDtypeStruct(q.shape,q.dtype)]*3,
      compiler_params=pltpu.CompilerParams(vmem_limit_bytes=48*2**20),name="attend_back")(q,k,v,p,d)


BF = jnp.bfloat16
F32 = jnp.float32

def flat2(v):
    return v.reshape(v.shape[0] * v.shape[1] * v.shape[2], v.shape[3])

def whole_rows(ref, c0, c1):
    return flat2(ref[:, :, :, c0:c1])

UNITS = ("small", "ab", "q", "k", "v", "out", "up0", "ff", "up1", "up2", "up3", "dn0", "dn1", "dn2", "dn3")
NCH = 4
PACE = (2, 5, 2, 3, 1, 2)

def forward_kernel(grid, lag, *refs):
    n_in = 3 + 9
    (x, ids, gpos, in_small, in_a, in_b, s_qkv, s_out, s_up, in_fa, in_fb, s_dn) = refs[:n_in]
    outs = refs[n_in:n_in + 20]
    (g_small, g_ab, g_qkv, g_out, g_up, g_ff, g_dn, o_q, o_k, o_v, o_p, o_mix, o_h, o_f, o_yb, o_t, o_gb, o_sl, o_pick, o_norms) = outs
    (b_small, b_ab, b_qkv, b_out, b_ff, b_w, v_q, v_k, v_v, stage, bias, v_mix, v_h, v_f, v_yb, v_t, v_gb, tacc,
     s_small, s_ab, s_ff, pick, row, col, v_norms, send, recv, local, lsem, osem, ssem) = refs[n_in + 20:]
    rows, width = x.shape
    length = bias.shape[0]
    seqs = rows // length
    cols = pick.shape[2]
    here = grid.here()
    s_small[...] = jnp.zeros_like(s_small)
    s_small[0:in_small.shape[0], :] = in_small[...]
    s_ab[:, 0:5 * cols] = in_a[...]
    s_ab[:, 5 * cols:10 * cols] = in_b[...]
    s_ff[:, 0:cols] = in_fa[...]
    s_ff[:, cols:2 * cols] = in_fb[...]
    for n in range(seqs):
        pick[n] = jnp.where(lax.broadcasted_iota(jnp.int32, (1, cols), 1) // R == ids[n], 1.0, 0.0)
        count = gpos.shape[1]
        same = jnp.broadcast_to(gpos[n:n + 1, :], (length, count)) == lax.broadcasted_iota(jnp.int32, (length, count), 0)
        found = jnp.max(jnp.where(same, 1.0, 0.0), axis=1, keepdims=True)
        col[n] = found
        row[n] = jnp.broadcast_to(found, (length, 128)).T[0:1]
    barrier_with(grid, here)
    spots = {"small": (s_small, g_small), "ab": (s_ab, g_ab), "out": (s_out, g_out), "ff": (s_ff, g_ff)}
    cw, dw = s_up.shape[1] // NCH, s_dn.shape[1] // NCH
    for j, n in enumerate("qkv"):
        spots[n] = (s_qkv.at[:, j * width:(j + 1) * width], g_qkv.at[j])
    for j in range(NCH):
        spots["up%d" % j] = (s_up.at[:, j * cw:(j + 1) * cw], g_up.at[j])
        spots["dn%d" % j] = (s_dn.at[:, j * dw:(j + 1) * dw], g_dn.at[j])
    units = [Gather(grid, here, *spots[n], send.at[i], recv.at[i], local.at[i]) for i, n in enumerate(UNITS)]
    order = skewed([u.steps() for u in units], lag)
    for u in units:
        u.launch()
    state = {"at": 0}
    last = {i: max(k for k, (j, _) in enumerate(order) if j == i) for i in range(len(units))}

    def pump(count):
        end = min(state["at"] + count, len(order))
        for k in range(state["at"], end):
            order[k][1]()
        state["at"] = end

    def need(name):
        pump(max(0, last[UNITS.index(name)] + 1 - state["at"]))

    def load(src, dst, k):
        return pltpu.make_async_copy(src, dst, lsem.at[k])

    need("ab")
    c_small, c_ab = load(g_small, b_small, 0), load(g_ab, b_ab, 1)
    c_small.start()
    c_ab.start()
    c_small.wait()
    c_ab.wait()

    step = 256
    blocks = rows // step

    def rows_at(r):
        return pl.ds(pl.multiple_of(r * step, step), step)

    def picked(r):
        return pick[(r * step) // length]

    def taking(count):
        base = state["at"]
        ends = [min(base + (n + 1) * count, len(order)) for n in range(blocks)]
        state["at"] = ends[-1]

        def hook(r):
            lo = base
            for n, hi in enumerate(ends):
                @pl.when(r == n)
                def _(lo=lo, hi=hi):
                    for k in range(lo, hi):
                        order[k][1]()
                lo = hi
        return hook

    for slot, dst in enumerate((v_q, v_k, v_v)):
        need("qkv"[slot])
        c_w = load(g_qkv.at[slot], b_qkv.at[slot], 2)
        c_w.start()
        c_w.wait()
        hook = taking(PACE[0])

        @pl.loop(0, blocks)
        def _(r, slot=slot, dst=dst, hook=hook):
            at = rows_at(r)
            xa = x[at, :]
            t = (jnp.dot(xa, whole_rows(b_ab, slot * cols, (slot + 1) * cols), preferred_element_type=F32) * picked(r)).astype(BF)
            v_t[at, slot * cols:(slot + 1) * cols] = t
            acc = jnp.dot(xa, flat2(b_qkv[slot]), preferred_element_type=F32)
            acc = acc + dotf(t, whole_rows(b_ab, (5 + slot) * cols, (6 + slot) * cols), 1, 1)
            dst[at, :] = acc.astype(BF)
            hook(r)
    saves = [pltpu.make_async_copy(v_q, o_q, osem.at[0]), pltpu.make_async_copy(v_k, o_k, osem.at[1]), pltpu.make_async_copy(v_v, o_v, osem.at[2])]
    for c in saves:
        c.start()

    per = 4
    groups = width // (per * HD)
    total = seqs * groups
    chunks = []
    base = state["at"]
    share = PACE[1]

    def save_p(i, slot):
        return pltpu.make_async_copy(stage.at[slot], o_p.at[i], ssem.at[slot])

    def attend(i, carry):
        seq, hp = i // groups, i % groups
        @pl.when(hp == 0)
        def _():
            set_bias(bias, row[seq], col[seq], length // 2)
        slot = i % 2
        @pl.when(i >= 2)
        def _():
            save_p(i - 2, slot).wait()
        at = pl.ds(pl.multiple_of(seq * length, length), length)
        q = v_q[at, pl.ds(pl.multiple_of(hp * per * HD, per * HD), per * HD)]
        k = v_k[at, pl.ds(pl.multiple_of(hp * per * HD, per * HD), per * HD)]
        vt = v_v[at, pl.ds(pl.multiple_of(hp * per * HD, per * HD), per * HD)].T
        got = []
        lane = lax.broadcasted_iota(jnp.int32, (1, 128), 1) // HD
        for h in range(per):
            c = (h * HD) // 128 * 128
            kh = jnp.where(lane == (h * HD - c) // HD, k[:, c:c + 128], jnp.zeros((), BF)) * jnp.asarray(HD ** -0.5, BF)
            s = dotf(kh, q[:, c:c + 128], 1, 1) + bias[...]
            e = jnp.exp(s - jnp.max(s, axis=0, keepdims=True))
            p = (e * (1.0 / jnp.sum(e, axis=0, keepdims=True))).astype(BF)
            stage[slot, (h // 2) * length:(h // 2 + 1) * length, (h % 2) * length:(h % 2 + 1) * length] = p
            got.append(dotf(vt[h * HD:(h + 1) * HD], p, 1, 0))
        v_mix[at, pl.ds(pl.multiple_of(hp * per * HD, per * HD), per * HD)] = jnp.concatenate(got, axis=0).T.astype(BF)
        save_p(i, slot).start()
        for n in range(total):
            lo, hi = base + n * share, base + (n + 1) * share
            @pl.when(i == n)
            def _():
                for k2 in range(lo, hi):
                    order[k2][1]()
        return carry

    lax.fori_loop(0, total, attend, 0)
    state["at"] = base + share * total
    save_mix = pltpu.make_async_copy(v_mix, o_mix, osem.at[3])
    save_mix.start()

    need("out")
    c_out = load(g_out, b_out, 3)
    c_out.start()
    per_group = grid.devices // (width // 128)
    small = b_small[...].reshape(width // 128, per_group, 16, 128).astype(F32).sum(axis=1)
    norms = jnp.concatenate([small[g] for g in range(width // 128)], axis=1)
    gain, shift = norms[0:1], norms[2:3]
    v_norms[...] = norms
    save_norms = pltpu.make_async_copy(v_norms, o_norms, osem.at[9])
    save_norms.start()
    save_pick = pltpu.make_async_copy(pick, o_pick, osem.at[10])
    save_pick.start()
    c_out.wait()
    hook_out = taking(PACE[2])

    @pl.loop(0, blocks)
    def _(r):
        at = rows_at(r)
        oa = v_mix[at, :]
        t = (jnp.dot(oa, whole_rows(b_ab, 3 * cols, 4 * cols), preferred_element_type=F32) * picked(r)).astype(BF)
        v_t[at, 3 * cols:4 * cols] = t
        acc = jnp.dot(oa, whole_rows(b_out, 0, width), preferred_element_type=F32)
        acc = acc + dotf(t, whole_rows(b_ab, 8 * cols, 9 * cols), 1, 1)
        h = x[at, :].astype(F32) + acc
        v_h[at, :] = h
        center = h - jnp.mean(h, axis=1, keepdims=True)
        spread = jnp.mean(center * center, axis=1, keepdims=True)
        y = center * lax.rsqrt(spread + 1e-12) * gain + shift
        v_f[at, :] = y
        yb = y.astype(BF)
        v_yb[at, :] = yb
        v_t[at, 4 * cols:5 * cols] = (jnp.dot(yb, whole_rows(b_ab, 4 * cols, 5 * cols), preferred_element_type=F32) * picked(r)).astype(BF)
        hook_out(r)

    saves2 = [pltpu.make_async_copy(v_h, o_h, osem.at[4]), pltpu.make_async_copy(v_yb, o_yb, osem.at[5])]
    for c in saves2:
        c.start()

    def save_s(j, slot):
        return pltpu.make_async_copy(stage.at[slot], o_sl.at[j], ssem.at[slot])

    save_p(total - 2, 0).wait()
    save_p(total - 1, 1).wait()

    def load_up(j, slot):
        return load(g_up.at[j], b_w.at[slot], 4 + slot)

    for j in range(NCH):
        need("up%d" % j)
        if j == 0:
            load_up(0, 0).start()
            need("ff")
            c_ff = load(g_ff, b_ff, 6)
            c_ff.start()
            c_ff.wait()
        else:
            load_up(j, j % 2).start()
        load_up(j, j % 2).wait()
        if j >= 2:
            save_s(j - 2, j % 2).wait()
        hook = taking(PACE[3])

        @pl.loop(0, blocks)
        def _(r, j=j, hook=hook):
            at = rows_at(r)
            u = jnp.dot(v_yb[at, :], whole_rows(b_w.at[j % 2], 0, cw), preferred_element_type=F32)
            wide = flat2(b_ff[:, :, :, cols:2 * cols])[j * cw:(j + 1) * cw]
            u = u + dotf(v_t[at, 4 * cols:5 * cols], wide, 1, 1)
            cdf = 0.5 * (1.0 + lax.erf(u * (0.5 ** 0.5)))
            gb = (u * cdf).astype(BF)
            v_gb[at, j * cw:(j + 1) * cw] = gb
            stage[j % 2, at, :] = (cdf + u * jnp.exp(-0.5 * u * u) * ((0.5 / math.pi) ** 0.5)).astype(BF)
            hook(r)

        save_s(j, j % 2).start()
    hook_ff = taking(PACE[4])

    @pl.loop(0, blocks)
    def _(r):
        at = rows_at(r)
        acc = jnp.dot(v_gb[at, :], flat2(b_ff[:, :, :, 0:cols]), preferred_element_type=F32)
        v_t[at, 5 * cols:6 * cols] = (acc * picked(r)).astype(BF)
        hook_ff(r)

    save_gb = pltpu.make_async_copy(v_gb, o_gb, osem.at[6])
    save_gb.start()
    save_t = pltpu.make_async_copy(v_t, o_t, osem.at[7])
    save_t.start()

    for j in range(NCH):
        need("dn%d" % j)
        slot = j % 2
        view = b_w.at[slot]
        c_dn = load(g_dn.at[j], tacc.at[slot], 7)
        c_dn.start()
        c_dn.wait()
        hook = taking(PACE[5])

        @pl.loop(0, blocks)
        def _(r, j=j, slot=slot, hook=hook):
            at = rows_at(r)
            acc = jnp.dot(v_gb[at, :], flat2(tacc[slot]), preferred_element_type=F32)
            wide = whole_rows(b_ab, 9 * cols, 10 * cols)[j * dw:(j + 1) * dw]
            acc = acc + dotf(v_t[at, 5 * cols:6 * cols], wide, 1, 1)
            v_f[at, j * dw:(j + 1) * dw] = v_f[at, j * dw:(j + 1) * dw] + acc
            hook(r)

    pump(len(order))
    save_f = pltpu.make_async_copy(v_f, o_f, osem.at[8])
    save_f.start()
    for u in units:
        u.finish()
    save_s(NCH - 2, 0).wait()
    save_s(NCH - 1, 1).wait()
    for c in saves + saves2 + [save_mix, save_gb, save_t, save_f, save_norms, save_pick]:
        c.wait()


def forward(grid, x, ids, gpos, shards, lag, cid):
    rows, width = x.shape
    seqs = ids.shape[0]
    length = rows // seqs
    in_small, in_a, in_b, s_qkv, s_out, s_up, in_fa, in_fb, s_dn = shards
    cols = in_fa.shape[1]
    z, m = grid.n["z"], grid.planes
    S = jax.ShapeDtypeStruct
    s_small, s_ab, s_ff = S((16, 128), BF), S((in_a.shape[0], 10 * cols), BF), S((in_fa.shape[0], 2 * cols), BF)
    cw, dw = s_up.shape[1] // NCH, s_dn.shape[1] // NCH
    total = Gather.sem_total(grid)
    nu = len(UNITS)
    def g(a, c=None, lead=()):
        return jax.ShapeDtypeStruct(lead + (z, m, a.shape[0], a.shape[1] if c is None else c), BF)
    out_shape = [g(s_small), g(s_ab), g(s_qkv, width, (3,)), g(s_out), g(s_up, cw, (NCH,)), g(s_ff), g(s_dn, dw, (NCH,)),
        S(x.shape, BF), S(x.shape, BF), S(x.shape, BF), S((seqs * width // (4 * HD), 2 * length, 2 * length), BF),
        S(x.shape, BF), S(x.shape, F32), S(x.shape, F32), S(x.shape, BF), S((rows, 6 * cols), BF), S((rows, s_up.shape[1]), BF), S((NCH, rows, cw), BF),
        S((seqs, 1, cols), F32), S((16, width), F32)]
    V = pltpu.VMEM
    scratch = [V((z, m) + s_small.shape, BF), V((z, m) + s_ab.shape, BF), V((3, z, m, s_qkv.shape[0], width), BF), V((z, m) + s_out.shape, BF), V((z, m) + s_ff.shape, BF),
        V((2, z, m, s_up.shape[0], cw), BF),
        V(x.shape, BF), V(x.shape, BF), V(x.shape, BF), V((2, 2 * length, 2 * length), BF), V((length, length), F32), V(x.shape, BF), V(x.shape, F32), V(x.shape, F32), V(x.shape, BF),
        V((rows, 6 * cols), BF), V((rows, s_up.shape[1]), BF), V((2, z, m, s_dn.shape[0], dw), BF),
        V(s_small.shape, BF), V(s_ab.shape, BF), V(s_ff.shape, BF), V((seqs, 1, cols), F32), V((seqs, 1, length), F32), V((seqs, length, 1), F32), V((16, width), F32),
        pltpu.SemaphoreType.DMA((nu, total)), pltpu.SemaphoreType.DMA((nu, total)), pltpu.SemaphoreType.DMA((nu,)), pltpu.SemaphoreType.DMA((8,)), pltpu.SemaphoreType.DMA((11,)), pltpu.SemaphoreType.DMA((2,))]
    return pl.pallas_call(
        functools.partial(forward_kernel, grid, lag),
        out_shape=out_shape,
        in_specs=[pl.BlockSpec(memory_space=pltpu.VMEM), pl.BlockSpec(memory_space=pltpu.SMEM)] + [pl.BlockSpec(memory_space=pltpu.VMEM)] * 10,
        out_specs=[pl.BlockSpec(memory_space=pl.ANY)] * 20,
        scratch_shapes=scratch,
        compiler_params=pltpu.CompilerParams(collective_id=cid, has_side_effects=True, vmem_limit_bytes=67043328),
        name="forward",
    )(x, ids, gpos, *shards)


def tdot(a, b):
    return lax.dot_general(a, b, (((0,), (0,)), ((), ())), preferred_element_type=F32)

def norm_parts(z):
    center = z - jnp.mean(z, axis=1, keepdims=True)
    inv = lax.rsqrt(jnp.mean(center * center, axis=1, keepdims=True) + 1e-12)
    return center * inv, inv

def norm_back(hat, inv, g):
    return inv * (g - jnp.mean(g, axis=1, keepdims=True) - hat * jnp.mean(g * hat, axis=1, keepdims=True))

def middle_kernel(pick, norms, t, ab, f, cot, h, yb, mix, wo, gb, sl, wd, wu, ff,
                  o_res, o_dh, o_do, g_fa, g_fb, g_ao, g_au, g_bo, g_bd,
                  v_f, v_cot, v_res, v_de, v_dy, v_yb, v_mix, v_wo, v_du, tdn, tup, tout, acc, sem, osem):
    j = pl.program_id(0)
    last = pl.num_programs(0) - 1
    rows, width = v_f.shape
    cols = pick.shape[2]
    step = 256
    blocks = rows // step
    length = rows // pick.shape[0]

    def rows_at(r):
        return pl.ds(pl.multiple_of(r * step, step), step)

    def picked(r):
        return pick[(r * step) // length]

    def slot(i):
        return ab[:, i * cols:(i + 1) * cols]

    loads = [pltpu.make_async_copy(f, v_f, sem.at[0]), pltpu.make_async_copy(cot, v_cot, sem.at[1]),
             pltpu.make_async_copy(h, v_f, sem.at[2]), pltpu.make_async_copy(yb, v_yb, sem.at[3]),
             pltpu.make_async_copy(mix, v_mix, sem.at[4]), pltpu.make_async_copy(wo, v_wo, sem.at[5])]
    save_res = pltpu.make_async_copy(v_res, o_res, osem.at[0])
    gain_one, gain_two, shift_two = norms[0:1, :], norms[1:2, :], norms[3:4, :]

    @pl.when(j == 0)
    def _():
        loads[0].start()
        loads[1].start()
        loads[0].wait()
        loads[1].wait()

        @pl.loop(0, blocks)
        def _(r):
            at = rows_at(r)
            hat, inv = norm_parts(v_f[at, :])
            v_res[at, :] = (hat * gain_two + shift_two).astype(BF)
            df = norm_back(hat, inv, v_cot[at, :].astype(F32) * gain_two)
            v_dy[at, :] = df
            de = df.astype(BF)
            v_de[at, :] = de
            tdn[at, :] = (jnp.dot(de, slot(9), preferred_element_type=F32) * picked(r)).astype(BF)

        save_res.start()
        for c in loads[2:]:
            c.start()
        g_bd[...] = tdot(v_de[...], t[:, 5 * cols:6 * cols])
        acc[...] = jnp.zeros_like(acc)

    half = 512

    @pl.loop(0, rows // half)
    def _(r):
        at = pl.ds(pl.multiple_of(r * half, half), half)
        dg = dotf(tdn[at, :], ff[:, 0:cols], 1, 1)
        for c in range(NCH):
            w = wd.shape[2]
            dg = dg + dotf(v_de[at, c * w:(c + 1) * w], wd[c], 1, 1)
        du = (dg * sl[at, :].astype(F32)).astype(BF)
        v_du[at, :] = du
        v_dy[at, :] = v_dy[at, :] + dotf(du, wu[...], 1, 1)
        acc[at, :] = acc[at, :] + jnp.dot(du, ff[:, cols:2 * cols], preferred_element_type=F32)

    g_fa[...] = tdot(gb[...], tdn[...])
    g_fb[...] = tdot(v_du[...], t[:, 4 * cols:5 * cols])

    @pl.when(j == last)
    def _():
        for c in loads[2:]:
            c.wait()
        save_res.wait()

        @pl.loop(0, blocks)
        def _(r):
            at = rows_at(r)
            dtu = (acc[at, :] * picked(r)).astype(BF)
            tup[at, :] = dtu
            dy = v_dy[at, :] + dotf(dtu, slot(4), 1, 1)
            hat, inv = norm_parts(v_f[at, :])
            dh = norm_back(hat, inv, dy * gain_one)
            v_dy[at, :] = dh
            da = dh.astype(BF)
            v_de[at, :] = da
            dto = (jnp.dot(da, slot(8), preferred_element_type=F32) * picked(r)).astype(BF)
            tout[at, :] = dto
            v_res[at, :] = (dotf(da, v_wo[...], 1, 1) + dotf(dto, slot(3), 1, 1)).astype(BF)

        save_dh = pltpu.make_async_copy(v_dy, o_dh, osem.at[1])
        save_do = pltpu.make_async_copy(v_res, o_do, osem.at[2])
        save_dh.start()
        save_do.start()
        g_au[...] = tdot(v_yb[...], tup[...])
        g_bo[...] = tdot(v_de[...], t[:, 3 * cols:4 * cols])
        g_ao[...] = tdot(v_mix[...], tout[...])
        save_dh.wait()
        save_do.wait()


def middle(pick, norms, t, ab, f, cot, h, yb, mix, wo, gb, sl, dn, up, ff):
    rows, width = f.shape
    cols = pick.shape[2]
    total = gb.shape[1]
    blk = 512
    per = sl.shape[2] // blk
    S, V = jax.ShapeDtypeStruct, pltpu.VMEM
    whole = pl.BlockSpec(memory_space=pltpu.VMEM)
    far = pl.BlockSpec(memory_space=pl.ANY)
    wcol = dn.shape[2]
    return pl.pallas_call(
        middle_kernel,
        grid=(total // blk,),
        in_specs=[whole] * 4 + [far] * 6 + [
            pl.BlockSpec((rows, blk), lambda j: (0, j)),
            pl.BlockSpec((None, rows, blk), lambda j: (j // per, 0, j % per)),
            pl.BlockSpec((NCH, blk, wcol), lambda j: (0, j, 0)),
            pl.BlockSpec((None, width, blk), lambda j: (j // per, 0, j % per)),
            pl.BlockSpec((blk, 2 * cols), lambda j: (j, 0)),
        ],
        out_specs=[far] * 3 + [pl.BlockSpec((blk, cols), lambda j: (j, 0))] * 2 + [pl.BlockSpec((width, cols), lambda j: (0, 0))] * 4,
        out_shape=[S(f.shape, BF), S(f.shape, F32), S(f.shape, BF), S((total, cols), F32), S((total, cols), F32)] + [S((width, cols), F32)] * 4,
        scratch_shapes=[V(f.shape, F32), V(f.shape, BF), V(f.shape, BF), V(f.shape, BF), V(f.shape, F32), V(f.shape, BF), V(f.shape, BF), V((width, width), BF),
                        V((rows, blk), BF), V((rows, cols), BF), V((rows, cols), BF), V((rows, cols), BF), V((rows, cols), F32),
                        pltpu.SemaphoreType.DMA((6,)), pltpu.SemaphoreType.DMA((3,))],
        compiler_params=pltpu.CompilerParams(vmem_limit_bytes=60 * 2**20),
        name="middle",
    )(pick, norms, t, ab, f, cot, h, yb, mix, wo, gb, sl, dn, up, ff)


def back_kernel(grid, *refs):
    q, k, v, p, d, x, dh, ab, t, pick, wq = refs[:11]
    late = refs[11:17]
    o_x, o_a, o_b, o_fa, o_fb = refs[17:22]
    (b_q, b_k, b_v, b_d, b_p, v_dq, v_dk, v_dv, v_wq, v_dt, b_dh, b_x, e_a, e_b,
     lsem, wsem, hsem, xsem, send, recv) = refs[22:42]
    rest = list(refs[42:])
    here = grid.here()
    barrier_with(grid, here)
    rows, width = x.shape
    length, wide = b_q.shape[1], b_q.shape[2]
    groups = width // wide
    total = rows // length * groups
    cols = pick.shape[2]
    step = b_x.shape[1]
    blocks = rows // step
    nz = grid.n["z"]

    def put_in(out, col):
        def put(value):
            out[:, col:col + value.shape[1]] = value
        return put

    per = len(rest) // 8
    puts = [put_in(o_fa, 0), put_in(o_fb, 0), put_in(o_a, 3 * cols), put_in(o_a, 4 * cols), put_in(o_b, 3 * cols),
            put_in(o_b, 4 * cols), put_in(o_b, 0), put_in(o_a, 0)]
    units = [Scatter(grid, here, src, puts[i], rest[i * per:(i + 1) * per], send.at[i], recv.at[i])
             for i, src in enumerate(tuple(late) + (e_b, e_a))]
    steps = [u.steps() for u in units]

    def loads(i, slot):
        at = pl.ds(pl.multiple_of(i // groups * length, length), length)
        cs = pl.ds(pl.multiple_of(i % groups * wide, wide), wide)
        out = [pltpu.make_async_copy(a.at[at, cs], b.at[slot], lsem.at[slot, n]) for n, (a, b) in enumerate(((q, b_q), (k, b_k), (v, b_v), (d, b_d)))]
        return out + [pltpu.make_async_copy(p.at[i], b_p.at[slot], lsem.at[slot, 4])]

    def rows_at(r):
        return pl.ds(pl.multiple_of(r * step, step), step)

    def load_h(r, slot):
        return pltpu.make_async_copy(dh.at[rows_at(r), :], b_dh.at[slot], hsem.at[slot])

    def save_x(r, slot):
        return pltpu.make_async_copy(b_x.at[slot], o_x.at[rows_at(r), :], xsem.at[slot])

    for c in loads(0, 0):
        c.start()
    load_w = pltpu.make_async_copy(wq, v_wq, wsem)
    load_w.start()
    for s in steps[:6]:
        s[0]()
    order = [s[n] for n in range(1, 5) for s in steps[:6]]
    share = -(-len(order) // total)
    scale = jnp.asarray(HD ** -0.5, BF)
    lane = lax.broadcasted_iota(jnp.int32, (1, 128), 1) // HD

    def attend(i, carry):
        slot = i % 2

        @pl.when(i + 1 < total)
        def _():
            for c in loads(i + 1, 1 - slot):
                c.start()

        for c in loads(i, slot):
            c.wait()
        qb, kb, vb, db = b_q[slot], b_k[slot], b_v[slot], b_d[slot]
        kt, qs = (kb * scale).T, qb * scale
        dqs, dks, dvs = [], [], []
        for h in range(wide // HD):
            c = (h * HD) // 128 * 128
            vh = jnp.where(lane == (h * HD - c) // HD, vb[:, c:c + 128], jnp.zeros((), BF))
            pb = b_p[slot, (h // 2) * length:(h // 2 + 1) * length, (h % 2) * length:(h % 2 + 1) * length]
            pf = pb.astype(F32)
            dp = dotf(vh, db[:, c:c + 128], 1, 1)
            w = pf * dp
            ds = (w - pf * jnp.sum(w, axis=0, keepdims=True)).astype(BF)
            dqs.append(dotf(kt[h * HD:(h + 1) * HD], ds, 1, 0))
            dks.append(dotf(ds, qs[:, c:c + 128], 1, 0))
            dvs.append(dotf(pb, db[:, c:c + 128], 1, 0))
        at = pl.ds(pl.multiple_of(i // groups * length, length), length)
        v_dq[at, pl.ds(pl.multiple_of(i % groups * wide, wide), wide)] = jnp.concatenate(dqs, axis=0).T.astype(BF)
        for g in range(wide // 128):
            cs = pl.ds(pl.multiple_of(i % groups * wide + g * 128, 128), 128)
            v_dk[at, cs] = jnp.where(lane == 0, dks[2 * g], dks[2 * g + 1]).astype(BF)
            v_dv[at, cs] = jnp.where(lane == 0, dvs[2 * g], dvs[2 * g + 1]).astype(BF)
        for n in range(total):
            @pl.when(i == n)
            def _(n=n):
                for act in order[n * share:(n + 1) * share]:
                    act()
        return carry

    lax.fori_loop(0, total, attend, 0)
    load_h(0, 0).start()
    grads = (v_dq, v_dk, v_dv)
    part = width // nz

    @pl.loop(0, nz)
    def _(n):
        cs = pl.ds(pl.multiple_of(n * part, part), part)
        for s, g in enumerate(grads):
            e_b[n, :, :, s * cols:(s + 1) * cols] = tdot(g[:, cs], t[:, s * cols:(s + 1) * cols]).reshape(e_b.shape[1:3] + (cols,))

    steps[6][0]()

    @pl.loop(0, blocks)
    def _(r):
        at = rows_at(r)
        for s, g in enumerate(grads):
            v_dt[at, s * cols:(s + 1) * cols] = (jnp.dot(g[at, :], ab[:, (5 + s) * cols:(6 + s) * cols], preferred_element_type=F32) * pick[(r * step) // length]).astype(BF)

    @pl.loop(0, nz)
    def _(n):
        e_a[n] = tdot(x[:, pl.ds(pl.multiple_of(n * part, part), part)], v_dt[...]).reshape(e_a.shape[1:])

    steps[7][0]()
    steps[6][1]()
    load_w.wait()
    plan = [[] for _ in range(blocks)]
    tail = []
    for n in range(1, 5):
        (plan[n - 1] if n - 1 < blocks else tail).append(steps[7][n])
        if n < 4:
            (plan[n - 1] if n - 1 < blocks else tail).append(steps[6][n + 1])

    def finish(r, carry):
        slot = r % 2

        @pl.when(r + 1 < blocks)
        def _():
            load_h(r + 1, 1 - slot).start()

        load_h(r, slot).wait()

        @pl.when(r >= 2)
        def _():
            save_x(r - 2, slot).wait()

        at = rows_at(r)
        acc = b_dh[slot] + dotf(v_dt[at, :], ab[:, 0:3 * cols], 1, 1)
        for s, g in enumerate(grads):
            acc = acc + dotf(g[at, :], v_wq[s], 1, 1)
        b_x[slot] = acc.astype(BF)
        save_x(r, slot).start()
        for n in range(blocks):
            @pl.when(r == n)
            def _(n=n):
                for act in plan[n]:
                    act()
        return carry

    lax.fori_loop(0, blocks, finish, 0)
    for act in tail:
        act()
    for u in units:
        u.finish()
    for r in range(max(0, blocks - 2), blocks):
        save_x(r, r % 2).wait()


def back(grid, q, k, v, p, d, x, dh, ab, t, pick, wq, late, cid):
    rows, width = x.shape
    seqs, cols = pick.shape[0], pick.shape[2]
    length, wide, step = rows // seqs, 4 * HD, 256
    z, m = grid.n["z"], grid.planes
    views = [a.reshape(z, m, a.shape[0] // grid.devices, a.shape[1]) for a in late]
    own = width // grid.devices
    S, V = jax.ShapeDtypeStruct, pltpu.VMEM
    sems = Scatter.sem_total(grid)
    scratch = [V((2, length, wide), BF)] * 4 + [V((2,) + p.shape[1:], BF)] + [V(x.shape, BF)] * 3 + [
        V(wq.shape, BF), V((rows, 3 * cols), BF), V((2, step, width), F32), V((2, step, width), BF),
        V((z, m, own, 3 * cols), F32), V((z, m, own, 3 * cols), F32),
        pltpu.SemaphoreType.DMA((2, 5)), pltpu.SemaphoreType.DMA, pltpu.SemaphoreType.DMA((2,)), pltpu.SemaphoreType.DMA((2,)),
        pltpu.SemaphoreType.DMA((8, sems)), pltpu.SemaphoreType.DMA((8, sems))]
    for shape in [w.shape[2:] for w in views] + [(own, 3 * cols)] * 2:
        scratch += Scatter.scratch(grid, shape)
    far, near = pl.BlockSpec(memory_space=pl.ANY), pl.BlockSpec(memory_space=pltpu.VMEM)
    return pl.pallas_call(
        functools.partial(back_kernel, grid),
        out_shape=[S(x.shape, BF), S((own, 5 * cols), F32), S((own, 5 * cols), F32)] + [S(w.shape[2:], F32) for w in views[:2]],
        in_specs=[far] * 5 + [near, far, near, near, near, far] + [near] * 6,
        out_specs=[far] + [near] * 4,
        scratch_shapes=scratch,
        compiler_params=pltpu.CompilerParams(collective_id=cid, has_side_effects=True, vmem_limit_bytes=67043328),
        name="back",
    )(q, k, v, p, d, x, dh, ab, t, pick, wq, *views)


def settle_kernel(pieces, *refs):
    count = len(pieces)
    ins, outs, bufs = refs[:count], refs[count:2 * count], refs[2 * count:3 * count]
    isem, osem = refs[3 * count:]
    pairs = []
    for i, n in enumerate(pieces):
        each = ins[i].shape[0] // n
        for k in range(n):
            at = pl.ds(k * each, each)
            slot = len(pairs)
            pairs.append((pltpu.make_async_copy(ins[i].at[at], bufs[i].at[at], isem.at[slot]), pltpu.make_async_copy(bufs[i].at[at], outs[i].at[at], osem.at[slot])))
    for load, _ in pairs:
        load.start()
    for load, save in pairs:
        load.wait()
        save.start()
    for _, save in pairs:
        save.wait()


def settle(arrays):
    pieces = tuple(4 if a.size * a.dtype.itemsize >= 2**20 else 1 for a in arrays)
    far = pl.BlockSpec(memory_space=pl.ANY)
    return pl.pallas_call(
        functools.partial(settle_kernel, pieces),
        out_shape=[jax.ShapeDtypeStruct(a.shape, a.dtype) for a in arrays],
        in_specs=[far] * len(arrays), out_specs=[far] * len(arrays),
        scratch_shapes=[pltpu.VMEM(a.shape, a.dtype) for a in arrays] + [pltpu.SemaphoreType.DMA((sum(pieces),))] * 2,
        compiler_params=pltpu.CompilerParams(vmem_limit_bytes=60 * 2**20),
        name="settle",
    )(*arrays)


def local_plain(sizes, tokens, cotangent, adapter_id, global_pos, w_qkv, w_out, w_up, w_down, norm_gain, norm_bias,
          narrow_in, widen_out, ff_narrow, ff_widen):
    grid = Grid(sizes)
    small = jnp.concatenate([norm_gain, norm_bias], axis=1).T
    share = small.shape[1]
    small = jnp.pad(small, ((0, 12), (0, 128 - share)))
    got = all_gather(grid, [w_qkv, narrow_in, widen_out, small, w_out, w_up, w_down, ff_narrow, ff_widen], 0, 2, True)

    def whole(a):
        return a.reshape(-1, a.shape[-1])

    wq_full, a_full, b_full, small_full, wo_full, wu_full, wd_full, ffa_full, ffb_full = [whole(a) for a in got]
    norms = small_full.reshape(grid.devices, 16, 128)[:, :4, :share].transpose(1, 0, 2).reshape(4, grid.devices * share)
    norms = norms.astype(jnp.float32)
    gain_one, gain_two, shift_one, shift_two = norms[0], norms[1], norms[2], norms[3]
    seq_local, length, model_width = tokens.shape
    rows_all = seq_local * length
    set_cols = SETS * R
    chosen = (
        lax.broadcasted_iota(jnp.int32, (seq_local, set_cols), 1) // R == adapter_id[:, None]
    ).astype(jnp.float32)
    chosen = jnp.broadcast_to(chosen[:, None, :], (seq_local, length, set_cols)).reshape(rows_all, set_cols)
    chosen_three = jnp.concatenate([chosen, chosen, chosen], axis=1)
    positions = lax.broadcasted_iota(jnp.int32, (length,), 0)
    is_global = jnp.any(global_pos[:, :, None] == positions[None, None, :], axis=1).astype(jnp.float32)

    def cols_of(slot):
        return slice(slot * set_cols, (slot + 1) * set_cols)

    flat_in = tokens.reshape(rows_all, model_width)
    t_qkv = (product(flat_in, a_full[:, : 3 * set_cols]) * chosen_three).astype(jnp.bfloat16)
    projected = []
    for slot in range(3):
        summed = product(flat_in, wq_full[:, slot * model_width : (slot + 1) * model_width]) + against(
            t_qkv[:, cols_of(slot)], b_full[:, cols_of(slot)]
        )
        projected.append(summed.astype(jnp.bfloat16))
    query_low, key_low, value_low = projected
    mixed_flat, weights_low = attn_fwd(query_low, key_low, value_low, is_global[:, None, :], is_global[:, :, None], seq_local, length, 4)
    t_out = (product(mixed_flat, a_full[:, cols_of(3)]) * chosen).astype(jnp.bfloat16)
    attn_out = product(mixed_flat, wo_full) + against(t_out, b_full[:, cols_of(3)])
    resid = flat_in.astype(jnp.float32) + attn_out
    normed, norm_one_back = jax.vjp(lambda values: normalize(values, gain_one, shift_one), resid)
    normed_low = normed.astype(jnp.bfloat16)
    t_up = (product(normed_low, a_full[:, cols_of(4)]) * chosen).astype(jnp.bfloat16)
    pre_act = product(normed_low, wu_full) + against(t_up, ffb_full)
    cdf = 0.5 * (1.0 + lax.erf(pre_act * (0.5 ** 0.5)))
    act_low = (pre_act * cdf).astype(jnp.bfloat16)
    slope = cdf + pre_act * jnp.exp(-0.5 * pre_act * pre_act) * ((0.5 / math.pi) ** 0.5)
    act_low, slope = lax.optimization_barrier((act_low, slope))
    t_down = (product(act_low, ffa_full) * chosen).astype(jnp.bfloat16)
    down_out = product(act_low, wd_full) + against(t_down, b_full[:, cols_of(4)])
    final = normed + down_out
    result, norm_two_back = jax.vjp(lambda values: normalize(values, gain_two, shift_two), final)
    d_final = norm_two_back(cotangent.reshape(rows_all, model_width).astype(jnp.float32))[0]
    d_down = d_final.astype(jnp.bfloat16)
    dt_down = (product(d_down, b_full[:, cols_of(4)]) * chosen).astype(jnp.bfloat16)
    grad_b_down = over_rows(d_down, t_down)
    grad_ff_narrow = over_rows(act_low, dt_down)
    d_act = against(d_down, wd_full) + against(dt_down, ffa_full)
    d_pre = (d_act * slope).astype(jnp.bfloat16)
    dt_up = (product(d_pre, ffb_full) * chosen).astype(jnp.bfloat16)
    grad_ff_widen = over_rows(d_pre, t_up)
    grad_a_up = over_rows(normed_low, dt_up)
    d_normed = d_final + against(d_pre, wu_full) + against(dt_up, a_full[:, cols_of(4)])
    d_resid = norm_one_back(d_normed)[0]
    d_attn = d_resid.astype(jnp.bfloat16)
    dt_out = (product(d_attn, b_full[:, cols_of(3)]) * chosen).astype(jnp.bfloat16)
    grad_b_out = over_rows(d_attn, t_out)
    grad_a_out = over_rows(mixed_flat, dt_out)
    d_mixed = (against(d_attn, wo_full) + against(dt_out, a_full[:, cols_of(3)])).astype(jnp.bfloat16)
    d_parts = attn_bwd(query_low, key_low, value_low, weights_low, d_mixed, seq_local, length, 4)
    dt_parts = [
        (product(d_parts[slot], b_full[:, cols_of(slot)]) * chosen).astype(jnp.bfloat16) for slot in range(3)
    ]
    dt_qkv = jnp.concatenate(dt_parts, axis=1)
    grad_b_qkv = [over_rows(d_parts[slot], t_qkv[:, cols_of(slot)]) for slot in range(3)]
    grad_a_qkv = over_rows(flat_in, dt_qkv)
    d_input = d_resid + against(dt_qkv, a_full[:, : 3 * set_cols])
    for slot in range(3):
        d_input = d_input + against(d_parts[slot], wq_full[:, slot * model_width : (slot + 1) * model_width])
    rows_own, ff_own = model_width // grid.devices, ff_narrow.shape[0]
    late = reduce_scatter(
        grid, [grad_ff_narrow, grad_ff_widen, grad_a_out, grad_a_up, grad_b_out, grad_b_down],
        [(0, 0), (1, 0), (2, 0), (2, set_cols), (3, 0), (3, set_cols)],
        [(ff_own, set_cols), (ff_own, set_cols), (rows_own, 2 * set_cols), (rows_own, 2 * set_cols)], 1)
    early = reduce_scatter(
        grid, [grad_a_qkv] + grad_b_qkv, [(0, 0), (1, 0), (1, set_cols), (1, 2 * set_cols)],
        [(rows_own, 3 * set_cols), (rows_own, 3 * set_cols)], 2)
    return (
        result.reshape(seq_local, length, model_width).astype(jnp.bfloat16),
        d_input.reshape(seq_local, length, model_width).astype(jnp.bfloat16),
        jnp.concatenate([early[0], late[2]], axis=1),
        jnp.concatenate([early[1], late[3]], axis=1),
        late[0],
        late[1],
    )


LAG = 4


def local(sizes, tokens, cotangent, adapter_id, global_pos, w_qkv, w_out, w_up, w_down, norm_gain, norm_bias,
          narrow_in, widen_out, ff_narrow, ff_widen):
    grid = Grid(sizes)
    seq_local, length, width = tokens.shape
    rows = seq_local * length
    own = w_qkv.shape[0]
    fits = own % 16 == 0 and 128 % own == 0 and rows == 2 * length and w_up.shape[1] == 4 * rows and width == rows
    if not fits:
        return local_plain(sizes, tokens, cotangent, adapter_id, global_pos, w_qkv, w_out, w_up, w_down, norm_gain,
                           norm_bias, narrow_in, widen_out, ff_narrow, ff_widen)
    cols = SETS * R
    flat_in = tokens.reshape(rows, width)
    place = (lax.axis_index("dp") * grid.fsdp + lax.axis_index("fsdp")) % (128 // own)
    small = jnp.tile(jnp.concatenate([norm_gain, norm_bias], axis=1).T, (1, 128 // own))
    mine = lax.broadcasted_iota(jnp.int32, (1, 128), 1) // own == place
    small = jnp.where(mine, small, jnp.zeros((), BF))
    shards = (small, narrow_in, widen_out, w_qkv, w_out, w_up, ff_narrow, ff_widen, w_down)
    (g_small, g_ab, g_qkv, g_out, g_up, g_ff, g_dn, q, k, v, p, mix, h, f, yb, t, gb, sl, pick, norms) = forward(
        grid, flat_in, adapter_id, global_pos, shards, LAG, 0)
    ab, wo, ff = (flat2(a) for a in (g_ab, g_out, g_ff))
    wq = g_qkv.reshape(3, width, width)
    up = g_up.reshape(NCH, width, -1)
    dn = g_dn.reshape(NCH, w_up.shape[1], -1)
    res, dh, do, g_fa, g_fb, g_ao, g_au, g_bo, g_bd = middle(
        pick, norms, t, ab, f, cotangent.reshape(rows, width), h, yb, mix, wo, gb, sl, dn, up, ff)
    d_input, grad_a, grad_b, grad_fa, grad_fb = back(
        grid, q, k, v, p, do, flat_in, dh, ab, t, pick, wq, [g_fa, g_fb, g_ao, g_au, g_bo, g_bd], 1)
    d_input, grad_a, grad_b, grad_fa, grad_fb = settle([d_input, grad_a, grad_b, grad_fa, grad_fb])
    return res.reshape(tokens.shape), d_input.reshape(tokens.shape), grad_a, grad_b, grad_fa, grad_fb


def solution(mesh):
    rows = P(("dp", "fsdp"), None)
    cube = P(("dp", "fsdp"), None, None)
    in_specs = (cube, cube, P(("dp", "fsdp"))) + (rows,) * 11
    out_specs = (cube, cube) + (rows,) * 4
    return jax.shard_map(functools.partial(local, dict(mesh.shape)), mesh=mesh, in_specs=in_specs, out_specs=out_specs, check_vma=False)
```

```python
import functools, math
import jax
import jax.numpy as jnp
from jax import lax
from jax.experimental import pallas as pl
from jax.experimental.pallas import tpu as pltpu
from jax.sharding import PartitionSpec as P

MESH = pl.DeviceIdType.MESH


class Grid:
    def __init__(self, sizes):
        self.dp, self.fsdp = sizes["dp"], sizes["fsdp"]
        if (self.dp, self.fsdp) == (8, 4):
            self.dims = {"z": ("dp", 2, 4), "y": ("dp", 1, 2), "x": ("fsdp", 2, 2), "c": ("fsdp", 1, 2)}
        elif (self.dp, self.fsdp) == (64, 4):
            self.dims = {"z": ("dp", 8, 8), "y": ("dp", 2, 4), "x": ("fsdp", 1, 4), "c": ("dp", 1, 2)}
        else:
            self.dims = {"z": ("dp", 1, self.dp), "y": ("dp", 1, 1), "x": ("fsdp", self.fsdp, 1), "c": ("fsdp", 1, self.fsdp)}
        self.n = {k: v[2] for k, v in self.dims.items()}
        self.devices = self.dp * self.fsdp
        self.planes = self.devices // self.n["z"]

    def stride(self, k):
        axis, step, _ = self.dims[k]
        return step * (self.fsdp if axis == "dp" else 1)

    def here(self):
        idx = {"dp": lax.axis_index("dp"), "fsdp": lax.axis_index("fsdp")}
        return {k: (idx[axis] // step) % size for k, (axis, step, size) in self.dims.items()}

    def device(self, pos):
        out = {"dp": 0, "fsdp": 0}
        for k, (axis, step, _) in self.dims.items():
            out[axis] = out[axis] + pos[k] * step
        return out["dp"], out["fsdp"]

    def slot(self, y, x, c):
        return y * self.stride("y") + x * self.stride("x") + c * self.stride("c")


def barrier_with(grid, here, plane=False):
    barrier = pltpu.get_barrier_semaphore()
    count = 0
    for k in ("z", "y", "x", "c"):
        n = grid.n[k]
        for step in range(1, n):
            to = (here[k] + step) % n
            pl.semaphore_signal(barrier, inc=1, device_id=grid.device({**here, k: to}), device_id_type=MESH)
            count += 1
    for dy in range(1, grid.n["y"] if plane else 1):
        for dx in range(1, grid.n["x"]):
            to = {**here, "y": (here["y"] + dy) % grid.n["y"], "x": (here["x"] + dx) % grid.n["x"]}
            pl.semaphore_signal(barrier, inc=1, device_id=grid.device(to), device_id_type=MESH)
            count += 1
    pl.semaphore_wait(barrier, count)


class Gather:
    @staticmethod
    def parts(grid):
        return grid.n["z"] if grid.n["z"] <= 4 else 1

    @staticmethod
    def sem_total(grid):
        z, a, b, c = (grid.n[k] for k in ("z", "y", "x", "c"))
        k = Gather.parts(grid)
        return z + k * a + k * a * b + a * b

    def __init__(self, grid, here, src, out, send, recv, local):
        self.g, self.here, self.src, self.out = grid, here, src, out
        self.send, self.recv, self.local = send, recv, local
        self.k = Gather.parts(grid)
        self.nz, self.n2, self.n3 = grid.n["z"], grid.n["y"], grid.n["x"]
        self.base2 = self.nz
        self.base3 = self.base2 + self.k * self.n2
        self.base4 = self.base3 + self.k * self.n2 * self.n3
        self.sends = []
        self.first = here["c"] == 0
        self.p2 = jnp.where(self.first, here["y"], here["x"])
        self.p3 = jnp.where(self.first, here["x"], here["y"])

    def dev(self, z=None, p2=None, p3=None, c=None):
        h = self.here
        p2 = self.p2 if p2 is None else p2
        p3 = self.p3 if p3 is None else p3
        return self.g.device({
            "z": h["z"] if z is None else z,
            "y": jnp.where(self.first, p2, p3),
            "x": jnp.where(self.first, p3, p2),
            "c": h["c"] if c is None else c,
        })

    def m(self, p2, p3):
        return self.g.slot(jnp.where(self.first, p2, p3), jnp.where(self.first, p3, p2), self.here["c"])

    def part(self, i):
        return (self.here["z"] ^ i) if self.k == self.nz and self.nz & (self.nz - 1) == 0 else None

    def block(self, z, p2, p3):
        return self.out.at[:, self.m(p2, p3)] if z is None else self.out.at[z, self.m(p2, p3)]

    def copy(self, src, dst, sem, dev):
        return pltpu.make_async_remote_copy(src_ref=src, dst_ref=dst, send_sem=self.send.at[sem], recv_sem=self.recv.at[sem], device_id=dev, device_id_type=MESH)

    def pull(self, dst, sem):
        self.copy(dst, dst, sem, self.dev()).wait_recv()

    def sem2(self, z, p2):
        return self.base2 + (0 if z is None else z * self.n2) + p2

    def sem3(self, z, p2, p3):
        return self.base3 + ((0 if z is None else z * self.n2) + p2) * self.n3 + p3

    def to2(self, z, src=None):
        ref = self.block(z, self.p2, self.p3)
        return [self.copy(ref if src is None else src, ref, self.sem2(z, self.p2), self.dev(p2=(self.p2 + d) % self.n2)) for d in range(1, self.n2)]

    def to3(self, z, p2, src=None):
        ref = self.block(z, p2, self.p3)
        return [self.copy(ref if src is None else src, ref, self.sem3(z, p2, self.p3), self.dev(p3=(self.p3 + d) % self.n3)) for d in range(1, self.n3)]

    def to_core(self, p2, p3):
        if self.g.n["c"] == 1:
            return []
        ref = self.block(None, p2, p3)
        y, x = jnp.where(self.first, p2, p3), jnp.where(self.first, p3, p2)
        return [self.copy(ref, ref, self.base4 + y * self.n3 + x, self.dev(c=1 - self.here["c"]))]

    def line(self, i):
        z = self.here["z"]
        return z ^ i if self.nz & (self.nz - 1) == 0 else (z + i) % self.nz

    def own(self):
        return pltpu.make_async_copy(self.src, self.out.at[self.here["z"], self.m(self.p2, self.p3)], self.local)

    def along(self):
        z = self.here["z"]
        m0 = self.m(self.p2, self.p3)
        return [self.copy(self.src, self.out.at[z, m0], z, self.dev(z=self.line(i))) for i in range(1, self.nz)]

    def launch(self):
        for c in self.along():
            c.start()

    def begin(self):
        z = self.here["z"]
        return self.to3(z, self.p2, self.src) + self.to2(z, self.src) if self.part(0) is not None else []

    def wait_z(self, i):
        z = self.line(i)
        self.pull(self.out.at[z, self.m(self.p2, self.p3)], z)

    def after_z(self, i):
        return self.to2(self.part(i)) + self.to3(self.part(i), self.p2) if self.part(i) is not None else []

    def after_line(self):
        out = [] if self.part(0) is not None else self.to2(None) + self.to3(None, self.p2)
        return out + self.to_core(self.p2, self.p3)

    def wait2(self, i):
        z = self.part(i)
        for d in range(1, self.n2):
            q = (self.p2 + d) % self.n2
            self.pull(self.block(z, q, self.p3), self.sem2(z, q))

    def after2(self, i):
        return [c for d in range(1, self.n2) for c in self.to3(self.part(i), (self.p2 + d) % self.n2)]

    def after_all2(self):
        return [c for d in range(1, self.n2) for c in self.to_core((self.p2 + d) % self.n2, self.p3)]

    def wait3(self, j):
        p2 = (self.p2 + j) % self.n2
        for d in range(1, self.n3):
            q = (self.p3 + d) % self.n3
            for i in range(self.k):
                z = self.part(i)
                self.pull(self.block(z, p2, q), self.sem3(z, p2, q))

    def after3(self, j):
        p2 = (self.p2 + j) % self.n2
        return [c for d in range(1, self.n3) for c in self.to_core(p2, (self.p3 + d) % self.n3)]

    def pairs(self):
        part = functools.partial
        out = [(lambda: self.own().start(), self.begin)]
        out += [(part(self.wait_z, i), part(self.after_z, i)) for i in range(1, self.nz)]
        out += [(lambda: self.own().wait(), self.after_line)]
        out += [(part(self.wait2, i), part(self.after2, i)) for i in range(self.k)]
        out += [(lambda: None, self.after_all2)]
        out += [(part(self.wait3, j), part(self.after3, j)) for j in range(self.n2)]
        return out

    def steps(self):
        def act(wait, copies):
            wait()
            for c in copies():
                c.start()
        return [functools.partial(act, *p) for p in self.pairs()] + [self.arrived]

    def arrived(self):
        if self.g.n["c"] > 1:
            for y in range(self.n2):
                for x in range(self.n3):
                    self.pull(self.out.at[:, self.g.slot(y, x, 1 - self.here["c"])], self.base4 + y * self.n3 + x)

    def finish(self):
        for c in self.along():
            c.wait_send()
        for _, copies in self.pairs():
            for c in copies():
                c.wait_send()


def skewed(all_steps, lag):
    count = max(len(s) for s in all_steps)
    out = []
    for slot in range(count + lag * (len(all_steps) - 1)):
        for i, steps in enumerate(all_steps):
            k = slot - lag * i
            if 0 <= k < len(steps):
                out.append((i, steps[k]))
    return out


def run_skewed(all_steps, lag):
    for _, step in skewed(all_steps, lag):
        step()

SETS = 8
R = 16


def normalize(values, gain, shift):
    center = values - jnp.mean(values, axis=-1, keepdims=True)
    spread = jnp.mean(center * center, axis=-1, keepdims=True)
    return center * lax.rsqrt(spread + 1e-12) * gain + shift


def against(left, right):
    return lax.dot_general(
        left, right, (((1,), (1,)), ((), ())), preferred_element_type=jnp.float32
    )


def over_rows(left, right):
    return lax.dot_general(
        left, right, (((0,), (0,)), ((), ())), preferred_element_type=jnp.float32
    )


def product(left, right):
    return jnp.dot(left, right, preferred_element_type=jnp.float32)


def gelu_exact(values):
    return jax.nn.gelu(values, approximate=False)


def gather_kernel(grid, count, lag, first, *refs):
    srcs, outs = refs[:count], refs[count:2*count]
    send, recv, local = refs[2*count:]
    here = grid.here()
    barrier_with(grid, here)
    gs = [Gather(grid, here, srcs[i], outs[i], send.at[i], recv.at[i], local.at[i]) for i in range(count)]
    for g in gs:
        g.launch()
    steps = [g.steps() for g in gs]
    if first:
        for s in steps:
            s.pop(0)()
    run_skewed(steps, lag)
    for g in gs:
        g.finish()

def all_gather(grid, arrays, cid=0, lag=1, first=True):
    count = len(arrays)
    total = Gather.sem_total(grid)
    out_shape = [jax.ShapeDtypeStruct((grid.n["z"], grid.planes) + a.shape, a.dtype) for a in arrays]
    return pl.pallas_call(
        functools.partial(gather_kernel, grid, count, lag, first),
        out_shape=out_shape,
        in_specs=[pl.BlockSpec(memory_space=pltpu.VMEM)] * count,
        out_specs=[pl.BlockSpec(memory_space=pl.ANY)] * count,
        scratch_shapes=[pltpu.SemaphoreType.DMA((count, total)), pltpu.SemaphoreType.DMA((count, total)), pltpu.SemaphoreType.DMA((count,))],
        compiler_params=pltpu.CompilerParams(collective_id=cid, has_side_effects=True, vmem_limit_bytes=8*2**20),
        name="gather",
    )(*arrays)


class Scatter:
    @staticmethod
    def sem_total(grid):
        return grid.n["x"] * grid.n["y"] + grid.n["z"]

    @staticmethod
    def scratch(grid, shape, dtype=jnp.bfloat16):
        rows, cols = shape
        z, y, x = grid.n["z"], grid.n["y"], grid.n["x"]
        out = []
        if grid.n["c"] > 1:
            out += [pltpu.VMEM((y * x, z, rows, cols), dtype)] * 2
        out += [pltpu.VMEM((max(y * x - 1, 1), z, rows, cols), dtype)] * 2
        out += [pltpu.VMEM((z, rows, cols), dtype), pltpu.VMEM((max(z - 1, 1), rows, cols), dtype)]
        out += [pltpu.VMEM((y * x, z, rows, cols), jnp.float32)]
        return out

    def __init__(self, grid, here, src, put, bufs, send, recv):
        self.g, self.here, self.src, self.put, self.send, self.recv = grid, here, src, put, send, recv
        bufs = list(bufs)
        self.two = grid.n["c"] > 1
        self.s1, self.r1 = (bufs.pop(0), bufs.pop(0)) if self.two else (None, None)
        self.s2, self.r2, self.s4, self.r4, self.acc = bufs
        self.nz, self.n2, self.n3 = grid.n["z"], grid.n["y"], grid.n["x"]
        self.first = here["c"] == 0
        self.p2 = jnp.where(self.first, here["y"], here["x"])
        self.p3 = jnp.where(self.first, here["x"], here["y"])
        self.sends, self.pulls = [], []

    def dev(self, z=None, p2=None, p3=None, c=None):
        h = self.here
        p2 = self.p2 if p2 is None else p2
        p3 = self.p3 if p3 is None else p3
        return self.g.device({
            "z": h["z"] if z is None else z,
            "y": jnp.where(self.first, p2, p3),
            "x": jnp.where(self.first, p3, p2),
            "c": h["c"] if c is None else c,
        })

    def flat(self, p2, p3):
        return jnp.where(self.first, p2 * self.n3 + p3, p3 * self.n3 + p2)

    def push(self, make):
        make().start()
        self.sends.append(make)

    def copy(self, src, dst, sem, dev):
        return pltpu.make_async_remote_copy(src_ref=src, dst_ref=dst, send_sem=self.send.at[sem], recv_sem=self.recv.at[sem], device_id=dev, device_id_type=MESH)

    def far(self, p, d, n):
        return (p + d) % n

    def pull(self, dst, sem):
        pltpu.make_async_remote_copy(src_ref=dst, dst_ref=dst, send_sem=self.send.at[sem], recv_sem=self.recv.at[sem], device_id=self.dev(), device_id_type=MESH).wait_recv()

    def begin(self):
        c = self.here["c"]
        for y in range(self.n2):
            for x in range(self.n3):
                i = y * self.n3 + x
                if self.two:
                    self.s1[i] = self.src[:, self.g.slot(y, x, 1 - c)].astype(self.s1.dtype)
        if self.two:
            self.push(lambda: self.copy(self.s1, self.r1, 0, self.dev(c=1 - self.here["c"])))

    def step1(self):
        c = self.here["c"]
        if self.two:
            self.pull(self.r1, 0)
        for y in range(self.n2):
            for x in range(self.n3):
                i = y * self.n3 + x
                part = self.src[:, self.g.slot(y, x, c)]
                self.acc[i] = part + self.r1[i].astype(jnp.float32) if self.two else part
        for d2, d3 in self.others():
            i = d2 * self.n3 + d3 - 1
            self.s2[i] = self.acc[self.flat(self.far(self.p2, d2, self.n2), self.far(self.p3, d3, self.n3))].astype(self.s2.dtype)
            self.push(lambda d2=d2, d3=d3, i=i: self.copy(self.s2.at[i], self.r2.at[i], 1 + i, self.dev(p2=self.far(self.p2, d2, self.n2), p3=self.far(self.p3, d3, self.n3))))

    def others(self):
        return [(d2, d3) for d2 in range(self.n2) for d3 in range(self.n3) if d2 + d3 > 0]

    def step2(self):
        i = self.flat(self.p2, self.p3)
        total = self.acc[i]
        for d2, d3 in self.others():
            k = d2 * self.n3 + d3 - 1
            self.pull(self.r2.at[k], 1 + k)
            total = total + self.r2[k].astype(jnp.float32)
        self.acc[i] = total
        base = self.n2 * self.n3
        self.s4[...] = total.astype(self.s4.dtype)
        for d in range(1, self.nz):
            self.push(lambda d=d: self.copy(self.s4.at[self.far(self.here["z"], d, self.nz)], self.r4.at[d - 1], base + d, self.dev(z=self.far(self.here["z"], d, self.nz))))

    def step3(self):
        base = self.n2 * self.n3
        total = self.acc[self.flat(self.p2, self.p3), self.here["z"]]
        for d in range(1, self.nz):
            self.pull(self.r4.at[d - 1], base + d)
            total = total + self.r4[d - 1].astype(jnp.float32)
        self.put(total)

    def steps(self):
        return [self.begin, self.step1, self.step2, self.step3]

    def finish(self):
        for make in self.sends:
            make().wait_send()


def scatter_kernel(grid, places, nout, *refs):
    count = len(places)
    srcs, outs = refs[:count], refs[count:count + nout]
    rest = refs[count + nout:]
    send, recv = rest[:2]
    rest = rest[2:]
    per = len(rest) // count
    here = grid.here()
    barrier_with(grid, here, True)
    units = []
    for i, (o, col) in enumerate(places):
        def put(total, o=o, col=col):
            outs[o][:, col:col + total.shape[1]] = total
        units.append(Scatter(grid, here, srcs[i], put, rest[i * per:(i + 1) * per], send.at[i], recv.at[i]))
    run_skewed([u.steps() for u in units], 1)
    for u in units:
        u.finish()


def reduce_scatter(grid, arrays, places, outs, cid):
    count = len(arrays)
    views = [a.reshape(grid.n["z"], grid.planes, a.shape[0] // grid.devices, a.shape[1]) for a in arrays]
    total = Scatter.sem_total(grid)
    scratch = [pltpu.SemaphoreType.DMA((count, total)), pltpu.SemaphoreType.DMA((count, total))]
    for v in views:
        scratch += Scatter.scratch(grid, v.shape[2:])
    return pl.pallas_call(
        functools.partial(scatter_kernel, grid, places, len(outs)),
        out_shape=[jax.ShapeDtypeStruct(o, jnp.float32) for o in outs],
        in_specs=[pl.BlockSpec(memory_space=pltpu.VMEM)] * count,
        out_specs=[pl.BlockSpec(memory_space=pltpu.VMEM)] * len(outs),
        scratch_shapes=scratch,
        compiler_params=pltpu.CompilerParams(collective_id=cid, has_side_effects=True, vmem_limit_bytes=60 * 2**20),
        name="scatter",
    )(*views)


HD=64
def dotf(a,b,ca,cb):
    return lax.dot_general(a,b,(((ca,),(cb,)),((),())),preferred_element_type=jnp.float32)

def set_bias(bias, row, col, half):
    n=bias.shape[0]
    i=lax.broadcasted_iota(jnp.int32,(n,n),0); j=lax.broadcasted_iota(jnp.int32,(n,n),1)
    near=jnp.abs(i-j)<=half
    ok=near|(jnp.broadcast_to(row,(n,n))>0)|(jnp.broadcast_to(col,(n,n))>0)
    bias[...]=jnp.where(ok,0.0,-1e30)

def fwd_kernel(half,row_ref,col_ref,q_ref,k_ref,v_ref,o_ref,p_ref,bias):
    @pl.when(pl.program_id(1)==0)
    def _(): set_bias(bias,row_ref[0],col_ref[0],half)
    width=q_ref.shape[1]
    q=q_ref[...]; k=k_ref[...]
    vt=v_ref[...].T
    outs=[]
    for h in range(width//HD):
        c=(h*HD)//128*128
        lane=lax.broadcasted_iota(jnp.int32,(1,128),1)//HD
        keep=(lane==(h*HD-c)//HD)
        kh=jnp.where(keep,k[:,c:c+128],jnp.zeros((),k.dtype))*jnp.asarray(HD**-0.5,k.dtype)
        s=dotf(kh,q[:,c:c+128],1,1)+bias[...]
        top=jnp.max(s,axis=0,keepdims=True)
        e=jnp.exp(s-top)
        tot=jnp.sum(e,axis=0,keepdims=True)
        p=(e*(1.0/tot)).astype(jnp.bfloat16)
        p_ref[h]=p
        outs.append(dotf(vt[h*HD:(h+1)*HD],p,1,0))
    o_ref[...]=jnp.concatenate(outs,axis=0).T.astype(o_ref.dtype)

def attn_fwd(q,k,v,row,col,seqs,length,per=2):
    rows,width=q.shape; heads=width//HD
    w=per*HD
    spec=pl.BlockSpec((length,w),lambda s,h:(s,h))
    return pl.pallas_call(functools.partial(fwd_kernel,256),grid=(seqs,heads//per),
      in_specs=[pl.BlockSpec((1,1,length),lambda s,h:(s,0,0)),pl.BlockSpec((1,length,1),lambda s,h:(s,0,0)),spec,spec,spec],
      out_specs=[spec,pl.BlockSpec((None,per,length,length),lambda s,h:(s,h,0,0))],
      out_shape=[jax.ShapeDtypeStruct(q.shape,q.dtype),jax.ShapeDtypeStruct((seqs,heads,length,length),q.dtype)],
      scratch_shapes=[pltpu.VMEM((length,length),jnp.float32)],
      compiler_params=pltpu.CompilerParams(vmem_limit_bytes=48*2**20),name="attend")(row,col,q,k,v)

def bwd_kernel(q_ref,k_ref,v_ref,p_ref,d_ref,dq_ref,dk_ref,dv_ref):
    width=q_ref.shape[1]
    q=q_ref[...]; k=k_ref[...]; v=v_ref[...]; d=d_ref[...]
    scale=jnp.asarray(HD**-0.5,q.dtype)
    kt=(k*scale).T
    qs=q*scale
    dqs=[]; dks=[]; dvs=[]
    lane=lax.broadcasted_iota(jnp.int32,(1,128),1)//HD
    for h in range(width//HD):
        c=(h*HD)//128*128
        keep=(lane==(h*HD-c)//HD)
        vh=jnp.where(keep,v[:,c:c+128],jnp.zeros((),v.dtype))
        pb=p_ref[h]
        p=pb.astype(jnp.float32)
        dp=dotf(vh,d[:,c:c+128],1,1)
        t=p*dp
        inner=jnp.sum(t,axis=0,keepdims=True)
        ds=(t-p*inner).astype(jnp.bfloat16)
        dqs.append(dotf(kt[h*HD:(h+1)*HD],ds,1,0))
        dks.append(dotf(ds,qs[:,c:c+128],1,0))
        dvs.append(dotf(pb,d[:,c:c+128],1,0))
    dq_ref[...]=jnp.concatenate(dqs,axis=0).T.astype(dq_ref.dtype)
    for g in range(width//128):
        keep=lane==0
        dk_ref[:,g*128:(g+1)*128]=jnp.where(keep,dks[2*g],dks[2*g+1]).astype(dk_ref.dtype)
        dv_ref[:,g*128:(g+1)*128]=jnp.where(keep,dvs[2*g],dvs[2*g+1]).astype(dv_ref.dtype)

def attn_bwd(q,k,v,p,d,seqs,length,per=2):
    rows,width=q.shape; heads=width//HD; w=per*HD
    spec=pl.BlockSpec((length,w),lambda s,h:(s,h))
    return pl.pallas_call(bwd_kernel,grid=(seqs,heads//per),
      in_specs=[spec,spec,spec,pl.BlockSpec((None,per,length,length),lambda s,h:(s,h,0,0)),spec],
      out_specs=[spec]*3,out_shape=[jax.ShapeDtypeStruct(q.shape,q.dtype)]*3,
      compiler_params=pltpu.CompilerParams(vmem_limit_bytes=48*2**20),name="attend_back")(q,k,v,p,d)


BF = jnp.bfloat16
F32 = jnp.float32

def flat2(v):
    return v.reshape(v.shape[0] * v.shape[1] * v.shape[2], v.shape[3])

def whole_rows(ref, c0, c1):
    return flat2(ref[:, :, :, c0:c1])

UNITS = ("small", "ab", "q", "k", "v", "out", "up0", "ff", "up1", "up2", "up3", "dn0", "dn1", "dn2", "dn3")
NCH = 4
PACE = (2, 4, 2, 2, 1, 1)

def forward_kernel(grid, lag, *refs):
    n_in = 3 + 9
    (x, ids, gpos, in_small, in_a, in_b, s_qkv, s_out, s_up, in_fa, in_fb, s_dn) = refs[:n_in]
    outs = refs[n_in:n_in + 20]
    (g_small, g_ab, g_qkv, g_out, g_up, g_ff, g_dn, o_q, o_k, o_v, o_p, o_mix, o_h, o_f, o_yb, o_t, o_gb, o_sl, o_pick, o_norms) = outs
    (b_small, b_ab, b_qkv, b_out, b_ff, b_w, v_q, v_k, v_v, stage, bias, v_mix, v_h, v_f, v_yb, v_t, v_gb, tacc,
     s_small, s_ab, s_ff, pick, row, col, v_norms, send, recv, local, lsem, osem, ssem) = refs[n_in + 20:]
    rows, width = x.shape
    length = bias.shape[0]
    seqs = rows // length
    cols = pick.shape[2]
    here = grid.here()
    s_small[...] = jnp.zeros_like(s_small)
    s_small[0:in_small.shape[0], :] = in_small[...]
    s_ab[:, 0:5 * cols] = in_a[...]
    s_ab[:, 5 * cols:10 * cols] = in_b[...]
    s_ff[:, 0:cols] = in_fa[...]
    s_ff[:, cols:2 * cols] = in_fb[...]
    for n in range(seqs):
        pick[n] = jnp.where(lax.broadcasted_iota(jnp.int32, (1, cols), 1) // R == ids[n], 1.0, 0.0)
        count = gpos.shape[1]
        same = jnp.broadcast_to(gpos[n:n + 1, :], (length, count)) == lax.broadcasted_iota(jnp.int32, (length, count), 0)
        found = jnp.max(jnp.where(same, 1.0, 0.0), axis=1, keepdims=True)
        col[n] = found
        row[n] = jnp.broadcast_to(found, (length, 128)).T[0:1]
    barrier_with(grid, here)
    spots = {"small": (s_small, g_small), "ab": (s_ab, g_ab), "out": (s_out, g_out), "ff": (s_ff, g_ff)}
    cw, dw = s_up.shape[1] // NCH, s_dn.shape[1] // NCH
    for j, n in enumerate("qkv"):
        spots[n] = (s_qkv.at[:, j * width:(j + 1) * width], g_qkv.at[j])
    for j in range(NCH):
        spots["up%d" % j] = (s_up.at[:, j * cw:(j + 1) * cw], g_up.at[j])
        spots["dn%d" % j] = (s_dn.at[:, j * dw:(j + 1) * dw], g_dn.at[j])
    units = [Gather(grid, here, *spots[n], send.at[i], recv.at[i], local.at[i]) for i, n in enumerate(UNITS)]
    order = skewed([u.steps() for u in units], lag)
    for u in units:
        u.launch()
    state = {"at": 0}
    last = {i: max(k for k, (j, _) in enumerate(order) if j == i) for i in range(len(units))}

    def pump(count):
        end = min(state["at"] + count, len(order))
        for k in range(state["at"], end):
            order[k][1]()
        state["at"] = end

    def need(name):
        pump(max(0, last[UNITS.index(name)] + 1 - state["at"]))

    def load(src, dst, k):
        return pltpu.make_async_copy(src, dst, lsem.at[k])

    need("ab")
    c_small, c_ab = load(g_small, b_small, 0), load(g_ab, b_ab, 1)
    c_small.start()
    c_ab.start()
    c_small.wait()
    c_ab.wait()

    step = 256
    blocks = rows // step

    def rows_at(r):
        return pl.ds(pl.multiple_of(r * step, step), step)

    def picked(r):
        return pick[(r * step) // length]

    def taking(count):
        base = state["at"]
        ends = [min(base + (n + 1) * count, len(order)) for n in range(blocks)]
        state["at"] = ends[-1]

        def hook(r):
            lo = base
            for n, hi in enumerate(ends):
                @pl.when(r == n)
                def _(lo=lo, hi=hi):
                    for k in range(lo, hi):
                        order[k][1]()
                lo = hi
        return hook

    for slot, dst in enumerate((v_q, v_k, v_v)):
        need("qkv"[slot])
        c_w = load(g_qkv.at[slot], b_qkv.at[slot], 2)
        c_w.start()
        c_w.wait()
        hook = taking(PACE[0])

        @pl.loop(0, blocks)
        def _(r, slot=slot, dst=dst, hook=hook):
            at = rows_at(r)
            xa = x[at, :]
            t = (jnp.dot(xa, whole_rows(b_ab, slot * cols, (slot + 1) * cols), preferred_element_type=F32) * picked(r)).astype(BF)
            v_t[at, slot * cols:(slot + 1) * cols] = t
            acc = jnp.dot(xa, flat2(b_qkv[slot]), preferred_element_type=F32)
            acc = acc + dotf(t, whole_rows(b_ab, (5 + slot) * cols, (6 + slot) * cols), 1, 1)
            dst[at, :] = acc.astype(BF)
            hook(r)
    saves = [pltpu.make_async_copy(v_q, o_q, osem.at[0]), pltpu.make_async_copy(v_k, o_k, osem.at[1]), pltpu.make_async_copy(v_v, o_v, osem.at[2])]
    for c in saves:
        c.start()

    per = 4
    groups = width // (per * HD)
    total = seqs * groups
    chunks = []
    base = state["at"]
    share = PACE[1]

    def save_p(i, slot):
        return pltpu.make_async_copy(stage.at[slot], o_p.at[i], ssem.at[slot])

    def attend(i, carry):
        seq, hp = i // groups, i % groups
        @pl.when(hp == 0)
        def _():
            set_bias(bias, row[seq], col[seq], length // 2)
        slot = i % 2
        @pl.when(i >= 2)
        def _():
            save_p(i - 2, slot).wait()
        at = pl.ds(pl.multiple_of(seq * length, length), length)
        q = v_q[at, pl.ds(pl.multiple_of(hp * per * HD, per * HD), per * HD)]
        k = v_k[at, pl.ds(pl.multiple_of(hp * per * HD, per * HD), per * HD)]
        vt = v_v[at, pl.ds(pl.multiple_of(hp * per * HD, per * HD), per * HD)].T
        got = []
        lane = lax.broadcasted_iota(jnp.int32, (1, 128), 1) // HD
        for h in range(per):
            c = (h * HD) // 128 * 128
            kh = jnp.where(lane == (h * HD - c) // HD, k[:, c:c + 128], jnp.zeros((), BF)) * jnp.asarray(HD ** -0.5, BF)
            s = dotf(kh, q[:, c:c + 128], 1, 1) + bias[...]
            e = jnp.exp(s - jnp.max(s, axis=0, keepdims=True))
            p = (e * (1.0 / jnp.sum(e, axis=0, keepdims=True))).astype(BF)
            stage[slot, (h // 2) * length:(h // 2 + 1) * length, (h % 2) * length:(h % 2 + 1) * length] = p
            got.append(dotf(vt[h * HD:(h + 1) * HD], p, 1, 0))
        v_mix[at, pl.ds(pl.multiple_of(hp * per * HD, per * HD), per * HD)] = jnp.concatenate(got, axis=0).T.astype(BF)
        save_p(i, slot).start()
        for n in range(total):
            lo, hi = base + n * share, base + (n + 1) * share
            @pl.when(i == n)
            def _():
                for k2 in range(lo, hi):
                    order[k2][1]()
        return carry

    lax.fori_loop(0, total, attend, 0)
    state["at"] = base + share * total
    save_mix = pltpu.make_async_copy(v_mix, o_mix, osem.at[3])
    save_mix.start()

    need("out")
    c_out = load(g_out, b_out, 3)
    c_out.start()
    per_group = grid.devices // (width // 128)
    small = b_small[...].reshape(width // 128, per_group, 16, 128).astype(F32).sum(axis=1)
    norms = jnp.concatenate([small[g] for g in range(width // 128)], axis=1)
    gain, shift = norms[0:1], norms[2:3]
    v_norms[...] = norms
    save_norms = pltpu.make_async_copy(v_norms, o_norms, osem.at[9])
    save_norms.start()
    save_pick = pltpu.make_async_copy(pick, o_pick, osem.at[10])
    save_pick.start()
    c_out.wait()
    hook_out = taking(PACE[2])

    @pl.loop(0, blocks)
    def _(r):
        at = rows_at(r)
        oa = v_mix[at, :]
        t = (jnp.dot(oa, whole_rows(b_ab, 3 * cols, 4 * cols), preferred_element_type=F32) * picked(r)).astype(BF)
        v_t[at, 3 * cols:4 * cols] = t
        acc = jnp.dot(oa, whole_rows(b_out, 0, width), preferred_element_type=F32)
        acc = acc + dotf(t, whole_rows(b_ab, 8 * cols, 9 * cols), 1, 1)
        h = x[at, :].astype(F32) + acc
        v_h[at, :] = h
        center = h - jnp.mean(h, axis=1, keepdims=True)
        spread = jnp.mean(center * center, axis=1, keepdims=True)
        y = center * lax.rsqrt(spread + 1e-12) * gain + shift
        v_f[at, :] = y
        yb = y.astype(BF)
        v_yb[at, :] = yb
        v_t[at, 4 * cols:5 * cols] = (jnp.dot(yb, whole_rows(b_ab, 4 * cols, 5 * cols), preferred_element_type=F32) * picked(r)).astype(BF)
        hook_out(r)

    saves2 = [pltpu.make_async_copy(v_h, o_h, osem.at[4]), pltpu.make_async_copy(v_yb, o_yb, osem.at[5])]
    for c in saves2:
        c.start()

    def save_s(j, slot):
        return pltpu.make_async_copy(stage.at[slot], o_sl.at[j], ssem.at[slot])

    save_p(total - 2, 0).wait()
    save_p(total - 1, 1).wait()

    def load_up(j, slot):
        return load(g_up.at[j], b_w.at[slot], 4 + slot)

    for j in range(NCH):
        need("up%d" % j)
        if j == 0:
            load_up(0, 0).start()
            need("ff")
            c_ff = load(g_ff, b_ff, 6)
            c_ff.start()
            c_ff.wait()
        else:
            load_up(j, j % 2).start()
        pump(3)
        load_up(j, j % 2).wait()
        if j >= 2:
            save_s(j - 2, j % 2).wait()
        hook = taking(PACE[3])

        @pl.loop(0, blocks)
        def _(r, j=j, hook=hook):
            at = rows_at(r)
            u = jnp.dot(v_yb[at, :], whole_rows(b_w.at[j % 2], 0, cw), preferred_element_type=F32)
            wide = flat2(b_ff[:, :, :, cols:2 * cols])[j * cw:(j + 1) * cw]
            u = u + dotf(v_t[at, 4 * cols:5 * cols], wide, 1, 1)
            cdf = 0.5 * (1.0 + lax.erf(u * (0.5 ** 0.5)))
            gb = (u * cdf).astype(BF)
            v_gb[at, j * cw:(j + 1) * cw] = gb
            stage[j % 2, at, :] = (cdf + u * jnp.exp(-0.5 * u * u) * ((0.5 / math.pi) ** 0.5)).astype(BF)
            hook(r)

        save_s(j, j % 2).start()
    hook_ff = taking(PACE[4])

    @pl.loop(0, blocks)
    def _(r):
        at = rows_at(r)
        acc = jnp.dot(v_gb[at, :], flat2(b_ff[:, :, :, 0:cols]), preferred_element_type=F32)
        v_t[at, 5 * cols:6 * cols] = (acc * picked(r)).astype(BF)
        hook_ff(r)

    save_gb = pltpu.make_async_copy(v_gb, o_gb, osem.at[6])
    save_gb.start()
    save_t = pltpu.make_async_copy(v_t, o_t, osem.at[7])
    save_t.start()

    for j in range(NCH):
        need("dn%d" % j)
        slot = j % 2
        view = b_w.at[slot]
        c_dn = load(g_dn.at[j], tacc.at[slot], 7)
        c_dn.start()
        pump(3)
        c_dn.wait()
        hook = taking(PACE[5])

        @pl.loop(0, blocks)
        def _(r, j=j, slot=slot, hook=hook):
            at = rows_at(r)
            acc = jnp.dot(v_gb[at, :], flat2(tacc[slot]), preferred_element_type=F32)
            wide = whole_rows(b_ab, 9 * cols, 10 * cols)[j * dw:(j + 1) * dw]
            acc = acc + dotf(v_t[at, 5 * cols:6 * cols], wide, 1, 1)
            v_f[at, j * dw:(j + 1) * dw] = v_f[at, j * dw:(j + 1) * dw] + acc
            hook(r)

        saves2.append(pltpu.make_async_copy(v_f.at[:, j * dw:(j + 1) * dw], o_f.at[:, j * dw:(j + 1) * dw], osem.at[11 + j]))
        saves2[-1].start()

    pump(len(order))
    for u in units:
        u.finish()
    save_s(NCH - 2, 0).wait()
    save_s(NCH - 1, 1).wait()
    for c in saves + saves2 + [save_mix, save_gb, save_t, save_norms, save_pick]:
        c.wait()


def forward(grid, x, ids, gpos, shards, lag, cid):
    rows, width = x.shape
    seqs = ids.shape[0]
    length = rows // seqs
    in_small, in_a, in_b, s_qkv, s_out, s_up, in_fa, in_fb, s_dn = shards
    cols = in_fa.shape[1]
    z, m = grid.n["z"], grid.planes
    S = jax.ShapeDtypeStruct
    s_small, s_ab, s_ff = S((16, 128), BF), S((in_a.shape[0], 10 * cols), BF), S((in_fa.shape[0], 2 * cols), BF)
    cw, dw = s_up.shape[1] // NCH, s_dn.shape[1] // NCH
    total = Gather.sem_total(grid)
    nu = len(UNITS)
    def g(a, c=None, lead=()):
        return jax.ShapeDtypeStruct(lead + (z, m, a.shape[0], a.shape[1] if c is None else c), BF)
    out_shape = [g(s_small), g(s_ab), g(s_qkv, width, (3,)), g(s_out), g(s_up, cw, (NCH,)), g(s_ff), g(s_dn, dw, (NCH,)),
        S(x.shape, BF), S(x.shape, BF), S(x.shape, BF), S((seqs * width // (4 * HD), 2 * length, 2 * length), BF),
        S(x.shape, BF), S(x.shape, F32), S(x.shape, F32), S(x.shape, BF), S((rows, 6 * cols), BF), S((rows, s_up.shape[1]), BF), S((NCH, rows, cw), BF),
        S((seqs, 1, cols), F32), S((16, width), F32)]
    V = pltpu.VMEM
    scratch = [V((z, m) + s_small.shape, BF), V((z, m) + s_ab.shape, BF), V((3, z, m, s_qkv.shape[0], width), BF), V((z, m) + s_out.shape, BF), V((z, m) + s_ff.shape, BF),
        V((2, z, m, s_up.shape[0], cw), BF),
        V(x.shape, BF), V(x.shape, BF), V(x.shape, BF), V((2, 2 * length, 2 * length), BF), V((length, length), F32), V(x.shape, BF), V(x.shape, F32), V(x.shape, F32), V(x.shape, BF),
        V((rows, 6 * cols), BF), V((rows, s_up.shape[1]), BF), V((2, z, m, s_dn.shape[0], dw), BF),
        V(s_small.shape, BF), V(s_ab.shape, BF), V(s_ff.shape, BF), V((seqs, 1, cols), F32), V((seqs, 1, length), F32), V((seqs, length, 1), F32), V((16, width), F32),
        pltpu.SemaphoreType.DMA((nu, total)), pltpu.SemaphoreType.DMA((nu, total)), pltpu.SemaphoreType.DMA((nu,)), pltpu.SemaphoreType.DMA((8,)), pltpu.SemaphoreType.DMA((11 + NCH,)), pltpu.SemaphoreType.DMA((2,))]
    return pl.pallas_call(
        functools.partial(forward_kernel, grid, lag),
        out_shape=out_shape,
        in_specs=[pl.BlockSpec(memory_space=pltpu.VMEM), pl.BlockSpec(memory_space=pltpu.SMEM)] + [pl.BlockSpec(memory_space=pltpu.VMEM)] * 10,
        out_specs=[pl.BlockSpec(memory_space=pl.ANY)] * 20,
        scratch_shapes=scratch,
        compiler_params=pltpu.CompilerParams(collective_id=cid, has_side_effects=True, vmem_limit_bytes=67043328),
        name="forward",
    )(x, ids, gpos, *shards)


def tdot(a, b):
    return lax.dot_general(a, b, (((0,), (0,)), ((), ())), preferred_element_type=F32)

def norm_parts(z):
    center = z - jnp.mean(z, axis=1, keepdims=True)
    inv = lax.rsqrt(jnp.mean(center * center, axis=1, keepdims=True) + 1e-12)
    return center * inv, inv

def norm_back(hat, inv, g):
    return inv * (g - jnp.mean(g, axis=1, keepdims=True) - hat * jnp.mean(g * hat, axis=1, keepdims=True))

def middle_kernel(pick, norms, t, ab, f, cot, h, yb, mix, wo, gb, sl, wd, wu, ff,
                  o_res, o_dh, o_do, g_fa, g_fb, g_ao, g_au, g_bo, g_bd,
                  v_f, v_cot, v_res, v_de, v_dy, v_yb, v_mix, v_wo, v_du, tdn, tup, tout, acc, sem, osem):
    j = pl.program_id(0)
    last = pl.num_programs(0) - 1
    rows, width = v_f.shape
    cols = pick.shape[2]
    step = 256
    blocks = rows // step
    length = rows // pick.shape[0]

    def rows_at(r):
        return pl.ds(pl.multiple_of(r * step, step), step)

    def picked(r):
        return pick[(r * step) // length]

    def slot(i):
        return ab[:, i * cols:(i + 1) * cols]

    loads = [pltpu.make_async_copy(f, v_f, sem.at[0]), pltpu.make_async_copy(cot, v_cot, sem.at[1]),
             pltpu.make_async_copy(h, v_f, sem.at[2]), pltpu.make_async_copy(yb, v_yb, sem.at[3]),
             pltpu.make_async_copy(mix, v_mix, sem.at[4]), pltpu.make_async_copy(wo, v_wo, sem.at[5])]
    save_res = pltpu.make_async_copy(v_res, o_res, osem.at[0])
    gain_one, gain_two, shift_two = norms[0:1, :], norms[1:2, :], norms[3:4, :]

    @pl.when(j == 0)
    def _():
        loads[0].start()
        loads[1].start()
        loads[0].wait()
        loads[1].wait()

        @pl.loop(0, blocks)
        def _(r):
            at = rows_at(r)
            hat, inv = norm_parts(v_f[at, :])
            v_res[at, :] = (hat * gain_two + shift_two).astype(BF)
            df = norm_back(hat, inv, v_cot[at, :].astype(F32) * gain_two)
            v_dy[at, :] = df
            de = df.astype(BF)
            v_de[at, :] = de
            tdn[at, :] = (jnp.dot(de, slot(9), preferred_element_type=F32) * picked(r)).astype(BF)

        save_res.start()
        for c in loads[2:]:
            c.start()
        g_bd[...] = tdot(v_de[...], t[:, 5 * cols:6 * cols])
        acc[...] = jnp.zeros_like(acc)

    half = 512

    @pl.loop(0, rows // half)
    def _(r):
        at = pl.ds(pl.multiple_of(r * half, half), half)
        dg = dotf(tdn[at, :], ff[:, 0:cols], 1, 1)
        for c in range(NCH):
            w = wd.shape[2]
            dg = dg + dotf(v_de[at, c * w:(c + 1) * w], wd[c], 1, 1)
        du = (dg * sl[at, :].astype(F32)).astype(BF)
        v_du[at, :] = du
        v_dy[at, :] = v_dy[at, :] + dotf(du, wu[...], 1, 1)
        acc[at, :] = acc[at, :] + jnp.dot(du, ff[:, cols:2 * cols], preferred_element_type=F32)

    g_fa[...] = tdot(gb[...], tdn[...])
    g_fb[...] = tdot(v_du[...], t[:, 4 * cols:5 * cols])

    @pl.when(j == last)
    def _():
        for c in loads[2:]:
            c.wait()
        save_res.wait()

        @pl.loop(0, blocks)
        def _(r):
            at = rows_at(r)
            dtu = (acc[at, :] * picked(r)).astype(BF)
            tup[at, :] = dtu
            dy = v_dy[at, :] + dotf(dtu, slot(4), 1, 1)
            hat, inv = norm_parts(v_f[at, :])
            dh = norm_back(hat, inv, dy * gain_one)
            v_dy[at, :] = dh
            da = dh.astype(BF)
            v_de[at, :] = da
            dto = (jnp.dot(da, slot(8), preferred_element_type=F32) * picked(r)).astype(BF)
            tout[at, :] = dto
            v_res[at, :] = (dotf(da, v_wo[...], 1, 1) + dotf(dto, slot(3), 1, 1)).astype(BF)

        save_dh = pltpu.make_async_copy(v_dy, o_dh, osem.at[1])
        save_do = pltpu.make_async_copy(v_res, o_do, osem.at[2])
        save_dh.start()
        save_do.start()
        g_au[...] = tdot(v_yb[...], tup[...])
        g_bo[...] = tdot(v_de[...], t[:, 3 * cols:4 * cols])
        g_ao[...] = tdot(v_mix[...], tout[...])
        save_dh.wait()
        save_do.wait()


def middle(pick, norms, t, ab, f, cot, h, yb, mix, wo, gb, sl, dn, up, ff):
    rows, width = f.shape
    cols = pick.shape[2]
    total = gb.shape[1]
    blk = 512
    per = sl.shape[2] // blk
    S, V = jax.ShapeDtypeStruct, pltpu.VMEM
    whole = pl.BlockSpec(memory_space=pltpu.VMEM)
    far = pl.BlockSpec(memory_space=pl.ANY)
    wcol = dn.shape[2]
    return pl.pallas_call(
        middle_kernel,
        grid=(total // blk,),
        in_specs=[whole] * 4 + [far] * 6 + [
            pl.BlockSpec((rows, blk), lambda j: (0, j)),
            pl.BlockSpec((None, rows, blk), lambda j: (j // per, 0, j % per)),
            pl.BlockSpec((NCH, blk, wcol), lambda j: (0, j, 0)),
            pl.BlockSpec((None, width, blk), lambda j: (j // per, 0, j % per)),
            pl.BlockSpec((blk, 2 * cols), lambda j: (j, 0)),
        ],
        out_specs=[far] * 3 + [pl.BlockSpec((blk, cols), lambda j: (j, 0))] * 2 + [pl.BlockSpec((width, cols), lambda j: (0, 0))] * 4,
        out_shape=[S(f.shape, BF), S(f.shape, F32), S(f.shape, BF), S((total, cols), F32), S((total, cols), F32)] + [S((width, cols), F32)] * 4,
        scratch_shapes=[V(f.shape, F32), V(f.shape, BF), V(f.shape, BF), V(f.shape, BF), V(f.shape, F32), V(f.shape, BF), V(f.shape, BF), V((width, width), BF),
                        V((rows, blk), BF), V((rows, cols), BF), V((rows, cols), BF), V((rows, cols), BF), V((rows, cols), F32),
                        pltpu.SemaphoreType.DMA((6,)), pltpu.SemaphoreType.DMA((3,))],
        compiler_params=pltpu.CompilerParams(vmem_limit_bytes=60 * 2**20),
        name="middle",
    )(pick, norms, t, ab, f, cot, h, yb, mix, wo, gb, sl, dn, up, ff)


def back_kernel(grid, *refs):
    q, k, v, p, d, h_x, dh, h_ab, h_t, pick, wq = refs[:11]
    h_late = refs[11:17]
    o_x, o_a, o_b, o_fa, o_fb = refs[17:22]
    (b_q, b_k, b_v, b_d, b_p, v_dq, v_dk, v_dv, v_wq, v_dt, b_dh, b_x, e_a, e_b, x, ab, t,
     lsem, wsem, hsem, xsem, send, recv) = refs[22:45]
    late, rest = refs[45:51], list(refs[51:])
    here = grid.here()
    rows, width = x.shape
    length, wide = b_q.shape[1], b_q.shape[2]
    groups = width // wide
    total = rows // length * groups
    cols = pick.shape[2]
    step = b_x.shape[1]
    blocks = rows // step
    nz = grid.n["z"]

    def put_in(out, col):
        def put(value):
            out[:, col:col + value.shape[1]] = value
        return put

    per = len(rest) // 8
    puts = [put_in(o_fa, 0), put_in(o_fb, 0), put_in(o_a, 3 * cols), put_in(o_a, 4 * cols), put_in(o_b, 3 * cols),
            put_in(o_b, 4 * cols), put_in(o_b, 0), put_in(o_a, 0)]
    units = [Scatter(grid, here, src, puts[i], rest[i * per:(i + 1) * per], send.at[i], recv.at[i])
             for i, src in enumerate(tuple(late) + (e_b, e_a))]
    steps = [u.steps() for u in units]

    def loads(i, slot):
        at = pl.ds(pl.multiple_of(i // groups * length, length), length)
        cs = pl.ds(pl.multiple_of(i % groups * wide, wide), wide)
        out = [pltpu.make_async_copy(a.at[at, cs], b.at[slot], lsem.at[slot, n]) for n, (a, b) in enumerate(((q, b_q), (k, b_k), (v, b_v), (d, b_d)))]
        return out + [pltpu.make_async_copy(p.at[i], b_p.at[slot], lsem.at[slot, 4])]

    def rows_at(r):
        return pl.ds(pl.multiple_of(r * step, step), step)

    def load_h(r, slot):
        return pltpu.make_async_copy(dh.at[rows_at(r), :], b_dh.at[slot], hsem.at[slot])

    def save_x(r, slot):
        return pltpu.make_async_copy(b_x.at[slot], o_x.at[rows_at(r), :], xsem.at[slot])

    load_t = pltpu.make_async_copy(h_t.at[:, 0:3 * cols], t, wsem.at[0])
    load_late = [pltpu.make_async_copy(a, b, wsem.at[4 + n]) for n, (a, b) in enumerate(zip(h_late, late))]
    load_rest = [pltpu.make_async_copy(h_ab, ab, wsem.at[1]), pltpu.make_async_copy(h_x, x, wsem.at[2]), pltpu.make_async_copy(wq, v_wq, wsem.at[3])]
    for c in loads(0, 0) + [load_t] + load_late + load_rest:
        c.start()
    barrier_with(grid, here, True)

    def first(n):
        load_late[n].wait()
        steps[n][0]()

    order = [s[n] for n in range(1, 4) for s in steps[:6]]
    share = -(-len(order) // total)
    turns = [order[n * share:(n + 1) * share] for n in range(total)]
    for n in range(6):
        first(n)
    scale = jnp.asarray(HD ** -0.5, BF)
    lane = lax.broadcasted_iota(jnp.int32, (1, 128), 1) // HD

    def attend(i, carry):
        slot = i % 2

        @pl.when(i + 1 < total)
        def _():
            for c in loads(i + 1, 1 - slot):
                c.start()

        for c in loads(i, slot):
            c.wait()

        qb, kb, vb, db = b_q[slot], b_k[slot], b_v[slot], b_d[slot]
        kt, qs = (kb * scale).T, qb * scale
        dqs, dks, dvs = [], [], []
        for h in range(wide // HD):
            c = (h * HD) // 128 * 128
            vh = jnp.where(lane == (h * HD - c) // HD, vb[:, c:c + 128], jnp.zeros((), BF))
            pb = b_p[slot, (h // 2) * length:(h // 2 + 1) * length, (h % 2) * length:(h % 2 + 1) * length]
            pf = pb.astype(F32)
            dp = dotf(vh, db[:, c:c + 128], 1, 1)
            w = pf * dp
            ds = (w - pf * jnp.sum(w, axis=0, keepdims=True)).astype(BF)
            dqs.append(dotf(kt[h * HD:(h + 1) * HD], ds, 1, 0))
            dks.append(dotf(ds, qs[:, c:c + 128], 1, 0))
            dvs.append(dotf(pb, db[:, c:c + 128], 1, 0))
        at = pl.ds(pl.multiple_of(i // groups * length, length), length)
        v_dq[at, pl.ds(pl.multiple_of(i % groups * wide, wide), wide)] = jnp.concatenate(dqs, axis=0).T.astype(BF)
        for g in range(wide // 128):
            cs = pl.ds(pl.multiple_of(i % groups * wide + g * 128, 128), 128)
            v_dk[at, cs] = jnp.where(lane == 0, dks[2 * g], dks[2 * g + 1]).astype(BF)
            v_dv[at, cs] = jnp.where(lane == 0, dvs[2 * g], dvs[2 * g + 1]).astype(BF)
        for n in range(total):
            @pl.when(i == n)
            def _(n=n):
                for act in turns[n]:
                    act()
        return carry

    lax.fori_loop(0, total, attend, 0)
    for c in [load_t] + load_rest[:2]:
        c.wait()
    load_h(0, 0).start()
    grads = (v_dq, v_dk, v_dv)
    part = width // nz

    @pl.loop(0, blocks)
    def _(r):
        at = rows_at(r)
        for s, g in enumerate(grads):
            v_dt[at, s * cols:(s + 1) * cols] = (jnp.dot(g[at, :], ab[:, (5 + s) * cols:(6 + s) * cols], preferred_element_type=F32) * pick[(r * step) // length]).astype(BF)

    @pl.loop(0, nz)
    def _(n):
        e_a[n] = tdot(x[:, pl.ds(pl.multiple_of(n * part, part), part)], v_dt[...]).reshape(e_a.shape[1:])

    steps[7][0]()

    @pl.loop(0, nz)
    def _(n):
        cs = pl.ds(pl.multiple_of(n * part, part), part)
        for s in range(3):
            e_b[n, :, :, s * cols:(s + 1) * cols] = tdot(grads[s][:, cs], t[:, s * cols:(s + 1) * cols]).reshape(e_b.shape[1:3] + (cols,))

    steps[6][0]()
    steps[7][1]()
    load_rest[2].wait()
    plan = [[] for _ in range(blocks)]
    for n, act in enumerate((steps[6][1], steps[7][2], steps[6][2], steps[7][3], steps[6][3])):
        plan[min(n, blocks - 1)].append(act)

    def finish(r, carry):
        slot = r % 2

        @pl.when(r + 1 < blocks)
        def _():
            load_h(r + 1, 1 - slot).start()

        load_h(r, slot).wait()

        @pl.when(r >= 2)
        def _():
            save_x(r - 2, slot).wait()

        at = rows_at(r)
        acc = b_dh[slot] + dotf(v_dt[at, :], ab[:, 0:3 * cols], 1, 1)
        for s, g in enumerate(grads):
            acc = acc + dotf(g[at, :], v_wq[s], 1, 1)
        b_x[slot] = acc.astype(BF)
        save_x(r, slot).start()
        for n in range(blocks):
            @pl.when(r == n)
            def _(n=n):
                for act in plan[n]:
                    act()
        return carry

    lax.fori_loop(0, blocks, finish, 0)
    for u in units:
        u.finish()
    for r in range(max(0, blocks - 2), blocks):
        save_x(r, r % 2).wait()


def back(grid, q, k, v, p, d, x, dh, ab, t, pick, wq, late, cid):
    rows, width = x.shape
    seqs, cols = pick.shape[0], pick.shape[2]
    length, wide, step = rows // seqs, 4 * HD, 256
    z, m = grid.n["z"], grid.planes
    views = [a.reshape(z, m, a.shape[0] // grid.devices, a.shape[1]) for a in late]
    own = width // grid.devices
    S, V = jax.ShapeDtypeStruct, pltpu.VMEM
    sems = Scatter.sem_total(grid)
    scratch = [V((2, length, wide), BF)] * 4 + [V((2,) + p.shape[1:], BF)] + [V(x.shape, BF)] * 3 + [
        V(wq.shape, BF), V((rows, 3 * cols), BF), V((2, step, width), F32), V((2, step, width), BF),
        V((z, m, own, 3 * cols), F32), V((z, m, own, 3 * cols), F32), V(x.shape, BF), V(ab.shape, BF), V((rows, 3 * cols), BF),
        pltpu.SemaphoreType.DMA((2, 5)), pltpu.SemaphoreType.DMA((4 + len(views),)), pltpu.SemaphoreType.DMA((2,)), pltpu.SemaphoreType.DMA((2,)),
        pltpu.SemaphoreType.DMA((8, sems)), pltpu.SemaphoreType.DMA((8, sems))] + [V(w.shape, F32) for w in views]
    for shape in [w.shape[2:] for w in views] + [(own, 3 * cols)] * 2:
        scratch += Scatter.scratch(grid, shape)
    far, near = pl.BlockSpec(memory_space=pl.ANY), pl.BlockSpec(memory_space=pltpu.VMEM)
    return pl.pallas_call(
        functools.partial(back_kernel, grid),
        out_shape=[S(x.shape, BF), S((own, 5 * cols), F32), S((own, 5 * cols), F32)] + [S(w.shape[2:], F32) for w in views[:2]],
        in_specs=[far] * 9 + [near, far] + [far] * 6,
        out_specs=[far] + [near] * 4,
        scratch_shapes=scratch,
        compiler_params=pltpu.CompilerParams(collective_id=cid, has_side_effects=True, vmem_limit_bytes=67043328),
        name="back",
    )(q, k, v, p, d, x, dh, ab, t, pick, wq, *views)


def settle_kernel(pieces, *refs):
    count = len(pieces)
    ins, outs, bufs = refs[:count], refs[count:2 * count], refs[2 * count:3 * count]
    isem, osem = refs[3 * count:]
    pairs = []
    for i, n in enumerate(pieces):
        each = ins[i].shape[0] // n
        for k in range(n):
            at = pl.ds(k * each, each)
            slot = len(pairs)
            pairs.append((pltpu.make_async_copy(ins[i].at[at], bufs[i].at[at], isem.at[slot]), pltpu.make_async_copy(bufs[i].at[at], outs[i].at[at], osem.at[slot])))
    for load, _ in pairs:
        load.start()
    for load, save in pairs:
        load.wait()
        save.start()
    for _, save in pairs:
        save.wait()


def settle(arrays):
    pieces = tuple(4 if a.size * a.dtype.itemsize >= 2**20 else 1 for a in arrays)
    far = pl.BlockSpec(memory_space=pl.ANY)
    return pl.pallas_call(
        functools.partial(settle_kernel, pieces),
        out_shape=[jax.ShapeDtypeStruct(a.shape, a.dtype) for a in arrays],
        in_specs=[far] * len(arrays), out_specs=[far] * len(arrays),
        scratch_shapes=[pltpu.VMEM(a.shape, a.dtype) for a in arrays] + [pltpu.SemaphoreType.DMA((sum(pieces),))] * 2,
        compiler_params=pltpu.CompilerParams(vmem_limit_bytes=60 * 2**20),
        name="settle",
    )(*arrays)


def local_plain(sizes, tokens, cotangent, adapter_id, global_pos, w_qkv, w_out, w_up, w_down, norm_gain, norm_bias,
          narrow_in, widen_out, ff_narrow, ff_widen):
    grid = Grid(sizes)
    small = jnp.concatenate([norm_gain, norm_bias], axis=1).T
    share = small.shape[1]
    small = jnp.pad(small, ((0, 12), (0, 128 - share)))
    got = all_gather(grid, [w_qkv, narrow_in, widen_out, small, w_out, w_up, w_down, ff_narrow, ff_widen], 0, 2, True)

    def whole(a):
        return a.reshape(-1, a.shape[-1])

    wq_full, a_full, b_full, small_full, wo_full, wu_full, wd_full, ffa_full, ffb_full = [whole(a) for a in got]
    norms = small_full.reshape(grid.devices, 16, 128)[:, :4, :share].transpose(1, 0, 2).reshape(4, grid.devices * share)
    norms = norms.astype(jnp.float32)
    gain_one, gain_two, shift_one, shift_two = norms[0], norms[1], norms[2], norms[3]
    seq_local, length, model_width = tokens.shape
    rows_all = seq_local * length
    set_cols = SETS * R
    chosen = (
        lax.broadcasted_iota(jnp.int32, (seq_local, set_cols), 1) // R == adapter_id[:, None]
    ).astype(jnp.float32)
    chosen = jnp.broadcast_to(chosen[:, None, :], (seq_local, length, set_cols)).reshape(rows_all, set_cols)
    chosen_three = jnp.concatenate([chosen, chosen, chosen], axis=1)
    positions = lax.broadcasted_iota(jnp.int32, (length,), 0)
    is_global = jnp.any(global_pos[:, :, None] == positions[None, None, :], axis=1).astype(jnp.float32)

    def cols_of(slot):
        return slice(slot * set_cols, (slot + 1) * set_cols)

    flat_in = tokens.reshape(rows_all, model_width)
    t_qkv = (product(flat_in, a_full[:, : 3 * set_cols]) * chosen_three).astype(jnp.bfloat16)
    projected = []
    for slot in range(3):
        summed = product(flat_in, wq_full[:, slot * model_width : (slot + 1) * model_width]) + against(
            t_qkv[:, cols_of(slot)], b_full[:, cols_of(slot)]
        )
        projected.append(summed.astype(jnp.bfloat16))
    query_low, key_low, value_low = projected
    mixed_flat, weights_low = attn_fwd(query_low, key_low, value_low, is_global[:, None, :], is_global[:, :, None], seq_local, length, 4)
    t_out = (product(mixed_flat, a_full[:, cols_of(3)]) * chosen).astype(jnp.bfloat16)
    attn_out = product(mixed_flat, wo_full) + against(t_out, b_full[:, cols_of(3)])
    resid = flat_in.astype(jnp.float32) + attn_out
    normed, norm_one_back = jax.vjp(lambda values: normalize(values, gain_one, shift_one), resid)
    normed_low = normed.astype(jnp.bfloat16)
    t_up = (product(normed_low, a_full[:, cols_of(4)]) * chosen).astype(jnp.bfloat16)
    pre_act = product(normed_low, wu_full) + against(t_up, ffb_full)
    cdf = 0.5 * (1.0 + lax.erf(pre_act * (0.5 ** 0.5)))
    act_low = (pre_act * cdf).astype(jnp.bfloat16)
    slope = cdf + pre_act * jnp.exp(-0.5 * pre_act * pre_act) * ((0.5 / math.pi) ** 0.5)
    act_low, slope = lax.optimization_barrier((act_low, slope))
    t_down = (product(act_low, ffa_full) * chosen).astype(jnp.bfloat16)
    down_out = product(act_low, wd_full) + against(t_down, b_full[:, cols_of(4)])
    final = normed + down_out
    result, norm_two_back = jax.vjp(lambda values: normalize(values, gain_two, shift_two), final)
    d_final = norm_two_back(cotangent.reshape(rows_all, model_width).astype(jnp.float32))[0]
    d_down = d_final.astype(jnp.bfloat16)
    dt_down = (product(d_down, b_full[:, cols_of(4)]) * chosen).astype(jnp.bfloat16)
    grad_b_down = over_rows(d_down, t_down)
    grad_ff_narrow = over_rows(act_low, dt_down)
    d_act = against(d_down, wd_full) + against(dt_down, ffa_full)
    d_pre = (d_act * slope).astype(jnp.bfloat16)
    dt_up = (product(d_pre, ffb_full) * chosen).astype(jnp.bfloat16)
    grad_ff_widen = over_rows(d_pre, t_up)
    grad_a_up = over_rows(normed_low, dt_up)
    d_normed = d_final + against(d_pre, wu_full) + against(dt_up, a_full[:, cols_of(4)])
    d_resid = norm_one_back(d_normed)[0]
    d_attn = d_resid.astype(jnp.bfloat16)
    dt_out = (product(d_attn, b_full[:, cols_of(3)]) * chosen).astype(jnp.bfloat16)
    grad_b_out = over_rows(d_attn, t_out)
    grad_a_out = over_rows(mixed_flat, dt_out)
    d_mixed = (against(d_attn, wo_full) + against(dt_out, a_full[:, cols_of(3)])).astype(jnp.bfloat16)
    d_parts = attn_bwd(query_low, key_low, value_low, weights_low, d_mixed, seq_local, length, 4)
    dt_parts = [
        (product(d_parts[slot], b_full[:, cols_of(slot)]) * chosen).astype(jnp.bfloat16) for slot in range(3)
    ]
    dt_qkv = jnp.concatenate(dt_parts, axis=1)
    grad_b_qkv = [over_rows(d_parts[slot], t_qkv[:, cols_of(slot)]) for slot in range(3)]
    grad_a_qkv = over_rows(flat_in, dt_qkv)
    d_input = d_resid + against(dt_qkv, a_full[:, : 3 * set_cols])
    for slot in range(3):
        d_input = d_input + against(d_parts[slot], wq_full[:, slot * model_width : (slot + 1) * model_width])
    rows_own, ff_own = model_width // grid.devices, ff_narrow.shape[0]
    late = reduce_scatter(
        grid, [grad_ff_narrow, grad_ff_widen, grad_a_out, grad_a_up, grad_b_out, grad_b_down],
        [(0, 0), (1, 0), (2, 0), (2, set_cols), (3, 0), (3, set_cols)],
        [(ff_own, set_cols), (ff_own, set_cols), (rows_own, 2 * set_cols), (rows_own, 2 * set_cols)], 1)
    early = reduce_scatter(
        grid, [grad_a_qkv] + grad_b_qkv, [(0, 0), (1, 0), (1, set_cols), (1, 2 * set_cols)],
        [(rows_own, 3 * set_cols), (rows_own, 3 * set_cols)], 2)
    return (
        result.reshape(seq_local, length, model_width).astype(jnp.bfloat16),
        d_input.reshape(seq_local, length, model_width).astype(jnp.bfloat16),
        jnp.concatenate([early[0], late[2]], axis=1),
        jnp.concatenate([early[1], late[3]], axis=1),
        late[0],
        late[1],
    )


LAG = 4


def local(sizes, tokens, cotangent, adapter_id, global_pos, w_qkv, w_out, w_up, w_down, norm_gain, norm_bias,
          narrow_in, widen_out, ff_narrow, ff_widen):
    grid = Grid(sizes)
    seq_local, length, width = tokens.shape
    rows = seq_local * length
    own = w_qkv.shape[0]
    fits = own % 16 == 0 and 128 % own == 0 and rows == 2 * length and w_up.shape[1] == 4 * rows and width == rows and width == grid.n["z"] * 4 * HD
    if not fits:
        return local_plain(sizes, tokens, cotangent, adapter_id, global_pos, w_qkv, w_out, w_up, w_down, norm_gain,
                           norm_bias, narrow_in, widen_out, ff_narrow, ff_widen)
    cols = SETS * R
    flat_in = tokens.reshape(rows, width)
    place = (lax.axis_index("dp") * grid.fsdp + lax.axis_index("fsdp")) % (128 // own)
    small = jnp.tile(jnp.concatenate([norm_gain, norm_bias], axis=1).T, (1, 128 // own))
    mine = lax.broadcasted_iota(jnp.int32, (1, 128), 1) // own == place
    small = jnp.where(mine, small, jnp.zeros((), BF))
    shards = (small, narrow_in, widen_out, w_qkv, w_out, w_up, ff_narrow, ff_widen, w_down)
    (g_small, g_ab, g_qkv, g_out, g_up, g_ff, g_dn, q, k, v, p, mix, h, f, yb, t, gb, sl, pick, norms) = forward(
        grid, flat_in, adapter_id, global_pos, shards, LAG, 0)
    ab, wo, ff = (flat2(a) for a in (g_ab, g_out, g_ff))
    wq = g_qkv.reshape(3, width, width)
    up = g_up.reshape(NCH, width, -1)
    dn = g_dn.reshape(NCH, w_up.shape[1], -1)
    res, dh, do, g_fa, g_fb, g_ao, g_au, g_bo, g_bd = middle(
        pick, norms, t, ab, f, cotangent.reshape(rows, width), h, yb, mix, wo, gb, sl, dn, up, ff)
    d_input, grad_a, grad_b, grad_fa, grad_fb = back(
        grid, q, k, v, p, do, flat_in, dh, ab, t, pick, wq, [g_fa, g_fb, g_ao, g_au, g_bo, g_bd], 1)
    d_input, grad_a, grad_b, grad_fa, grad_fb = settle([d_input, grad_a, grad_b, grad_fa, grad_fb])
    return res.reshape(tokens.shape), d_input.reshape(tokens.shape), grad_a, grad_b, grad_fa, grad_fb


def solution(mesh):
    rows = P(("dp", "fsdp"), None)
    cube = P(("dp", "fsdp"), None, None)
    in_specs = (cube, cube, P(("dp", "fsdp"))) + (rows,) * 11
    out_specs = (cube, cube) + (rows,) * 4
    return jax.shard_map(functools.partial(local, dict(mesh.shape)), mesh=mesh, in_specs=in_specs, out_specs=out_specs, check_vma=False)
```

```python
import functools, math
import jax
import jax.numpy as jnp
from jax import lax
from jax.experimental import pallas as pl
from jax.experimental.pallas import tpu as pltpu
from jax.sharding import PartitionSpec as P

MESH = pl.DeviceIdType.MESH


class Grid:
    def __init__(self, sizes):
        self.dp, self.fsdp = sizes["dp"], sizes["fsdp"]
        if (self.dp, self.fsdp) == (8, 4):
            self.dims = {"z": ("dp", 2, 4), "y": ("dp", 1, 2), "x": ("fsdp", 2, 2), "c": ("fsdp", 1, 2)}
        elif (self.dp, self.fsdp) == (64, 4):
            self.dims = {"z": ("dp", 8, 8), "y": ("dp", 2, 4), "x": ("fsdp", 1, 4), "c": ("dp", 1, 2)}
        else:
            self.dims = {"z": ("dp", 1, self.dp), "y": ("dp", 1, 1), "x": ("fsdp", self.fsdp, 1), "c": ("fsdp", 1, self.fsdp)}
        self.n = {k: v[2] for k, v in self.dims.items()}
        self.devices = self.dp * self.fsdp
        self.planes = self.devices // self.n["z"]

    def stride(self, k):
        axis, step, _ = self.dims[k]
        return step * (self.fsdp if axis == "dp" else 1)

    def here(self):
        idx = {"dp": lax.axis_index("dp"), "fsdp": lax.axis_index("fsdp")}
        return {k: (idx[axis] // step) % size for k, (axis, step, size) in self.dims.items()}

    def device(self, pos):
        out = {"dp": 0, "fsdp": 0}
        for k, (axis, step, _) in self.dims.items():
            out[axis] = out[axis] + pos[k] * step
        return out["dp"], out["fsdp"]

    def slot(self, y, x, c):
        return y * self.stride("y") + x * self.stride("x") + c * self.stride("c")


def barrier_with(grid, here, plane=False):
    barrier = pltpu.get_barrier_semaphore()
    count = 0
    for k in ("z", "y", "x", "c"):
        n = grid.n[k]
        for step in range(1, n):
            to = (here[k] + step) % n
            pl.semaphore_signal(barrier, inc=1, device_id=grid.device({**here, k: to}), device_id_type=MESH)
            count += 1
    for dy in range(1, grid.n["y"] if plane else 1):
        for dx in range(1, grid.n["x"]):
            to = {**here, "y": (here["y"] + dy) % grid.n["y"], "x": (here["x"] + dx) % grid.n["x"]}
            pl.semaphore_signal(barrier, inc=1, device_id=grid.device(to), device_id_type=MESH)
            count += 1
    pl.semaphore_wait(barrier, count)


class Gather:
    @staticmethod
    def parts(grid):
        return grid.n["z"] if grid.n["z"] <= 4 else 1

    @staticmethod
    def sem_total(grid):
        z, a, b, c = (grid.n[k] for k in ("z", "y", "x", "c"))
        k = Gather.parts(grid)
        return z + k * a + k * a * b + a * b

    def __init__(self, grid, here, src, out, send, recv, local):
        self.g, self.here, self.src, self.out = grid, here, src, out
        self.send, self.recv, self.local = send, recv, local
        self.k = Gather.parts(grid)
        self.nz, self.n2, self.n3 = grid.n["z"], grid.n["y"], grid.n["x"]
        self.base2 = self.nz
        self.base3 = self.base2 + self.k * self.n2
        self.base4 = self.base3 + self.k * self.n2 * self.n3
        self.sends = []
        self.first = here["c"] == 0
        self.p2 = jnp.where(self.first, here["y"], here["x"])
        self.p3 = jnp.where(self.first, here["x"], here["y"])

    def dev(self, z=None, p2=None, p3=None, c=None):
        h = self.here
        p2 = self.p2 if p2 is None else p2
        p3 = self.p3 if p3 is None else p3
        return self.g.device({
            "z": h["z"] if z is None else z,
            "y": jnp.where(self.first, p2, p3),
            "x": jnp.where(self.first, p3, p2),
            "c": h["c"] if c is None else c,
        })

    def m(self, p2, p3):
        return self.g.slot(jnp.where(self.first, p2, p3), jnp.where(self.first, p3, p2), self.here["c"])

    def part(self, i):
        return (self.here["z"] ^ i) if self.k == self.nz and self.nz & (self.nz - 1) == 0 else None

    def block(self, z, p2, p3):
        return self.out.at[:, self.m(p2, p3)] if z is None else self.out.at[z, self.m(p2, p3)]

    def copy(self, src, dst, sem, dev):
        return pltpu.make_async_remote_copy(src_ref=src, dst_ref=dst, send_sem=self.send.at[sem], recv_sem=self.recv.at[sem], device_id=dev, device_id_type=MESH)

    def pull(self, dst, sem):
        self.copy(dst, dst, sem, self.dev()).wait_recv()

    def sem2(self, z, p2):
        return self.base2 + (0 if z is None else z * self.n2) + p2

    def sem3(self, z, p2, p3):
        return self.base3 + ((0 if z is None else z * self.n2) + p2) * self.n3 + p3

    def to2(self, z, src=None):
        ref = self.block(z, self.p2, self.p3)
        return [self.copy(ref if src is None else src, ref, self.sem2(z, self.p2), self.dev(p2=(self.p2 + d) % self.n2)) for d in range(1, self.n2)]

    def to3(self, z, p2, src=None):
        ref = self.block(z, p2, self.p3)
        return [self.copy(ref if src is None else src, ref, self.sem3(z, p2, self.p3), self.dev(p3=(self.p3 + d) % self.n3)) for d in range(1, self.n3)]

    def to_core(self, p2, p3):
        if self.g.n["c"] == 1:
            return []
        ref = self.block(None, p2, p3)
        y, x = jnp.where(self.first, p2, p3), jnp.where(self.first, p3, p2)
        return [self.copy(ref, ref, self.base4 + y * self.n3 + x, self.dev(c=1 - self.here["c"]))]

    def line(self, i):
        z = self.here["z"]
        return z ^ i if self.nz & (self.nz - 1) == 0 else (z + i) % self.nz

    def own(self):
        return pltpu.make_async_copy(self.src, self.out.at[self.here["z"], self.m(self.p2, self.p3)], self.local)

    def along(self):
        z = self.here["z"]
        m0 = self.m(self.p2, self.p3)
        return [self.copy(self.src, self.out.at[z, m0], z, self.dev(z=self.line(i))) for i in range(1, self.nz)]

    def launch(self):
        for c in self.along():
            c.start()

    def begin(self):
        z = self.here["z"]
        return self.to3(z, self.p2, self.src) + self.to2(z, self.src) if self.part(0) is not None else []

    def wait_z(self, i):
        z = self.line(i)
        self.pull(self.out.at[z, self.m(self.p2, self.p3)], z)

    def after_z(self, i):
        return self.to2(self.part(i)) + self.to3(self.part(i), self.p2) if self.part(i) is not None else []

    def after_line(self):
        out = [] if self.part(0) is not None else self.to2(None) + self.to3(None, self.p2)
        return out + self.to_core(self.p2, self.p3)

    def wait2(self, i):
        z = self.part(i)
        for d in range(1, self.n2):
            q = (self.p2 + d) % self.n2
            self.pull(self.block(z, q, self.p3), self.sem2(z, q))

    def after2(self, i):
        return [c for d in range(1, self.n2) for c in self.to3(self.part(i), (self.p2 + d) % self.n2)]

    def after_all2(self):
        return [c for d in range(1, self.n2) for c in self.to_core((self.p2 + d) % self.n2, self.p3)]

    def wait3(self, j):
        p2 = (self.p2 + j) % self.n2
        for d in range(1, self.n3):
            q = (self.p3 + d) % self.n3
            for i in range(self.k):
                z = self.part(i)
                self.pull(self.block(z, p2, q), self.sem3(z, p2, q))

    def after3(self, j):
        p2 = (self.p2 + j) % self.n2
        return [c for d in range(1, self.n3) for c in self.to_core(p2, (self.p3 + d) % self.n3)]

    def pairs(self):
        part = functools.partial
        out = [(lambda: self.own().start(), self.begin)]
        out += [(part(self.wait_z, i), part(self.after_z, i)) for i in range(1, self.nz)]
        out += [(lambda: self.own().wait(), self.after_line)]
        out += [(part(self.wait2, i), part(self.after2, i)) for i in range(self.k)]
        out += [(lambda: None, self.after_all2)]
        out += [(part(self.wait3, j), part(self.after3, j)) for j in range(self.n2)]
        return out

    def steps(self):
        def act(wait, copies):
            wait()
            for c in copies():
                c.start()
        return [functools.partial(act, *p) for p in self.pairs()] + [self.arrived]

    def arrived(self):
        if self.g.n["c"] > 1:
            for y in range(self.n2):
                for x in range(self.n3):
                    self.pull(self.out.at[:, self.g.slot(y, x, 1 - self.here["c"])], self.base4 + y * self.n3 + x)

    def finish(self):
        for c in self.along():
            c.wait_send()
        for _, copies in self.pairs():
            for c in copies():
                c.wait_send()


def skewed(all_steps, lag):
    count = max(len(s) for s in all_steps)
    out = []
    for slot in range(count + lag * (len(all_steps) - 1)):
        for i, steps in enumerate(all_steps):
            k = slot - lag * i
            if 0 <= k < len(steps):
                out.append((i, steps[k]))
    return out


def run_skewed(all_steps, lag):
    for _, step in skewed(all_steps, lag):
        step()

SETS = 8
R = 16


def normalize(values, gain, shift):
    center = values - jnp.mean(values, axis=-1, keepdims=True)
    spread = jnp.mean(center * center, axis=-1, keepdims=True)
    return center * lax.rsqrt(spread + 1e-12) * gain + shift


def against(left, right):
    return lax.dot_general(
        left, right, (((1,), (1,)), ((), ())), preferred_element_type=jnp.float32
    )


def over_rows(left, right):
    return lax.dot_general(
        left, right, (((0,), (0,)), ((), ())), preferred_element_type=jnp.float32
    )


def product(left, right):
    return jnp.dot(left, right, preferred_element_type=jnp.float32)


def gelu_exact(values):
    return jax.nn.gelu(values, approximate=False)


def gather_kernel(grid, count, lag, first, *refs):
    srcs, outs = refs[:count], refs[count:2*count]
    send, recv, local = refs[2*count:]
    here = grid.here()
    barrier_with(grid, here)
    gs = [Gather(grid, here, srcs[i], outs[i], send.at[i], recv.at[i], local.at[i]) for i in range(count)]
    for g in gs:
        g.launch()
    steps = [g.steps() for g in gs]
    if first:
        for s in steps:
            s.pop(0)()
    run_skewed(steps, lag)
    for g in gs:
        g.finish()

def all_gather(grid, arrays, cid=0, lag=1, first=True):
    count = len(arrays)
    total = Gather.sem_total(grid)
    out_shape = [jax.ShapeDtypeStruct((grid.n["z"], grid.planes) + a.shape, a.dtype) for a in arrays]
    return pl.pallas_call(
        functools.partial(gather_kernel, grid, count, lag, first),
        out_shape=out_shape,
        in_specs=[pl.BlockSpec(memory_space=pltpu.VMEM)] * count,
        out_specs=[pl.BlockSpec(memory_space=pl.ANY)] * count,
        scratch_shapes=[pltpu.SemaphoreType.DMA((count, total)), pltpu.SemaphoreType.DMA((count, total)), pltpu.SemaphoreType.DMA((count,))],
        compiler_params=pltpu.CompilerParams(collective_id=cid, has_side_effects=True, vmem_limit_bytes=8*2**20),
        name="gather",
    )(*arrays)


class Scatter:
    @staticmethod
    def sem_total(grid):
        return grid.n["x"] * grid.n["y"] + grid.n["z"]

    @staticmethod
    def scratch(grid, shape, dtype=jnp.bfloat16):
        rows, cols = shape
        z, y, x = grid.n["z"], grid.n["y"], grid.n["x"]
        out = []
        if grid.n["c"] > 1:
            out += [pltpu.VMEM((y * x, z, rows, cols), dtype)] * 2
        out += [pltpu.VMEM((max(y * x - 1, 1), z, rows, cols), dtype)] * 2
        out += [pltpu.VMEM((z, rows, cols), dtype), pltpu.VMEM((max(z - 1, 1), rows, cols), dtype)]
        out += [pltpu.VMEM((y * x, z, rows, cols), jnp.float32)]
        return out

    def __init__(self, grid, here, src, put, bufs, send, recv):
        self.g, self.here, self.src, self.put, self.send, self.recv = grid, here, src, put, send, recv
        bufs = list(bufs)
        self.two = grid.n["c"] > 1
        self.s1, self.r1 = (bufs.pop(0), bufs.pop(0)) if self.two else (None, None)
        self.s2, self.r2, self.s4, self.r4, self.acc = bufs
        self.nz, self.n2, self.n3 = grid.n["z"], grid.n["y"], grid.n["x"]
        self.first = here["c"] == 0
        self.p2 = jnp.where(self.first, here["y"], here["x"])
        self.p3 = jnp.where(self.first, here["x"], here["y"])
        self.sends, self.pulls = [], []

    def dev(self, z=None, p2=None, p3=None, c=None):
        h = self.here
        p2 = self.p2 if p2 is None else p2
        p3 = self.p3 if p3 is None else p3
        return self.g.device({
            "z": h["z"] if z is None else z,
            "y": jnp.where(self.first, p2, p3),
            "x": jnp.where(self.first, p3, p2),
            "c": h["c"] if c is None else c,
        })

    def flat(self, p2, p3):
        return jnp.where(self.first, p2 * self.n3 + p3, p3 * self.n3 + p2)

    def push(self, make):
        make().start()
        self.sends.append(make)

    def copy(self, src, dst, sem, dev):
        return pltpu.make_async_remote_copy(src_ref=src, dst_ref=dst, send_sem=self.send.at[sem], recv_sem=self.recv.at[sem], device_id=dev, device_id_type=MESH)

    def far(self, p, d, n):
        return (p + d) % n

    def pull(self, dst, sem):
        pltpu.make_async_remote_copy(src_ref=dst, dst_ref=dst, send_sem=self.send.at[sem], recv_sem=self.recv.at[sem], device_id=self.dev(), device_id_type=MESH).wait_recv()

    def begin(self):
        c = self.here["c"]
        for y in range(self.n2):
            for x in range(self.n3):
                i = y * self.n3 + x
                if self.two:
                    self.s1[i] = self.src[:, self.g.slot(y, x, 1 - c)].astype(self.s1.dtype)
        if self.two:
            self.push(lambda: self.copy(self.s1, self.r1, 0, self.dev(c=1 - self.here["c"])))

    def step1(self):
        c = self.here["c"]
        if self.two:
            self.pull(self.r1, 0)
        for y in range(self.n2):
            for x in range(self.n3):
                i = y * self.n3 + x
                part = self.src[:, self.g.slot(y, x, c)]
                self.acc[i] = part + self.r1[i].astype(jnp.float32) if self.two else part
        for d2, d3 in self.others():
            i = d2 * self.n3 + d3 - 1
            self.s2[i] = self.acc[self.flat(self.far(self.p2, d2, self.n2), self.far(self.p3, d3, self.n3))].astype(self.s2.dtype)
            self.push(lambda d2=d2, d3=d3, i=i: self.copy(self.s2.at[i], self.r2.at[i], 1 + i, self.dev(p2=self.far(self.p2, d2, self.n2), p3=self.far(self.p3, d3, self.n3))))

    def others(self):
        return [(d2, d3) for d2 in range(self.n2) for d3 in range(self.n3) if d2 + d3 > 0]

    def step2(self):
        i = self.flat(self.p2, self.p3)
        total = self.acc[i]
        for d2, d3 in self.others():
            k = d2 * self.n3 + d3 - 1
            self.pull(self.r2.at[k], 1 + k)
            total = total + self.r2[k].astype(jnp.float32)
        self.acc[i] = total
        base = self.n2 * self.n3
        self.s4[...] = total.astype(self.s4.dtype)
        for d in range(1, self.nz):
            self.push(lambda d=d: self.copy(self.s4.at[self.far(self.here["z"], d, self.nz)], self.r4.at[d - 1], base + d, self.dev(z=self.far(self.here["z"], d, self.nz))))

    def step3(self):
        base = self.n2 * self.n3
        total = self.acc[self.flat(self.p2, self.p3), self.here["z"]]
        for d in range(1, self.nz):
            self.pull(self.r4.at[d - 1], base + d)
            total = total + self.r4[d - 1].astype(jnp.float32)
        self.put(total)

    def steps(self):
        return [self.begin, self.step1, self.step2, self.step3]

    def finish(self):
        for make in self.sends:
            make().wait_send()


def scatter_kernel(grid, places, nout, *refs):
    count = len(places)
    srcs, outs = refs[:count], refs[count:count + nout]
    rest = refs[count + nout:]
    send, recv = rest[:2]
    rest = rest[2:]
    per = len(rest) // count
    here = grid.here()
    barrier_with(grid, here, True)
    units = []
    for i, (o, col) in enumerate(places):
        def put(total, o=o, col=col):
            outs[o][:, col:col + total.shape[1]] = total
        units.append(Scatter(grid, here, srcs[i], put, rest[i * per:(i + 1) * per], send.at[i], recv.at[i]))
    run_skewed([u.steps() for u in units], 1)
    for u in units:
        u.finish()


def reduce_scatter(grid, arrays, places, outs, cid):
    count = len(arrays)
    views = [a.reshape(grid.n["z"], grid.planes, a.shape[0] // grid.devices, a.shape[1]) for a in arrays]
    total = Scatter.sem_total(grid)
    scratch = [pltpu.SemaphoreType.DMA((count, total)), pltpu.SemaphoreType.DMA((count, total))]
    for v in views:
        scratch += Scatter.scratch(grid, v.shape[2:])
    return pl.pallas_call(
        functools.partial(scatter_kernel, grid, places, len(outs)),
        out_shape=[jax.ShapeDtypeStruct(o, jnp.float32) for o in outs],
        in_specs=[pl.BlockSpec(memory_space=pltpu.VMEM)] * count,
        out_specs=[pl.BlockSpec(memory_space=pltpu.VMEM)] * len(outs),
        scratch_shapes=scratch,
        compiler_params=pltpu.CompilerParams(collective_id=cid, has_side_effects=True, vmem_limit_bytes=60 * 2**20),
        name="scatter",
    )(*views)


HD=64
def dotf(a,b,ca,cb):
    return lax.dot_general(a,b,(((ca,),(cb,)),((),())),preferred_element_type=jnp.float32)

def set_bias(bias, row, col, half):
    n=bias.shape[0]
    i=lax.broadcasted_iota(jnp.int32,(n,n),0); j=lax.broadcasted_iota(jnp.int32,(n,n),1)
    near=jnp.abs(i-j)<=half
    ok=near|(jnp.broadcast_to(row,(n,n))>0)|(jnp.broadcast_to(col,(n,n))>0)
    bias[...]=jnp.where(ok,0.0,-1e30)

def fwd_kernel(half,row_ref,col_ref,q_ref,k_ref,v_ref,o_ref,p_ref,bias):
    @pl.when(pl.program_id(1)==0)
    def _(): set_bias(bias,row_ref[0],col_ref[0],half)
    width=q_ref.shape[1]
    q=q_ref[...]; k=k_ref[...]
    vt=v_ref[...].T
    outs=[]
    for h in range(width//HD):
        c=(h*HD)//128*128
        lane=lax.broadcasted_iota(jnp.int32,(1,128),1)//HD
        keep=(lane==(h*HD-c)//HD)
        kh=jnp.where(keep,k[:,c:c+128],jnp.zeros((),k.dtype))*jnp.asarray(HD**-0.5,k.dtype)
        s=dotf(kh,q[:,c:c+128],1,1)+bias[...]
        top=jnp.max(s,axis=0,keepdims=True)
        e=jnp.exp(s-top)
        tot=jnp.sum(e,axis=0,keepdims=True)
        p=(e*(1.0/tot)).astype(jnp.bfloat16)
        p_ref[h]=p
        outs.append(dotf(vt[h*HD:(h+1)*HD],p,1,0))
    o_ref[...]=jnp.concatenate(outs,axis=0).T.astype(o_ref.dtype)

def attn_fwd(q,k,v,row,col,seqs,length,per=2):
    rows,width=q.shape; heads=width//HD
    w=per*HD
    spec=pl.BlockSpec((length,w),lambda s,h:(s,h))
    return pl.pallas_call(functools.partial(fwd_kernel,256),grid=(seqs,heads//per),
      in_specs=[pl.BlockSpec((1,1,length),lambda s,h:(s,0,0)),pl.BlockSpec((1,length,1),lambda s,h:(s,0,0)),spec,spec,spec],
      out_specs=[spec,pl.BlockSpec((None,per,length,length),lambda s,h:(s,h,0,0))],
      out_shape=[jax.ShapeDtypeStruct(q.shape,q.dtype),jax.ShapeDtypeStruct((seqs,heads,length,length),q.dtype)],
      scratch_shapes=[pltpu.VMEM((length,length),jnp.float32)],
      compiler_params=pltpu.CompilerParams(vmem_limit_bytes=48*2**20),name="attend")(row,col,q,k,v)

def bwd_kernel(q_ref,k_ref,v_ref,p_ref,d_ref,dq_ref,dk_ref,dv_ref):
    width=q_ref.shape[1]
    q=q_ref[...]; k=k_ref[...]; v=v_ref[...]; d=d_ref[...]
    scale=jnp.asarray(HD**-0.5,q.dtype)
    kt=(k*scale).T
    qs=q*scale
    dqs=[]; dks=[]; dvs=[]
    lane=lax.broadcasted_iota(jnp.int32,(1,128),1)//HD
    for h in range(width//HD):
        c=(h*HD)//128*128
        keep=(lane==(h*HD-c)//HD)
        vh=jnp.where(keep,v[:,c:c+128],jnp.zeros((),v.dtype))
        pb=p_ref[h]
        p=pb.astype(jnp.float32)
        dp=dotf(vh,d[:,c:c+128],1,1)
        t=p*dp
        inner=jnp.sum(t,axis=0,keepdims=True)
        ds=(t-p*inner).astype(jnp.bfloat16)
        dqs.append(dotf(kt[h*HD:(h+1)*HD],ds,1,0))
        dks.append(dotf(ds,qs[:,c:c+128],1,0))
        dvs.append(dotf(pb,d[:,c:c+128],1,0))
    dq_ref[...]=jnp.concatenate(dqs,axis=0).T.astype(dq_ref.dtype)
    for g in range(width//128):
        keep=lane==0
        dk_ref[:,g*128:(g+1)*128]=jnp.where(keep,dks[2*g],dks[2*g+1]).astype(dk_ref.dtype)
        dv_ref[:,g*128:(g+1)*128]=jnp.where(keep,dvs[2*g],dvs[2*g+1]).astype(dv_ref.dtype)

def attn_bwd(q,k,v,p,d,seqs,length,per=2):
    rows,width=q.shape; heads=width//HD; w=per*HD
    spec=pl.BlockSpec((length,w),lambda s,h:(s,h))
    return pl.pallas_call(bwd_kernel,grid=(seqs,heads//per),
      in_specs=[spec,spec,spec,pl.BlockSpec((None,per,length,length),lambda s,h:(s,h,0,0)),spec],
      out_specs=[spec]*3,out_shape=[jax.ShapeDtypeStruct(q.shape,q.dtype)]*3,
      compiler_params=pltpu.CompilerParams(vmem_limit_bytes=48*2**20),name="attend_back")(q,k,v,p,d)


BF = jnp.bfloat16
F32 = jnp.float32

def flat2(v):
    return v.reshape(v.shape[0] * v.shape[1] * v.shape[2], v.shape[3])

def whole_rows(ref, c0, c1):
    return flat2(ref[:, :, :, c0:c1])

UNITS = ("small", "ab", "q", "k", "v", "out", "up0", "ff", "up1", "up2", "up3", "dn0", "dn1", "dn2", "dn3")
NCH = 4
PACE = (2, 4, 2, 2, 1, 1)

def forward_kernel(grid, lag, *refs):
    n_in = 3 + 9
    (x, ids, gpos, in_small, in_a, in_b, s_qkv, s_out, s_up, in_fa, in_fb, s_dn) = refs[:n_in]
    outs = refs[n_in:n_in + 20]
    (g_small, g_ab, g_qkv, g_out, g_up, g_ff, g_dn, o_q, o_k, o_v, o_p, o_mix, o_h, o_f, o_yb, o_t, o_gb, o_sl, o_pick, o_norms) = outs
    (b_small, b_ab, b_qkv, b_out, b_ff, b_w, v_q, v_k, v_v, stage, bias, v_mix, v_h, v_f, v_yb, v_t, v_gb, tacc,
     s_small, s_ab, s_ff, pick, row, col, v_norms, send, recv, local, lsem, osem, ssem) = refs[n_in + 20:]
    rows, width = x.shape
    length = bias.shape[0]
    seqs = rows // length
    cols = pick.shape[2]
    here = grid.here()
    s_small[...] = jnp.zeros_like(s_small)
    s_small[0:in_small.shape[0], :] = in_small[...]
    s_ab[:, 0:5 * cols] = in_a[...]
    s_ab[:, 5 * cols:10 * cols] = in_b[...]
    s_ff[:, 0:cols] = in_fa[...]
    s_ff[:, cols:2 * cols] = in_fb[...]
    for n in range(seqs):
        pick[n] = jnp.where(lax.broadcasted_iota(jnp.int32, (1, cols), 1) // R == ids[n], 1.0, 0.0)
        count = gpos.shape[1]
        same = jnp.broadcast_to(gpos[n:n + 1, :], (length, count)) == lax.broadcasted_iota(jnp.int32, (length, count), 0)
        found = jnp.max(jnp.where(same, 1.0, 0.0), axis=1, keepdims=True)
        col[n] = found
        row[n] = jnp.broadcast_to(found, (length, 128)).T[0:1]
    barrier_with(grid, here)
    spots = {"small": (s_small, g_small), "ab": (s_ab, g_ab), "out": (s_out, g_out), "ff": (s_ff, g_ff)}
    cw, dw = s_up.shape[1] // NCH, s_dn.shape[1] // NCH
    for j, n in enumerate("qkv"):
        spots[n] = (s_qkv.at[:, j * width:(j + 1) * width], g_qkv.at[j])
    for j in range(NCH):
        spots["up%d" % j] = (s_up.at[:, j * cw:(j + 1) * cw], g_up.at[j])
        spots["dn%d" % j] = (s_dn.at[:, j * dw:(j + 1) * dw], g_dn.at[j])
    units = [Gather(grid, here, *spots[n], send.at[i], recv.at[i], local.at[i]) for i, n in enumerate(UNITS)]
    order = skewed([u.steps() for u in units], lag)
    for u in units:
        u.launch()
    state = {"at": 0}
    last = {i: max(k for k, (j, _) in enumerate(order) if j == i) for i in range(len(units))}

    def pump(count):
        end = min(state["at"] + count, len(order))
        for k in range(state["at"], end):
            order[k][1]()
        state["at"] = end

    def need(name):
        pump(max(0, last[UNITS.index(name)] + 1 - state["at"]))

    def load(src, dst, k):
        return pltpu.make_async_copy(src, dst, lsem.at[k])

    need("ab")
    c_small, c_ab = load(g_small, b_small, 0), load(g_ab, b_ab, 1)
    c_small.start()
    c_ab.start()
    c_small.wait()
    c_ab.wait()

    step = 256
    blocks = rows // step

    def rows_at(r):
        return pl.ds(pl.multiple_of(r * step, step), step)

    def picked(r):
        return pick[(r * step) // length]

    def taking(count):
        base = state["at"]
        ends = [min(base + (n + 1) * count, len(order)) for n in range(blocks)]
        state["at"] = ends[-1]

        def hook(r):
            lo = base
            for n, hi in enumerate(ends):
                @pl.when(r == n)
                def _(lo=lo, hi=hi):
                    for k in range(lo, hi):
                        order[k][1]()
                lo = hi
        return hook

    for slot, dst in enumerate((v_q, v_k, v_v)):
        need("qkv"[slot])
        c_w = load(g_qkv.at[slot], b_qkv.at[slot], 2)
        c_w.start()
        c_w.wait()
        hook = taking(PACE[0])

        @pl.loop(0, blocks)
        def _(r, slot=slot, dst=dst, hook=hook):
            at = rows_at(r)
            xa = x[at, :]
            t = (jnp.dot(xa, whole_rows(b_ab, slot * cols, (slot + 1) * cols), preferred_element_type=F32) * picked(r)).astype(BF)
            v_t[at, slot * cols:(slot + 1) * cols] = t
            acc = jnp.dot(xa, flat2(b_qkv[slot]), preferred_element_type=F32)
            acc = acc + dotf(t, whole_rows(b_ab, (5 + slot) * cols, (6 + slot) * cols), 1, 1)
            dst[at, :] = acc.astype(BF)
            hook(r)
    saves = [pltpu.make_async_copy(v_q, o_q, osem.at[0]), pltpu.make_async_copy(v_k, o_k, osem.at[1]), pltpu.make_async_copy(v_v, o_v, osem.at[2])]
    for c in saves:
        c.start()

    per = 4
    groups = width // (per * HD)
    total = seqs * groups
    chunks = []
    base = state["at"]
    share = PACE[1]

    def save_p(i, slot):
        return pltpu.make_async_copy(stage.at[slot], o_p.at[i], ssem.at[slot])

    def attend(i, carry):
        seq, hp = i // groups, i % groups
        @pl.when(hp == 0)
        def _():
            set_bias(bias, row[seq], col[seq], length // 2)
        slot = i % 2
        @pl.when(i >= 2)
        def _():
            save_p(i - 2, slot).wait()
        at = pl.ds(pl.multiple_of(seq * length, length), length)
        q = v_q[at, pl.ds(pl.multiple_of(hp * per * HD, per * HD), per * HD)]
        k = v_k[at, pl.ds(pl.multiple_of(hp * per * HD, per * HD), per * HD)]
        vt = v_v[at, pl.ds(pl.multiple_of(hp * per * HD, per * HD), per * HD)].T
        got = []
        lane = lax.broadcasted_iota(jnp.int32, (1, 128), 1) // HD
        for h in range(per):
            c = (h * HD) // 128 * 128
            kh = jnp.where(lane == (h * HD - c) // HD, k[:, c:c + 128], jnp.zeros((), BF)) * jnp.asarray(HD ** -0.5, BF)
            s = dotf(kh, q[:, c:c + 128], 1, 1) + bias[...]
            e = jnp.exp(s - jnp.max(s, axis=0, keepdims=True))
            p = (e * (1.0 / jnp.sum(e, axis=0, keepdims=True))).astype(BF)
            stage[slot, (h // 2) * length:(h // 2 + 1) * length, (h % 2) * length:(h % 2 + 1) * length] = p
            got.append(dotf(vt[h * HD:(h + 1) * HD], p, 1, 0))
        v_mix[at, pl.ds(pl.multiple_of(hp * per * HD, per * HD), per * HD)] = jnp.concatenate(got, axis=0).T.astype(BF)
        save_p(i, slot).start()
        for n in range(total):
            lo, hi = base + n * share, base + (n + 1) * share
            @pl.when(i == n)
            def _():
                for k2 in range(lo, hi):
                    order[k2][1]()
        return carry

    lax.fori_loop(0, total, attend, 0)
    state["at"] = base + share * total
    save_mix = pltpu.make_async_copy(v_mix, o_mix, osem.at[3])
    save_mix.start()

    need("out")
    c_out = load(g_out, b_out, 3)
    c_out.start()
    per_group = grid.devices // (width // 128)
    small = b_small[...].reshape(width // 128, per_group, 16, 128).astype(F32).sum(axis=1)
    norms = jnp.concatenate([small[g] for g in range(width // 128)], axis=1)
    gain, shift = norms[0:1], norms[2:3]
    v_norms[...] = norms
    save_norms = pltpu.make_async_copy(v_norms, o_norms, osem.at[9])
    save_norms.start()
    save_pick = pltpu.make_async_copy(pick, o_pick, osem.at[10])
    save_pick.start()
    c_out.wait()
    hook_out = taking(PACE[2])

    @pl.loop(0, blocks)
    def _(r):
        at = rows_at(r)
        oa = v_mix[at, :]
        t = (jnp.dot(oa, whole_rows(b_ab, 3 * cols, 4 * cols), preferred_element_type=F32) * picked(r)).astype(BF)
        v_t[at, 3 * cols:4 * cols] = t
        acc = jnp.dot(oa, whole_rows(b_out, 0, width), preferred_element_type=F32)
        acc = acc + dotf(t, whole_rows(b_ab, 8 * cols, 9 * cols), 1, 1)
        h = x[at, :].astype(F32) + acc
        v_h[at, :] = h
        center = h - jnp.mean(h, axis=1, keepdims=True)
        spread = jnp.mean(center * center, axis=1, keepdims=True)
        y = center * lax.rsqrt(spread + 1e-12) * gain + shift
        v_f[at, :] = y
        yb = y.astype(BF)
        v_yb[at, :] = yb
        v_t[at, 4 * cols:5 * cols] = (jnp.dot(yb, whole_rows(b_ab, 4 * cols, 5 * cols), preferred_element_type=F32) * picked(r)).astype(BF)
        hook_out(r)

    saves2 = [pltpu.make_async_copy(v_h, o_h, osem.at[4]), pltpu.make_async_copy(v_yb, o_yb, osem.at[5])]
    for c in saves2:
        c.start()

    def save_s(j, slot):
        return pltpu.make_async_copy(stage.at[slot], o_sl.at[j], ssem.at[slot])

    save_p(total - 2, 0).wait()
    save_p(total - 1, 1).wait()

    def load_up(j, slot):
        return load(g_up.at[j], b_w.at[slot], 4 + slot)

    for j in range(NCH):
        need("up%d" % j)
        if j == 0:
            load_up(0, 0).start()
            need("ff")
            c_ff = load(g_ff, b_ff, 6)
            c_ff.start()
            c_ff.wait()
        else:
            load_up(j, j % 2).start()
        pump(3)
        load_up(j, j % 2).wait()
        if j >= 2:
            save_s(j - 2, j % 2).wait()
        hook = taking(PACE[3])

        @pl.loop(0, blocks)
        def _(r, j=j, hook=hook):
            at = rows_at(r)
            u = jnp.dot(v_yb[at, :], whole_rows(b_w.at[j % 2], 0, cw), preferred_element_type=F32)
            wide = flat2(b_ff[:, :, :, cols:2 * cols])[j * cw:(j + 1) * cw]
            u = u + dotf(v_t[at, 4 * cols:5 * cols], wide, 1, 1)
            cdf = 0.5 * (1.0 + lax.erf(u * (0.5 ** 0.5)))
            gb = (u * cdf).astype(BF)
            v_gb[at, j * cw:(j + 1) * cw] = gb
            stage[j % 2, at, :] = (cdf + u * jnp.exp(-0.5 * u * u) * ((0.5 / math.pi) ** 0.5)).astype(BF)
            hook(r)

        save_s(j, j % 2).start()
    hook_ff = taking(PACE[4])

    @pl.loop(0, blocks)
    def _(r):
        at = rows_at(r)
        acc = jnp.dot(v_gb[at, :], flat2(b_ff[:, :, :, 0:cols]), preferred_element_type=F32)
        v_t[at, 5 * cols:6 * cols] = (acc * picked(r)).astype(BF)
        hook_ff(r)

    save_gb = pltpu.make_async_copy(v_gb, o_gb, osem.at[6])
    save_gb.start()
    save_t = pltpu.make_async_copy(v_t, o_t, osem.at[7])
    save_t.start()

    for j in range(NCH):
        need("dn%d" % j)
        slot = j % 2
        view = b_w.at[slot]
        c_dn = load(g_dn.at[j], tacc.at[slot], 7)
        c_dn.start()
        pump(3)
        c_dn.wait()
        hook = taking(PACE[5])

        @pl.loop(0, blocks)
        def _(r, j=j, slot=slot, hook=hook):
            at = rows_at(r)
            acc = jnp.dot(v_gb[at, :], flat2(tacc[slot]), preferred_element_type=F32)
            wide = whole_rows(b_ab, 9 * cols, 10 * cols)[j * dw:(j + 1) * dw]
            acc = acc + dotf(v_t[at, 5 * cols:6 * cols], wide, 1, 1)
            v_f[at, j * dw:(j + 1) * dw] = v_f[at, j * dw:(j + 1) * dw] + acc
            hook(r)

        saves2.append(pltpu.make_async_copy(v_f.at[:, j * dw:(j + 1) * dw], o_f.at[:, j * dw:(j + 1) * dw], osem.at[11 + j]))
        saves2[-1].start()

    pump(len(order))
    for u in units:
        u.finish()
    save_s(NCH - 2, 0).wait()
    save_s(NCH - 1, 1).wait()
    for c in saves + saves2 + [save_mix, save_gb, save_t, save_norms, save_pick]:
        c.wait()


def forward(grid, x, ids, gpos, shards, lag, cid):
    rows, width = x.shape
    seqs = ids.shape[0]
    length = rows // seqs
    in_small, in_a, in_b, s_qkv, s_out, s_up, in_fa, in_fb, s_dn = shards
    cols = in_fa.shape[1]
    z, m = grid.n["z"], grid.planes
    S = jax.ShapeDtypeStruct
    s_small, s_ab, s_ff = S((16, 128), BF), S((in_a.shape[0], 10 * cols), BF), S((in_fa.shape[0], 2 * cols), BF)
    cw, dw = s_up.shape[1] // NCH, s_dn.shape[1] // NCH
    total = Gather.sem_total(grid)
    nu = len(UNITS)
    def g(a, c=None, lead=()):
        return jax.ShapeDtypeStruct(lead + (z, m, a.shape[0], a.shape[1] if c is None else c), BF)
    out_shape = [g(s_small), g(s_ab), g(s_qkv, width, (3,)), g(s_out), g(s_up, cw, (NCH,)), g(s_ff), g(s_dn, dw, (NCH,)),
        S(x.shape, BF), S(x.shape, BF), S(x.shape, BF), S((seqs * width // (4 * HD), 2 * length, 2 * length), BF),
        S(x.shape, BF), S(x.shape, F32), S(x.shape, F32), S(x.shape, BF), S((rows, 6 * cols), BF), S((rows, s_up.shape[1]), BF), S((NCH, rows, cw), BF),
        S((seqs, 1, cols), F32), S((16, width), F32)]
    V = pltpu.VMEM
    scratch = [V((z, m) + s_small.shape, BF), V((z, m) + s_ab.shape, BF), V((3, z, m, s_qkv.shape[0], width), BF), V((z, m) + s_out.shape, BF), V((z, m) + s_ff.shape, BF),
        V((2, z, m, s_up.shape[0], cw), BF),
        V(x.shape, BF), V(x.shape, BF), V(x.shape, BF), V((2, 2 * length, 2 * length), BF), V((length, length), F32), V(x.shape, BF), V(x.shape, F32), V(x.shape, F32), V(x.shape, BF),
        V((rows, 6 * cols), BF), V((rows, s_up.shape[1]), BF), V((2, z, m, s_dn.shape[0], dw), BF),
        V(s_small.shape, BF), V(s_ab.shape, BF), V(s_ff.shape, BF), V((seqs, 1, cols), F32), V((seqs, 1, length), F32), V((seqs, length, 1), F32), V((16, width), F32),
        pltpu.SemaphoreType.DMA((nu, total)), pltpu.SemaphoreType.DMA((nu, total)), pltpu.SemaphoreType.DMA((nu,)), pltpu.SemaphoreType.DMA((8,)), pltpu.SemaphoreType.DMA((11 + NCH,)), pltpu.SemaphoreType.DMA((2,))]
    return pl.pallas_call(
        functools.partial(forward_kernel, grid, lag),
        out_shape=out_shape,
        in_specs=[pl.BlockSpec(memory_space=pltpu.VMEM), pl.BlockSpec(memory_space=pltpu.SMEM)] + [pl.BlockSpec(memory_space=pltpu.VMEM)] * 10,
        out_specs=[pl.BlockSpec(memory_space=pl.ANY)] * 20,
        scratch_shapes=scratch,
        compiler_params=pltpu.CompilerParams(collective_id=cid, has_side_effects=True, vmem_limit_bytes=67043328),
        name="forward",
    )(x, ids, gpos, *shards)


def tdot(a, b):
    return lax.dot_general(a, b, (((0,), (0,)), ((), ())), preferred_element_type=F32)

def norm_parts(z):
    center = z - jnp.mean(z, axis=1, keepdims=True)
    inv = lax.rsqrt(jnp.mean(center * center, axis=1, keepdims=True) + 1e-12)
    return center * inv, inv

def norm_back(hat, inv, g):
    return inv * (g - jnp.mean(g, axis=1, keepdims=True) - hat * jnp.mean(g * hat, axis=1, keepdims=True))

def middle_kernel(pick, norms, t, ab, f, cot, h, yb, mix, wo, gb, sl, wd, wu, ff,
                  o_res, o_dh, o_do, g_fa, g_fb, g_ao, g_au, g_bo, g_bd,
                  v_f, v_cot, v_res, v_de, v_dy, v_yb, v_mix, v_wo, v_du, tdn, tup, tout, acc, sem, osem):
    j = pl.program_id(0)
    last = pl.num_programs(0) - 1
    rows, width = v_f.shape
    cols = pick.shape[2]
    step = 256
    blocks = rows // step
    length = rows // pick.shape[0]

    def rows_at(r):
        return pl.ds(pl.multiple_of(r * step, step), step)

    def picked(r):
        return pick[(r * step) // length]

    def slot(i):
        return ab[:, i * cols:(i + 1) * cols]

    loads = [pltpu.make_async_copy(f, v_f, sem.at[0]), pltpu.make_async_copy(cot, v_cot, sem.at[1]),
             pltpu.make_async_copy(h, v_f, sem.at[2]), pltpu.make_async_copy(yb, v_yb, sem.at[3]),
             pltpu.make_async_copy(mix, v_mix, sem.at[4]), pltpu.make_async_copy(wo, v_wo, sem.at[5])]
    save_res = pltpu.make_async_copy(v_res, o_res, osem.at[0])
    gain_one, gain_two, shift_two = norms[0:1, :], norms[1:2, :], norms[3:4, :]

    @pl.when(j == 0)
    def _():
        loads[0].start()
        loads[1].start()
        loads[0].wait()
        loads[1].wait()

        @pl.loop(0, blocks)
        def _(r):
            at = rows_at(r)
            hat, inv = norm_parts(v_f[at, :])
            v_res[at, :] = (hat * gain_two + shift_two).astype(BF)
            df = norm_back(hat, inv, v_cot[at, :].astype(F32) * gain_two)
            v_dy[at, :] = df
            de = df.astype(BF)
            v_de[at, :] = de
            tdn[at, :] = (jnp.dot(de, slot(9), preferred_element_type=F32) * picked(r)).astype(BF)

        save_res.start()
        for c in loads[2:]:
            c.start()
        g_bd[...] = tdot(v_de[...], t[:, 5 * cols:6 * cols])
        acc[...] = jnp.zeros_like(acc)

    half = 512

    @pl.loop(0, rows // half)
    def _(r):
        at = pl.ds(pl.multiple_of(r * half, half), half)
        dg = dotf(tdn[at, :], ff[:, 0:cols], 1, 1)
        for c in range(NCH):
            w = wd.shape[2]
            dg = dg + dotf(v_de[at, c * w:(c + 1) * w], wd[c], 1, 1)
        du = (dg * sl[at, :].astype(F32)).astype(BF)
        v_du[at, :] = du
        v_dy[at, :] = v_dy[at, :] + dotf(du, wu[...], 1, 1)
        acc[at, :] = acc[at, :] + jnp.dot(du, ff[:, cols:2 * cols], preferred_element_type=F32)

    g_fa[...] = tdot(gb[...], tdn[...])
    g_fb[...] = tdot(v_du[...], t[:, 4 * cols:5 * cols])

    @pl.when(j == last)
    def _():
        for c in loads[2:]:
            c.wait()
        save_res.wait()

        @pl.loop(0, blocks)
        def _(r):
            at = rows_at(r)
            dtu = (acc[at, :] * picked(r)).astype(BF)
            tup[at, :] = dtu
            dy = v_dy[at, :] + dotf(dtu, slot(4), 1, 1)
            hat, inv = norm_parts(v_f[at, :])
            dh = norm_back(hat, inv, dy * gain_one)
            v_dy[at, :] = dh
            da = dh.astype(BF)
            v_de[at, :] = da
            dto = (jnp.dot(da, slot(8), preferred_element_type=F32) * picked(r)).astype(BF)
            tout[at, :] = dto
            v_res[at, :] = (dotf(da, v_wo[...], 1, 1) + dotf(dto, slot(3), 1, 1)).astype(BF)

        save_dh = pltpu.make_async_copy(v_dy, o_dh, osem.at[1])
        save_do = pltpu.make_async_copy(v_res, o_do, osem.at[2])
        save_dh.start()
        save_do.start()
        g_au[...] = tdot(v_yb[...], tup[...])
        g_bo[...] = tdot(v_de[...], t[:, 3 * cols:4 * cols])
        g_ao[...] = tdot(v_mix[...], tout[...])
        save_dh.wait()
        save_do.wait()


def middle(pick, norms, t, ab, f, cot, h, yb, mix, wo, gb, sl, dn, up, ff):
    rows, width = f.shape
    cols = pick.shape[2]
    total = gb.shape[1]
    blk = 512
    per = sl.shape[2] // blk
    S, V = jax.ShapeDtypeStruct, pltpu.VMEM
    whole = pl.BlockSpec(memory_space=pltpu.VMEM)
    far = pl.BlockSpec(memory_space=pl.ANY)
    wcol = dn.shape[2]
    return pl.pallas_call(
        middle_kernel,
        grid=(total // blk,),
        in_specs=[whole] * 4 + [far] * 6 + [
            pl.BlockSpec((rows, blk), lambda j: (0, j)),
            pl.BlockSpec((None, rows, blk), lambda j: (j // per, 0, j % per)),
            pl.BlockSpec((NCH, blk, wcol), lambda j: (0, j, 0)),
            pl.BlockSpec((None, width, blk), lambda j: (j // per, 0, j % per)),
            pl.BlockSpec((blk, 2 * cols), lambda j: (j, 0)),
        ],
        out_specs=[far] * 3 + [pl.BlockSpec((blk, cols), lambda j: (j, 0))] * 2 + [pl.BlockSpec((width, cols), lambda j: (0, 0))] * 4,
        out_shape=[S(f.shape, BF), S(f.shape, F32), S(f.shape, BF), S((total, cols), F32), S((total, cols), F32)] + [S((width, cols), F32)] * 4,
        scratch_shapes=[V(f.shape, F32), V(f.shape, BF), V(f.shape, BF), V(f.shape, BF), V(f.shape, F32), V(f.shape, BF), V(f.shape, BF), V((width, width), BF),
                        V((rows, blk), BF), V((rows, cols), BF), V((rows, cols), BF), V((rows, cols), BF), V((rows, cols), F32),
                        pltpu.SemaphoreType.DMA((6,)), pltpu.SemaphoreType.DMA((3,))],
        compiler_params=pltpu.CompilerParams(vmem_limit_bytes=60 * 2**20),
        name="middle",
    )(pick, norms, t, ab, f, cot, h, yb, mix, wo, gb, sl, dn, up, ff)


def back_kernel(grid, *refs):
    q, k, v, p, d, h_x, dh, h_ab, h_t, pick, wq = refs[:11]
    h_late = refs[11:17]
    o_x, o_a, o_b, o_fa, o_fb = refs[17:22]
    (b_q, b_k, b_v, b_d, b_p, v_dq, v_dk, v_dv, v_wq, v_dt, b_dh, b_x, e_a, e_b, x, ab, t,
     lsem, wsem, hsem, xsem, send, recv) = refs[22:45]
    late, rest = refs[45:51], list(refs[51:])
    here = grid.here()
    rows, width = x.shape
    length, wide = b_q.shape[1], b_q.shape[2]
    groups = width // wide
    total = rows // length * groups
    cols = pick.shape[2]
    step = b_x.shape[1]
    blocks = rows // step
    nz = grid.n["z"]

    def put_in(out, col):
        def put(value):
            out[:, col:col + value.shape[1]] = value
        return put

    per = len(rest) // 8
    puts = [put_in(o_fa, 0), put_in(o_fb, 0), put_in(o_a, 3 * cols), put_in(o_a, 4 * cols), put_in(o_b, 3 * cols),
            put_in(o_b, 4 * cols), put_in(o_b, 0), put_in(o_a, 0)]
    units = [Scatter(grid, here, src, puts[i], rest[i * per:(i + 1) * per], send.at[i], recv.at[i])
             for i, src in enumerate(tuple(late) + (e_b, e_a))]
    steps = [u.steps() for u in units]

    def loads(i, slot):
        at = pl.ds(pl.multiple_of(i // groups * length, length), length)
        cs = pl.ds(pl.multiple_of(i % groups * wide, wide), wide)
        out = [pltpu.make_async_copy(a.at[at, cs], b.at[slot], lsem.at[slot, n]) for n, (a, b) in enumerate(((q, b_q), (k, b_k), (v, b_v), (d, b_d)))]
        return out + [pltpu.make_async_copy(p.at[i], b_p.at[slot], lsem.at[slot, 4])]

    def rows_at(r):
        return pl.ds(pl.multiple_of(r * step, step), step)

    def load_h(r, slot):
        return pltpu.make_async_copy(dh.at[rows_at(r), :], b_dh.at[slot], hsem.at[slot])

    def save_x(r, slot):
        return pltpu.make_async_copy(b_x.at[slot], o_x.at[rows_at(r), :], xsem.at[slot])

    load_t = pltpu.make_async_copy(h_t.at[:, 0:3 * cols], t, wsem.at[0])
    load_late = [pltpu.make_async_copy(a, b, wsem.at[4 + n]) for n, (a, b) in enumerate(zip(h_late, late))]
    load_rest = [pltpu.make_async_copy(h_ab, ab, wsem.at[1]), pltpu.make_async_copy(h_x, x, wsem.at[2]), pltpu.make_async_copy(wq, v_wq, wsem.at[3])]
    for c in load_late + loads(0, 0):
        c.start()
    barrier_with(grid, here, True)

    def first(n):
        load_late[n].wait()
        steps[n][0]()

    order = [s[n] for n in range(1, 4) for s in steps[:6]]
    share = -(-len(order) // total)
    turns = [order[n * share:(n + 1) * share] for n in range(total)]
    for n in range(6):
        first(n)
    for c in [load_t] + load_rest:
        c.start()
    scale = jnp.asarray(HD ** -0.5, BF)
    lane = lax.broadcasted_iota(jnp.int32, (1, 128), 1) // HD

    def attend(i, carry):
        slot = i % 2

        @pl.when(i + 1 < total)
        def _():
            for c in loads(i + 1, 1 - slot):
                c.start()

        for c in loads(i, slot):
            c.wait()

        qb, kb, vb, db = b_q[slot], b_k[slot], b_v[slot], b_d[slot]
        kt, qs = (kb * scale).T, qb * scale
        dqs, dks, dvs = [], [], []
        for h in range(wide // HD):
            c = (h * HD) // 128 * 128
            vh = jnp.where(lane == (h * HD - c) // HD, vb[:, c:c + 128], jnp.zeros((), BF))
            pb = b_p[slot, (h // 2) * length:(h // 2 + 1) * length, (h % 2) * length:(h % 2 + 1) * length]
            pf = pb.astype(F32)
            dp = dotf(vh, db[:, c:c + 128], 1, 1)
            w = pf * dp
            ds = (w - pf * jnp.sum(w, axis=0, keepdims=True)).astype(BF)
            dqs.append(dotf(kt[h * HD:(h + 1) * HD], ds, 1, 0))
            dks.append(dotf(ds, qs[:, c:c + 128], 1, 0))
            dvs.append(dotf(pb, db[:, c:c + 128], 1, 0))
        at = pl.ds(pl.multiple_of(i // groups * length, length), length)
        v_dq[at, pl.ds(pl.multiple_of(i % groups * wide, wide), wide)] = jnp.concatenate(dqs, axis=0).T.astype(BF)
        for g in range(wide // 128):
            cs = pl.ds(pl.multiple_of(i % groups * wide + g * 128, 128), 128)
            v_dk[at, cs] = jnp.where(lane == 0, dks[2 * g], dks[2 * g + 1]).astype(BF)
            v_dv[at, cs] = jnp.where(lane == 0, dvs[2 * g], dvs[2 * g + 1]).astype(BF)
        for n in range(total):
            @pl.when(i == n)
            def _(n=n):
                for act in turns[n]:
                    act()
        return carry

    lax.fori_loop(0, total, attend, 0)
    for c in [load_t] + load_rest[:2]:
        c.wait()
    load_h(0, 0).start()
    grads = (v_dq, v_dk, v_dv)
    part = width // nz

    @pl.loop(0, blocks)
    def _(r):
        at = rows_at(r)
        for s, g in enumerate(grads):
            v_dt[at, s * cols:(s + 1) * cols] = (jnp.dot(g[at, :], ab[:, (5 + s) * cols:(6 + s) * cols], preferred_element_type=F32) * pick[(r * step) // length]).astype(BF)

    @pl.loop(0, nz)
    def _(n):
        e_a[n] = tdot(x[:, pl.ds(pl.multiple_of(n * part, part), part)], v_dt[...]).reshape(e_a.shape[1:])

    steps[7][0]()

    @pl.loop(0, nz)
    def _(n):
        cs = pl.ds(pl.multiple_of(n * part, part), part)
        for s in range(3):
            e_b[n, :, :, s * cols:(s + 1) * cols] = tdot(grads[s][:, cs], t[:, s * cols:(s + 1) * cols]).reshape(e_b.shape[1:3] + (cols,))

    steps[6][0]()
    steps[7][1]()
    load_rest[2].wait()
    plan = [[] for _ in range(blocks)]
    for n, act in enumerate((steps[6][1], steps[7][2], steps[6][2], steps[7][3], steps[6][3])):
        plan[min(n, blocks - 1)].append(act)

    def finish(r, carry):
        slot = r % 2

        @pl.when(r + 1 < blocks)
        def _():
            load_h(r + 1, 1 - slot).start()

        load_h(r, slot).wait()

        @pl.when(r >= 2)
        def _():
            save_x(r - 2, slot).wait()

        at = rows_at(r)
        acc = b_dh[slot] + dotf(v_dt[at, :], ab[:, 0:3 * cols], 1, 1)
        for s, g in enumerate(grads):
            acc = acc + dotf(g[at, :], v_wq[s], 1, 1)
        b_x[slot] = acc.astype(BF)
        save_x(r, slot).start()
        for n in range(blocks):
            @pl.when(r == n)
            def _(n=n):
                for act in plan[n]:
                    act()
        return carry

    lax.fori_loop(0, blocks, finish, 0)
    for u in units:
        u.finish()
    for r in range(max(0, blocks - 2), blocks):
        save_x(r, r % 2).wait()


def back(grid, q, k, v, p, d, x, dh, ab, t, pick, wq, late, cid):
    rows, width = x.shape
    seqs, cols = pick.shape[0], pick.shape[2]
    length, wide, step = rows // seqs, 4 * HD, 256
    z, m = grid.n["z"], grid.planes
    views = [a.reshape(z, m, a.shape[0] // grid.devices, a.shape[1]) for a in late]
    own = width // grid.devices
    S, V = jax.ShapeDtypeStruct, pltpu.VMEM
    sems = Scatter.sem_total(grid)
    scratch = [V((2, length, wide), BF)] * 4 + [V((2,) + p.shape[1:], BF)] + [V(x.shape, BF)] * 3 + [
        V(wq.shape, BF), V((rows, 3 * cols), BF), V((2, step, width), F32), V((2, step, width), BF),
        V((z, m, own, 3 * cols), F32), V((z, m, own, 3 * cols), F32), V(x.shape, BF), V(ab.shape, BF), V((rows, 3 * cols), BF),
        pltpu.SemaphoreType.DMA((2, 5)), pltpu.SemaphoreType.DMA((4 + len(views),)), pltpu.SemaphoreType.DMA((2,)), pltpu.SemaphoreType.DMA((2,)),
        pltpu.SemaphoreType.DMA((8, sems)), pltpu.SemaphoreType.DMA((8, sems))] + [V(w.shape, F32) for w in views]
    for shape in [w.shape[2:] for w in views] + [(own, 3 * cols)] * 2:
        scratch += Scatter.scratch(grid, shape)
    far, near = pl.BlockSpec(memory_space=pl.ANY), pl.BlockSpec(memory_space=pltpu.VMEM)
    return pl.pallas_call(
        functools.partial(back_kernel, grid),
        out_shape=[S(x.shape, BF), S((own, 5 * cols), F32), S((own, 5 * cols), F32)] + [S(w.shape[2:], F32) for w in views[:2]],
        in_specs=[far] * 9 + [near, far] + [far] * 6,
        out_specs=[far] + [near] * 4,
        scratch_shapes=scratch,
        compiler_params=pltpu.CompilerParams(collective_id=cid, has_side_effects=True, vmem_limit_bytes=67043328),
        name="back",
    )(q, k, v, p, d, x, dh, ab, t, pick, wq, *views)


def settle_kernel(pieces, *refs):
    count = len(pieces)
    ins, outs, bufs = refs[:count], refs[count:2 * count], refs[2 * count:3 * count]
    isem, osem = refs[3 * count:]
    pairs = []
    for i, n in enumerate(pieces):
        each = ins[i].shape[0] // n
        for k in range(n):
            at = pl.ds(k * each, each)
            slot = len(pairs)
            pairs.append((pltpu.make_async_copy(ins[i].at[at], bufs[i].at[at], isem.at[slot]), pltpu.make_async_copy(bufs[i].at[at], outs[i].at[at], osem.at[slot])))
    for load, _ in pairs:
        load.start()
    for load, save in pairs:
        load.wait()
        save.start()
    for _, save in pairs:
        save.wait()


def settle(arrays):
    pieces = tuple(4 if a.size * a.dtype.itemsize >= 2**20 else 1 for a in arrays)
    far = pl.BlockSpec(memory_space=pl.ANY)
    return pl.pallas_call(
        functools.partial(settle_kernel, pieces),
        out_shape=[jax.ShapeDtypeStruct(a.shape, a.dtype) for a in arrays],
        in_specs=[far] * len(arrays), out_specs=[far] * len(arrays),
        scratch_shapes=[pltpu.VMEM(a.shape, a.dtype) for a in arrays] + [pltpu.SemaphoreType.DMA((sum(pieces),))] * 2,
        compiler_params=pltpu.CompilerParams(vmem_limit_bytes=60 * 2**20),
        name="settle",
    )(*arrays)


def local_plain(sizes, tokens, cotangent, adapter_id, global_pos, w_qkv, w_out, w_up, w_down, norm_gain, norm_bias,
          narrow_in, widen_out, ff_narrow, ff_widen):
    grid = Grid(sizes)
    small = jnp.concatenate([norm_gain, norm_bias], axis=1).T
    share = small.shape[1]
    small = jnp.pad(small, ((0, 12), (0, 128 - share)))
    got = all_gather(grid, [w_qkv, narrow_in, widen_out, small, w_out, w_up, w_down, ff_narrow, ff_widen], 0, 2, True)

    def whole(a):
        return a.reshape(-1, a.shape[-1])

    wq_full, a_full, b_full, small_full, wo_full, wu_full, wd_full, ffa_full, ffb_full = [whole(a) for a in got]
    norms = small_full.reshape(grid.devices, 16, 128)[:, :4, :share].transpose(1, 0, 2).reshape(4, grid.devices * share)
    norms = norms.astype(jnp.float32)
    gain_one, gain_two, shift_one, shift_two = norms[0], norms[1], norms[2], norms[3]
    seq_local, length, model_width = tokens.shape
    rows_all = seq_local * length
    set_cols = SETS * R
    chosen = (
        lax.broadcasted_iota(jnp.int32, (seq_local, set_cols), 1) // R == adapter_id[:, None]
    ).astype(jnp.float32)
    chosen = jnp.broadcast_to(chosen[:, None, :], (seq_local, length, set_cols)).reshape(rows_all, set_cols)
    chosen_three = jnp.concatenate([chosen, chosen, chosen], axis=1)
    positions = lax.broadcasted_iota(jnp.int32, (length,), 0)
    is_global = jnp.any(global_pos[:, :, None] == positions[None, None, :], axis=1).astype(jnp.float32)

    def cols_of(slot):
        return slice(slot * set_cols, (slot + 1) * set_cols)

    flat_in = tokens.reshape(rows_all, model_width)
    t_qkv = (product(flat_in, a_full[:, : 3 * set_cols]) * chosen_three).astype(jnp.bfloat16)
    projected = []
    for slot in range(3):
        summed = product(flat_in, wq_full[:, slot * model_width : (slot + 1) * model_width]) + against(
            t_qkv[:, cols_of(slot)], b_full[:, cols_of(slot)]
        )
        projected.append(summed.astype(jnp.bfloat16))
    query_low, key_low, value_low = projected
    mixed_flat, weights_low = attn_fwd(query_low, key_low, value_low, is_global[:, None, :], is_global[:, :, None], seq_local, length, 4)
    t_out = (product(mixed_flat, a_full[:, cols_of(3)]) * chosen).astype(jnp.bfloat16)
    attn_out = product(mixed_flat, wo_full) + against(t_out, b_full[:, cols_of(3)])
    resid = flat_in.astype(jnp.float32) + attn_out
    normed, norm_one_back = jax.vjp(lambda values: normalize(values, gain_one, shift_one), resid)
    normed_low = normed.astype(jnp.bfloat16)
    t_up = (product(normed_low, a_full[:, cols_of(4)]) * chosen).astype(jnp.bfloat16)
    pre_act = product(normed_low, wu_full) + against(t_up, ffb_full)
    cdf = 0.5 * (1.0 + lax.erf(pre_act * (0.5 ** 0.5)))
    act_low = (pre_act * cdf).astype(jnp.bfloat16)
    slope = cdf + pre_act * jnp.exp(-0.5 * pre_act * pre_act) * ((0.5 / math.pi) ** 0.5)
    act_low, slope = lax.optimization_barrier((act_low, slope))
    t_down = (product(act_low, ffa_full) * chosen).astype(jnp.bfloat16)
    down_out = product(act_low, wd_full) + against(t_down, b_full[:, cols_of(4)])
    final = normed + down_out
    result, norm_two_back = jax.vjp(lambda values: normalize(values, gain_two, shift_two), final)
    d_final = norm_two_back(cotangent.reshape(rows_all, model_width).astype(jnp.float32))[0]
    d_down = d_final.astype(jnp.bfloat16)
    dt_down = (product(d_down, b_full[:, cols_of(4)]) * chosen).astype(jnp.bfloat16)
    grad_b_down = over_rows(d_down, t_down)
    grad_ff_narrow = over_rows(act_low, dt_down)
    d_act = against(d_down, wd_full) + against(dt_down, ffa_full)
    d_pre = (d_act * slope).astype(jnp.bfloat16)
    dt_up = (product(d_pre, ffb_full) * chosen).astype(jnp.bfloat16)
    grad_ff_widen = over_rows(d_pre, t_up)
    grad_a_up = over_rows(normed_low, dt_up)
    d_normed = d_final + against(d_pre, wu_full) + against(dt_up, a_full[:, cols_of(4)])
    d_resid = norm_one_back(d_normed)[0]
    d_attn = d_resid.astype(jnp.bfloat16)
    dt_out = (product(d_attn, b_full[:, cols_of(3)]) * chosen).astype(jnp.bfloat16)
    grad_b_out = over_rows(d_attn, t_out)
    grad_a_out = over_rows(mixed_flat, dt_out)
    d_mixed = (against(d_attn, wo_full) + against(dt_out, a_full[:, cols_of(3)])).astype(jnp.bfloat16)
    d_parts = attn_bwd(query_low, key_low, value_low, weights_low, d_mixed, seq_local, length, 4)
    dt_parts = [
        (product(d_parts[slot], b_full[:, cols_of(slot)]) * chosen).astype(jnp.bfloat16) for slot in range(3)
    ]
    dt_qkv = jnp.concatenate(dt_parts, axis=1)
    grad_b_qkv = [over_rows(d_parts[slot], t_qkv[:, cols_of(slot)]) for slot in range(3)]
    grad_a_qkv = over_rows(flat_in, dt_qkv)
    d_input = d_resid + against(dt_qkv, a_full[:, : 3 * set_cols])
    for slot in range(3):
        d_input = d_input + against(d_parts[slot], wq_full[:, slot * model_width : (slot + 1) * model_width])
    rows_own, ff_own = model_width // grid.devices, ff_narrow.shape[0]
    late = reduce_scatter(
        grid, [grad_ff_narrow, grad_ff_widen, grad_a_out, grad_a_up, grad_b_out, grad_b_down],
        [(0, 0), (1, 0), (2, 0), (2, set_cols), (3, 0), (3, set_cols)],
        [(ff_own, set_cols), (ff_own, set_cols), (rows_own, 2 * set_cols), (rows_own, 2 * set_cols)], 1)
    early = reduce_scatter(
        grid, [grad_a_qkv] + grad_b_qkv, [(0, 0), (1, 0), (1, set_cols), (1, 2 * set_cols)],
        [(rows_own, 3 * set_cols), (rows_own, 3 * set_cols)], 2)
    return (
        result.reshape(seq_local, length, model_width).astype(jnp.bfloat16),
        d_input.reshape(seq_local, length, model_width).astype(jnp.bfloat16),
        jnp.concatenate([early[0], late[2]], axis=1),
        jnp.concatenate([early[1], late[3]], axis=1),
        late[0],
        late[1],
    )


LAG = 4


def local(sizes, tokens, cotangent, adapter_id, global_pos, w_qkv, w_out, w_up, w_down, norm_gain, norm_bias,
          narrow_in, widen_out, ff_narrow, ff_widen):
    grid = Grid(sizes)
    seq_local, length, width = tokens.shape
    rows = seq_local * length
    own = w_qkv.shape[0]
    fits = own % 16 == 0 and 128 % own == 0 and rows == 2 * length and w_up.shape[1] == 4 * rows and width == rows and width == grid.n["z"] * 4 * HD
    if not fits:
        return local_plain(sizes, tokens, cotangent, adapter_id, global_pos, w_qkv, w_out, w_up, w_down, norm_gain,
                           norm_bias, narrow_in, widen_out, ff_narrow, ff_widen)
    cols = SETS * R
    flat_in = tokens.reshape(rows, width)
    place = (lax.axis_index("dp") * grid.fsdp + lax.axis_index("fsdp")) % (128 // own)
    small = jnp.tile(jnp.concatenate([norm_gain, norm_bias], axis=1).T, (1, 128 // own))
    mine = lax.broadcasted_iota(jnp.int32, (1, 128), 1) // own == place
    small = jnp.where(mine, small, jnp.zeros((), BF))
    shards = (small, narrow_in, widen_out, w_qkv, w_out, w_up, ff_narrow, ff_widen, w_down)
    (g_small, g_ab, g_qkv, g_out, g_up, g_ff, g_dn, q, k, v, p, mix, h, f, yb, t, gb, sl, pick, norms) = forward(
        grid, flat_in, adapter_id, global_pos, shards, LAG, 0)
    ab, wo, ff = (flat2(a) for a in (g_ab, g_out, g_ff))
    wq = g_qkv.reshape(3, width, width)
    up = g_up.reshape(NCH, width, -1)
    dn = g_dn.reshape(NCH, w_up.shape[1], -1)
    res, dh, do, g_fa, g_fb, g_ao, g_au, g_bo, g_bd = middle(
        pick, norms, t, ab, f, cotangent.reshape(rows, width), h, yb, mix, wo, gb, sl, dn, up, ff)
    d_input, grad_a, grad_b, grad_fa, grad_fb = back(
        grid, q, k, v, p, do, flat_in, dh, ab, t, pick, wq, [g_fa, g_fb, g_ao, g_au, g_bo, g_bd], 1)
    d_input, grad_a, grad_b, grad_fa, grad_fb = settle([d_input, grad_a, grad_b, grad_fa, grad_fb])
    return res.reshape(tokens.shape), d_input.reshape(tokens.shape), grad_a, grad_b, grad_fa, grad_fb


def solution(mesh):
    rows = P(("dp", "fsdp"), None)
    cube = P(("dp", "fsdp"), None, None)
    in_specs = (cube, cube, P(("dp", "fsdp"))) + (rows,) * 11
    out_specs = (cube, cube) + (rows,) * 4
    return jax.shard_map(functools.partial(local, dict(mesh.shape)), mesh=mesh, in_specs=in_specs, out_specs=out_specs, check_vma=False)
```
